32 devices in a mesh: arm: 4 (over y, x), blk: 8 (over z, core).
Axes of the slice: x: 2, y: 2, z: 4, core: 2. Of those that a mesh axis runs over, the one named last changes fastest.
Arguments:
- site_one: float32 [2, 2, 8, 8, 128, 128], P(None, None, 'arm', 'blk'), may hold values from -6 to 6
- site_two: float32 [2, 2, 8, 8, 128, 128], P(None, None, 'arm', 'blk'), may hold values from -6 to 6
- impurity: float32 [2, 2, 8, 8, 128, 128], P(None, None, 'arm', 'blk'), may hold values from -6 to 6
- left_block: float32 [8, 8, 128, 128], P('arm', 'blk'), may hold values from -0.5 to 0.5
- left_hopping: float32 [8, 8, 128, 128], P('arm', 'blk'), may hold values from -0.5 to 0.5
- right_blocks: float32 [8, 8, 3, 2, 128, 128], P('arm', 'blk'), may hold values from -0.5 to 0.5
- chain: float32 [8, 3, 3], P('arm'), may hold values from 0.25 to 1.25
- interaction: float32 [8, 8], P('arm'), may hold values from 0.1 to 0.8
- dims: int32 [8, 4, 8], P('arm'), may hold values from 1 to 128, 768 in all within a row
Outputs:
- site_one_new: float32 [2, 2, 8, 8, 128, 128], P(None, None, 'arm', 'blk')
- site_two_new: float32 [2, 2, 8, 8, 128, 128], P(None, None, 'arm', 'blk')
- impurity_new: float32 [2, 2, 8, 8, 128, 128], P(None, None, 'arm', 'blk')
The draws below stay inside these ranges and needn't reach their ends.
Inputs may be any that keep to these rules, and one draw needn't show every extreme that they name: `dims`: each row of 8 sector dimensions sums to 768 and its largest entry equals 128.
All inputs are finite; a program needn't handle non-finite values.
Results may differ from the reference program's by a relative error of at most 0.0003.
Values sent between devices are 32-bit elements; how exact they have to be, the bound alone decides.
A program may use at most 64 MiB of HBM per device.

```python
import math
import jax
import jax.numpy as jnp
import numpy as np
from jax import lax

ARMS = 8
M = 128
KRYLOV = 3
NSEC = 8
CHI = 768
SEC_MOST = 128


def steps_of(stream_key, shape, split, low, high):
    def one(axis_at, parts):
        heights = jax.random.uniform(jax.random.fold_in(jax.random.fold_in(stream_key, 6), axis_at), (parts,), jnp.float32, low / len(split), high / len(split))
        return jnp.repeat(jnp.exp(heights), shape[axis_at] // parts).reshape((-1,) + (1,) * (len(shape) - axis_at - 1))

    factor_of = one(*split[0])
    for cut in split[1:]:
        factor_of = factor_of * one(*cut)
    return factor_of


def length_profile(amount, total, limit, skew):
    portions = [(1 << 20) // math.isqrt(standing ** skew) + 1 for standing in range(2, amount + 1)]
    spare, counts = total - limit - (amount - 1), [1] * (amount - 1)
    while spare > 0:
        movable = [i for i in range(amount - 1) if counts[i] < limit]
        whole, remaining = sum([portions[i] for i in movable]), spare
        for i in movable:
            addition = min(limit - counts[i], max(1, remaining * portions[i] // whole), spare)
            counts[i] = counts[i] + addition
            spare = spare - addition
    return np.array([limit] + counts)


def ragged_sizes(rng, count, total, bound, slope):
    if count == 2:
        one = jax.random.randint(rng, (), max(1, total - bound), min(bound, total - 1) + 1)
        return jnp.stack([one, total - one])
    tallies = jnp.asarray(length_profile(count, total, bound, slope), jnp.int32)
    pairs = (count - 1) // 2
    giver, sink = tallies[1:1 + 2 * pairs:2], tallies[2:2 + 2 * pairs:2]
    margin = jnp.minimum(giver - 1, bound - sink)
    moved = jax.random.randint(jax.random.fold_in(rng, 1), (pairs,), 0, 1 << 20) % (margin + 1)
    tallies = tallies.at[1:1 + 2 * pairs:2].set(giver - moved).at[2:2 + 2 * pairs:2].set(sink + moved)
    return tallies[jax.random.permutation(jax.random.fold_in(rng, 2), count)]


def centred(own_key, extent, scale, bound, shards=(), kind=jnp.bfloat16):
    level = steps_of(own_key, extent, shards, -0.22, 0.18) if shards else 1.0
    array = jax.random.normal(own_key, extent, jnp.float32) * scale * level
    return jnp.minimum(jnp.maximum(array, -bound), bound).astype(kind)


def setup_inputs(seed: int = 0) -> dict:
    streams_of = jax.random.split(jax.random.key(seed), 10)
    return {
        "site_one": centred(streams_of[0], (2, 2, ARMS, NSEC, M, M), 1.0, 6.0, ((2, 4), (3, 8)), jnp.float32),
        "site_two": centred(streams_of[1], (2, 2, ARMS, NSEC, M, M), 1.0, 6.0, ((2, 4), (3, 8)), jnp.float32),
        "impurity": centred(streams_of[2], (2, 2, ARMS, NSEC, M, M), 1.0, 6.0, ((2, 4), (3, 8)), jnp.float32),
        "left_block": centred(streams_of[3], (ARMS, NSEC, M, M), M ** -0.5, 0.5, ((0, 4), (1, 8)), jnp.float32),
        "left_hopping": centred(streams_of[4], (ARMS, NSEC, M, M), M ** -0.5, 0.5, ((0, 4), (1, 8)), jnp.float32),
        "right_blocks": centred(streams_of[5], (ARMS, NSEC, 3, 2, M, M), M ** -0.5, 0.5, ((0, 4), (1, 8)), jnp.float32),
        "chain": jnp.clip(0.25 + 1.0 * jax.random.uniform(streams_of[6], (ARMS, 3, 3), jnp.float32) ** steps_of(streams_of[6], (ARMS, 3, 3), ((0, 4),), -0.2, 0.2), 0.25, 1.25),
        "interaction": jnp.clip(0.1 + 0.7 * jax.random.uniform(streams_of[7], (ARMS, ARMS), jnp.float32) ** steps_of(streams_of[7], (ARMS, ARMS), ((0, 4),), -0.2, 0.2), 0.1, 0.8),
        "dims": jax.vmap(lambda own: ragged_sizes(own, NSEC, CHI, SEC_MOST, 1))(jax.random.split(streams_of[8], ARMS * 4)).reshape((ARMS, 4, NSEC)).astype(jnp.int32),
    }


HIGHEST = lax.Precision.HIGHEST
TIME_STEP = 0.4
EPSILON = 1e-06
taylor_terms = 12
halvings = 5
sector_bound = 3.0

def symmetric(blocks):
    return 0.5 * (blocks + jnp.swapaxes(blocks, -1, -2))

def left_apply(operator, part):
    if operator.shape[0] == 1:
        return jnp.einsum('aqij,caqjl->caqil', operator[0], part, precision=HIGHEST)
    form = 'aqij,aqjl->aqil'
    real = jnp.einsum(form, operator[0], part[0], precision=HIGHEST) - jnp.einsum(form, operator[1], part[1], precision=HIGHEST)
    imag = jnp.einsum(form, operator[0], part[1], precision=HIGHEST) + jnp.einsum(form, operator[1], part[0], precision=HIGHEST)
    return jnp.stack([real, imag])

def adjoint_product(first, second):
    form = 'aqji,aqjl->aqil'
    real = jnp.einsum(form, first[0], second[0], precision=HIGHEST) + jnp.einsum(form, first[1], second[1], precision=HIGHEST)
    imag = jnp.einsum(form, first[0], second[1], precision=HIGHEST) - jnp.einsum(form, first[1], second[0], precision=HIGHEST)
    return jnp.stack([real, imag])

def conj_transpose(matrix):
    return jnp.stack([jnp.swapaxes(matrix[0], -1, -2), -jnp.swapaxes(matrix[1], -1, -2)])

def right_apply(part, operator):
    return jnp.einsum('caqij,aqjl->caqil', part, operator, precision=HIGHEST)

def right_transposed(part, operator):
    return jnp.einsum('caqij,aqlj->caqil', part, operator, precision=HIGHEST)

def per_arm(values):
    return values[None, :, None, None, None]

def arm_scalar(values):
    return values[:, None, None, None]

def inner(first, second):
    return lax.optimization_barrier(jnp.sum(first * second, axis=(0, 1, 3, 4, 5)))

def apply_operator(state, lower, upper, left, hop_up, hop_down, right_pair, coupling, energy, left_rate, right_rate, live_mask):
    empty_part = left_apply(left, state[0]) + right_apply(state[0], right_pair[0]) + per_arm(left_rate) * left_apply(hop_down, upper) + per_arm(right_rate) * right_transposed(state[1], coupling)
    filled_part = left_apply(left, state[1]) + right_apply(state[1], right_pair[1]) + per_arm(energy) * state[1] + per_arm(left_rate) * left_apply(hop_up, lower) + per_arm(right_rate) * right_apply(state[0], coupling)
    return jnp.stack([empty_part, filled_part]) * live_mask

def batched(first, second):
    return jnp.einsum('aij,ajk->aik', first, second, precision=HIGHEST)

def krylov_exponential(alphas, betas):
    count = len(alphas)
    diagonal = jnp.stack(alphas, axis=1)
    offdiag = jnp.concatenate([jnp.stack(betas, axis=1), jnp.zeros_like(diagonal[:, :1])], axis=1)
    identity = jnp.eye(count, dtype=jnp.float32)
    above = jnp.eye(count, k=1, dtype=jnp.float32)
    below = jnp.eye(count, k=-1, dtype=jnp.float32)
    tridiag = diagonal[:, :, None] * identity + offdiag[:, :, None] * above + offdiag[:, None, :] * below
    scaled = TIME_STEP / 2.0 ** halvings * tridiag
    power = jnp.broadcast_to(identity, scaled.shape)
    real = power
    imag = jnp.zeros_like(power)
    for order in range(1, taylor_terms + 1):
        power = batched(power, scaled) / order
        phase = order % 4
        if phase == 1:
            imag = imag - power
        elif phase == 2:
            real = real - power
        elif phase == 3:
            imag = imag + power
        else:
            real = real + power
    for turn in range(halvings):
        real, imag = (batched(real, real) - batched(imag, imag), batched(real, imag) + batched(imag, real))
    return (real[:, :, 0], imag[:, :, 0])

def combine(basis, norm, real_coef, imag_coef):
    real_sum = 0.0
    imag_sum = 0.0
    for order, vector in enumerate(basis):
        cosine = arm_scalar(real_coef[:, order])
        sine = arm_scalar(imag_coef[:, order])
        real_sum = real_sum + cosine * vector[:, 0] - sine * vector[:, 1]
        imag_sum = imag_sum + cosine * vector[:, 1] + sine * vector[:, 0]
    return jnp.stack([real_sum, imag_sum], axis=1) * arm_scalar(norm)

def krylov(state, apply_fn):
    norm = jnp.sqrt(inner(state, state) + EPSILON)
    vector = state / arm_scalar(norm)
    basis = []
    alphas = []
    betas = []
    for step in range(KRYLOV):
        basis.append(vector)
        image = apply_fn(vector)
        diagonal_term = inner(vector, image)
        alphas.append(diagonal_term)
        if step + 1 < KRYLOV:
            image = image - arm_scalar(diagonal_term) * vector
            if step > 0:
                image = image - arm_scalar(betas[-1]) * basis[-2]
            beta_next = jnp.sqrt(inner(image, image) + EPSILON)
            betas.append(beta_next)
            vector = image / arm_scalar(beta_next)
    real_coef, imag_coef = krylov_exponential(alphas, betas)
    return (combine(basis, norm, real_coef, imag_coef), norm)

def next_sector(values, axis):
    tail = lax.slice_in_dim(values, 1, values.shape[axis], axis=axis)
    return jnp.concatenate([tail, jnp.zeros_like(lax.slice_in_dim(values, 0, 1, axis=axis))], axis=axis)

def prior_sector(values, axis):
    head = lax.slice_in_dim(values, 0, values.shape[axis] - 1, axis=axis)
    return jnp.concatenate([jnp.zeros_like(lax.slice_in_dim(values, 0, 1, axis=axis)), head], axis=axis)

def build_mask(left_dims, right_dims, width):
    rows = lax.broadcasted_iota(jnp.int32, (width, width), 0)
    columns = lax.broadcasted_iota(jnp.int32, (width, width), 1)
    inside = (rows < left_dims[None, None, :, :, None, None]) & (columns < right_dims[:, None, :, :, None, None])
    return inside.astype(jnp.float32)

def sector_scaled(evolved, norm, sectors):
    sector_square = lax.optimization_barrier(jnp.sum(evolved * evolved, axis=(0, 1, 4, 5)))
    factor = sector_bound / jnp.sqrt(sector_square + (norm * norm / sectors)[:, None])
    return evolved * factor[None, None, :, :, None, None]

def handover_terms(scaled, left, energy):
    own = adjoint_product(scaled[0], left_apply(left, scaled[0]))
    lifted = left_apply(left, scaled[1]) + per_arm(energy) * scaled[1]
    linked = adjoint_product(scaled[1], scaled[0])
    return (own, jnp.stack([adjoint_product(scaled[1], lifted), linked]), linked)

def reference(site_one, site_two, impurity, left_block, left_hopping, right_blocks, chain, interaction, dims):
    width = site_one.shape[-1]
    following = next_sector(dims, 2)
    live = [build_mask(dims[:, bond], jnp.stack([dims[:, bond + 1], following[:, bond + 1]]), width) for bond in range(3)]
    rights = symmetric(right_blocks[:, :, :, 0])
    rights_next = next_sector(rights, 1)
    left = symmetric(left_block)[None]
    hop_up = left_hopping[None]
    hop_down = jnp.swapaxes(prior_sector(left_hopping, 1), -1, -2)[None]
    filled = impurity * live[2]
    occupation = lax.optimization_barrier(jnp.sum(filled[1] * filled[1], axis=(0, 2, 3, 4))) / (inner(filled, filled) + EPSILON)
    energies = [chain[:, 0, 0], chain[:, 1, 0], chain[:, 2, 0] + jnp.dot(interaction, occupation, precision=HIGHEST)]
    sources = (site_one, site_two, impurity)
    results = []
    for tensor in range(3):
        live_mask = live[tensor]
        right_pair = jnp.stack([rights[:, :, tensor], rights_next[:, :, tensor]])
        coupling = right_blocks[:, :, tensor, 1]

        def apply_fn(vector):
            lower = next_sector(vector[0], 2)
            upper = prior_sector(vector[1], 2)
            return apply_operator(vector, lower, upper, left, hop_up, hop_down, right_pair, coupling, energies[tensor], chain[:, tensor, 1], chain[:, tensor, 2], live_mask)
        evolved, norm = krylov(sources[tensor] * live_mask, apply_fn)
        results.append(evolved)
        if tensor < 2:
            scaled = sector_scaled(evolved, norm, float(NSEC))
            own, stacked, linked = handover_terms(scaled, left, energies[tensor])
            moved = prior_sector(stacked, 3)
            left = own + moved[0]
            hop_up = conj_transpose(linked)
            hop_down = moved[1]
    return (results[0], results[1], results[2])
```

```python
import functools

import jax
import jax.numpy as jnp
from jax import lax
from jax.experimental import pallas as pl
from jax.experimental.pallas import tpu as pltpu
from jax.sharding import PartitionSpec as P

KRYLOV = 3
TENSORS = 3
TIME_STEP = 0.4
EPSILON = 1e-06
TAYLOR = 12
HALVINGS = 5
SECTOR_BOUND = 3.0
F32 = jnp.float32
BF16 = jnp.bfloat16


def split(x):
    high = x.astype(BF16)
    return high, (x - high.astype(F32)).astype(BF16)


def rows_of(a):
    return [a[0], a[0], a[1]]


def columns_of(b):
    return [b[0], b[1], b[0]]


def long_dot(left, right):
    return jnp.dot(
        jnp.concatenate(left, axis=1), jnp.concatenate(right, axis=0), preferred_element_type=F32)


def dot3(a, b):
    return long_dot(rows_of(a), columns_of(b))


def put(ref, a, x):
    high, low = split(x)
    ref[0, a] = high
    ref[1, a] = low


def get(ref, a):
    return ref[0, a], ref[1, a]


def complex_block(real, imag):
    return jnp.concatenate(
        [jnp.concatenate([real, -imag], axis=1), jnp.concatenate([imag, real], axis=1)], axis=0
    )


def column_sum(x):
    return jnp.sum(x, axis=0, keepdims=True)


def exponential(alphas, betas):
    step = TIME_STEP / 2.0**HALVINGS
    zero = jnp.zeros_like(alphas[0])
    one = jnp.ones_like(zero)
    s = {(0, 0): alphas[0], (1, 1): alphas[1], (2, 2): alphas[2], (0, 1): betas[0], (1, 2): betas[1]}
    s = {key: step * value for key, value in s.items()}
    keys = [(0, 0), (0, 1), (0, 2), (1, 1), (1, 2), (2, 2)]

    def at(m, i, j):
        return m[(min(i, j), max(i, j))]

    def times_s(m):
        out = {}
        for i, j in keys:
            terms = [at(m, i, k) * at(s, k, j) for k in range(3) if abs(k - j) < 2]
            out[(i, j)] = functools.reduce(jnp.add, terms)
        return out

    power = {key: one if key[0] == key[1] else zero for key in keys}
    real = dict(power)
    imag = {key: zero for key in keys}
    for order in range(1, TAYLOR + 1):
        power = {key: value * (1.0 / order) for key, value in times_s(power).items()}
        phase = order % 4
        target = imag if phase % 2 else real
        for key in keys:
            target[key] = target[key] - power[key] if phase in (1, 2) else target[key] + power[key]
    for _ in range(HALVINGS):
        new_real, new_imag = {}, {}
        for i, j in keys:
            re = im = None
            for k in range(3):
                a, b, c, d = at(real, i, k), at(imag, i, k), at(real, k, j), at(imag, k, j)
                x, y = a * c - b * d, a * d + b * c
                re, im = (x, y) if re is None else (re + x, im + y)
            new_real[(i, j)], new_imag[(i, j)] = re, im
        real, imag = new_real, new_imag
    return [at(real, k, 0) for k in range(3)], [at(imag, k, 0) for k in range(3)]


def kernel(
    count, arms, total_arms_dev,
    site0, site1, site2, left_in, hop_in, right_in, chain, inter, dims,
    out0, out1, out2,
    z, w, h, y, v1, v2, up, low, rnext, pmove, gmove,
    lop, rop, hu, hd, lown, part, red, tot, coef, occ_src, occ_all, erow,
    up_s, up_r, low_s, low_r, rn_s, rn_r, mv_s, mv_r, hop_s, hop_r, red_s, red_r, occ_s, occ_r,
):
    me = lax.axis_index("blk")
    arm = lax.axis_index("arm")
    width = left_in.shape[-1]
    sites, outs = (site0, site1, site2), (out0, out1, out2)
    has_next, has_prev = me < count - 1, me > 0
    nxt, prv = lax.rem(me + 1, count), lax.rem(me + count - 1, count)

    def peer(d):
        return lax.rem(me + d, count)

    def arm_peer(d):
        return lax.rem(arm + d, total_arms_dev)

    barrier = pltpu.get_barrier_semaphore()

    @pl.loop(1, count)
    def _(d):
        pl.semaphore_signal(barrier, inc=1, device_id={"blk": peer(d)})

    for d in range(1, total_arms_dev):
        pl.semaphore_signal(barrier, inc=1, device_id={"arm": arm_peer(d)})
    pl.semaphore_wait(barrier, count - 1 + total_arms_dev - 1)

    def up_copy(i, src, a):
        return pltpu.make_async_remote_copy(
            src_ref=src.at[1, a], dst_ref=up.at[i, a], send_sem=up_s.at[i, a],
            recv_sem=up_r.at[i, a], device_id={"blk": nxt})

    def low_copy(i, src, a):
        return pltpu.make_async_remote_copy(
            src_ref=src.at[0, a], dst_ref=low.at[i, a], send_sem=low_s.at[i, a],
            recv_sem=low_r.at[i, a], device_id={"blk": prv})

    def right_copy(t):
        return pltpu.make_async_remote_copy(
            src_ref=right_in.at[:, 0, t, 0], dst_ref=rnext.at[t], send_sem=rn_s.at[t],
            recv_sem=rn_r.at[t], device_id={"blk": prv})

    def hop_copy():
        return pltpu.make_async_remote_copy(
            src_ref=hop_in.at[:, 0], dst_ref=lown, send_sem=hop_s, recv_sem=hop_r,
            device_id={"blk": nxt})

    def move_copy(t, n, a):
        buf = (pmove, gmove)[n]
        return pltpu.make_async_remote_copy(
            src_ref=buf.at[t, 0, a], dst_ref=buf.at[t, 1, a], send_sem=mv_s.at[t, n, a],
            recv_sem=mv_r.at[t, n, a], device_id={"blk": nxt})

    def start_halo(i, src, a):
        @pl.when(has_next)
        def _():
            up_copy(i, src, a).start()

        @pl.when(has_prev)
        def _():
            low_copy(i, src, a).start()

    def start_halos(i, src):
        @pl.loop(0, arms)
        def _(a):
            start_halo(i, src, a)

    def wait_halo(i, src, a):
        @pl.when(has_prev)
        def _():
            up_copy(i, src, a).wait_recv()

        @pl.when(has_next)
        def _():
            low_copy(i, src, a).wait_recv()

    def end_halo(i, src):
        @pl.loop(0, arms)
        def _(a):
            @pl.when(has_next)
            def _():
                up_copy(i, src, a).wait_send()

            @pl.when(has_prev)
            def _():
                low_copy(i, src, a).wait_send()

    def start_reduce(r):
        @pl.loop(1, count)
        def _(d):
            pltpu.make_async_remote_copy(
                src_ref=part.at[r], dst_ref=red.at[r, d - 1], send_sem=red_s.at[r],
                recv_sem=red_r.at[r], device_id={"blk": peer(d)}).start()

    def wait_reduce(r):
        pltpu.make_async_copy(red.at[r], red.at[r], red_r.at[r]).wait()
        whole = part[r] + jnp.sum(red[r], axis=0)
        tot[...] = jnp.broadcast_to(jnp.sum(whole, axis=1, keepdims=True), whole.shape)

    def end_reduce(r):
        pltpu.make_async_copy(red.at[r], red.at[r], red_s.at[r]).wait()

    def total(n):
        return tot[n * arms:(n + 1) * arms, :]

    def add_row(r, n, a, row):
        part[r, pl.ds(n * arms + a, 1), :] = row

    def mask(t, s, a):
        rows = lax.broadcasted_iota(jnp.int32, (width, width), 0)
        cols = lax.broadcasted_iota(jnp.int32, (width, width), 1)
        m_left = dims[a, t, me]
        if s == 0:
            m_right = dims[a, t + 1, me]
        else:
            m_right = jnp.where(has_next, dims[a, t + 1, nxt], 0)
        one = jnp.where((rows < m_left) & (cols < m_right), 1.0, 0.0).astype(F32)
        return jnp.concatenate([one, one], axis=0)

    def load_source(t):
        @pl.loop(0, arms)
        def _(a):
            for s in range(2):
                both = jnp.concatenate([sites[t][s, 0, a, 0], sites[t][s, 1, a, 0]], axis=0)
                z[t, s, a] = both * mask(t, s, a)

    @pl.when(has_prev)
    def _():
        right_copy(0).start()

    @pl.when(has_next)
    def _():
        hop_copy().start()

    load_source(0)
    start_halos(0, z.at[0])
    part[...] = jnp.zeros_like(part)
    occ_src[...] = jnp.zeros_like(occ_src)
    load_source(2)
    occ_round = 2 * TENSORS

    @pl.loop(0, arms)
    def _(a):
        empty, filled = z[2, 0, a], z[2, 1, a]
        square = column_sum(filled * filled)
        add_row(occ_round, 0, a, square)
        add_row(occ_round, 1, a, square + column_sum(empty * empty))

    start_reduce(occ_round)
    load_source(1)

    @pl.when(jnp.logical_not(has_prev))
    def _():
        up[...] = jnp.zeros_like(up)
        for buf in (pmove, gmove):
            buf[:, 1] = jnp.zeros_like(buf[:, 1])

    @pl.when(jnp.logical_not(has_next))
    def _():
        low[...] = jnp.zeros_like(low)
        rnext[...] = jnp.zeros_like(rnext)

    @pl.when(jnp.logical_not(has_prev))
    def _():
        lown[...] = jnp.zeros_like(lown)

    zero = jnp.zeros((width, width), F32)
    rows = lax.broadcasted_iota(jnp.int32, (width, width), 0)
    cols = lax.broadcasted_iota(jnp.int32, (width, width), 1)
    eye = jnp.where(rows == cols, 1.0, 0.0).astype(F32)

    @pl.loop(0, arms)
    def _(a):
        left = left_in[a, 0]
        put(lop, a, complex_block(0.5 * (left + left.T), zero))
        put(hu, a, complex_block(chain[0, a, 1] * hop_in[a, 0], zero))
        erow[0, pl.ds(a, 1), :] = jnp.full((1, width), chain[0, a, 0], F32)
        erow[1, pl.ds(a, 1), :] = jnp.full((1, width), chain[1, a, 0], F32)

    @pl.when(has_prev)
    def _():
        hop_copy().wait_recv()

    @pl.loop(0, arms)
    def _(a):
        put(hd, a, complex_block(chain[0, a, 1] * lown[a].T, zero))

    def build_right(t):
        @pl.when(has_next)
        def _():
            right_copy(t).wait_recv()

        @pl.loop(0, arms)
        def _(a):
            own, other = right_in[a, 0, t, 0], rnext[t, a]
            couple = chain[t, a, 2] * right_in[a, 0, t, 1]
            first = 0.5 * (own + own.T)
            second = 0.5 * (other + other.T) + eye * erow[t, pl.ds(a, 1), :]
            top = jnp.concatenate([first, couple], axis=1)
            bottom = jnp.concatenate([couple.T, second], axis=1)
            put(rop, a, jnp.concatenate([top, bottom], axis=0))

    def right_part(src):
        @pl.loop(0, arms)
        def _(a):
            both = split(jnp.concatenate([src[0, a], src[1, a]], axis=1))
            image = dot3(both, get(rop, a))
            y[0, a] = image[:, :width]
            y[1, a] = image[:, width:]

    def local_part(src):
        for a in range(arms):
            both = split(jnp.concatenate([src[0, a], src[1, a]], axis=1))
            image = long_dot(
                rows_of(both) + rows_of(get(lop, a)), columns_of(get(rop, a)) + columns_of(both))
            y[0, a] = image[:, :width]
            y[1, a] = image[:, width:]

    def finished(t, i, src, a):
        wait_halo(i, src, a)
        return (
            (y[0, a] + dot3(get(hd, a), split(up[i, a]))) * mask(t, 0, a),
            (y[1, a] + dot3(get(hu, a), split(low[i, a]))) * mask(t, 1, a),
        )

    def row_of(n, a):
        return coef[n, pl.ds(a, 1), :]

    def set_rows(n, value):
        coef[n, 0:arms, :] = value

    for t in range(TENSORS):
        r0, reduce0 = 3 * t, 2 * t
        if t == 0:
            build_right(0)
            local_part(z.at[t])

        @pl.loop(0, arms)
        def _(a):
            if t > 0:
                @pl.when(has_prev)
                def _():
                    move_copy(t - 1, 0, a).wait_recv()
                    move_copy(t - 1, 1, a).wait_recv()

                packed = pmove[t - 1, 1, a]
                mirror = packed.T
                real = jnp.where(rows <= cols, packed, mirror)
                imag = jnp.where(rows > cols, packed, jnp.where(rows < cols, -mirror, 0.0))
                own = v1[0, a]
                put(lop, a, complex_block(own[:width] + real, own[width:] + imag))
                rate = chain[t, a, 1]
                put(hd, a, complex_block(
                    rate * gmove[t - 1, 1, a, 0], rate * gmove[t - 1, 1, a, 1]))
                both = split(jnp.concatenate([z[t, 0, a], z[t, 1, a]], axis=1))
                product = dot3(get(lop, a), both)
                y[0, a] = y[0, a] + product[:, :width]
                y[1, a] = y[1, a] + product[:, width:]
            image = finished(t, r0, z.at[t], a)
            for s in range(2):
                w[t, s, a] = image[s]
            start_halo(r0 + 1, w.at[t], a)
            sums = [0.0, 0.0, 0.0]
            for s in range(2):
                base = z[t, s, a]
                for n, pair in enumerate(((base, base), (base, image[s]), (image[s], image[s]))):
                    sums[n] = sums[n] + column_sum(pair[0] * pair[1])
            for n in range(3):
                add_row(reduce0, n, a, sums[n])

        start_reduce(reduce0)
        local_part(w.at[t])
        if t == 0:
            wait_reduce(occ_round)
            occ_src[0:arms, :] = total(0) / (total(1) + EPSILON)
            for d in range(1, total_arms_dev):
                pltpu.make_async_remote_copy(
                    src_ref=occ_src, dst_ref=occ_all.at[d - 1], send_sem=occ_s.at[d - 1],
                    recv_sem=occ_r.at[d - 1], device_id={"arm": arm_peer(d)}).start()

        @pl.loop(0, arms)
        def _(a):
            image = finished(t, r0 + 1, w.at[t], a)
            for s in range(2):
                h[t, s, a] = image[s]
            start_halo(r0 + 2, h.at[t], a)

        local_part(h.at[t])
        wait_reduce(reduce0)
        norm_square = total(0) + EPSILON
        norm = jnp.sqrt(norm_square)
        alpha0 = total(1) / norm_square
        beta1 = jnp.sqrt(jnp.maximum(total(2) / norm_square - alpha0 * alpha0, 0.0) + EPSILON)
        inverse = 1.0 / norm
        set_rows(0, alpha0)
        set_rows(1, inverse / beta1)
        set_rows(3, inverse)

        @pl.loop(0, arms)
        def _(a):
            alpha, scale, inv = row_of(0, a), row_of(1, a), row_of(3, a)
            sums = [0.0] * 4
            for s in range(2):
                vector = (w[t, s, a] - alpha * z[t, s, a]) * scale
                new = (h[t, s, a] - alpha * w[t, s, a]) * scale
                before = w[t, s, a] * inv
                v1[s, a] = vector
                v2[s, a] = new
                pairs = ((vector, new), (new, new), (before, new), (vector, before))
                for n, pair in enumerate(pairs):
                    sums[n] = sums[n] + column_sum(pair[0] * pair[1])
            for n in range(4):
                add_row(reduce0 + 1, n, a, sums[n])

        @pl.loop(0, arms)
        def _(a):
            image = finished(t, r0 + 2, h.at[t], a)
            alpha, scale = row_of(0, a), row_of(1, a)
            last = 0.0
            for s in range(2):
                last = last + column_sum(v2[s, a] * ((image[s] - alpha * h[t, s, a]) * scale))
            add_row(reduce0 + 1, 4, a, last)

        start_reduce(reduce0 + 1)
        if t + 1 < TENSORS:
            @pl.when(has_prev)
            def _():
                right_copy(t + 1).start()

            start_halos(r0 + 3, z.at[t + 1])
        if t == 1:
            for d in range(1, total_arms_dev):
                pltpu.make_async_remote_copy(
                    src_ref=occ_src, dst_ref=occ_all.at[d - 1], send_sem=occ_s.at[d - 1],
                    recv_sem=occ_r.at[d - 1], device_id={"arm": arm_peer(d)}).wait()

            @pl.loop(0, arms)
            def _(a):
                energy = jnp.full((1, width), chain[2, a, 0], F32)
                for d in range(total_arms_dev):
                    owner = lax.rem(arm + total_arms_dev - d, total_arms_dev)
                    for j in range(arms):
                        values = occ_src[j:j + 1, :] if d == 0 else occ_all[d - 1, j:j + 1, :]
                        energy = energy + inter[a, owner * arms + j] * values
                erow[2, pl.ds(a, 1), :] = energy

        if t + 1 < TENSORS:
            build_right(t + 1)
            right_part(z.at[t + 1])
        wait_reduce(reduce0 + 1)
        alpha1, square1, cross, link, third = (total(n) for n in range(5))
        beta2_square = jnp.maximum(square1 - alpha1 * alpha1 - beta1 * beta1, 0.0) + EPSILON
        beta2 = jnp.sqrt(beta2_square)
        alpha2 = (
            third - alpha1 * (2.0 * square1 - alpha1 * alpha1)
            - beta1 * (2.0 * cross - 2.0 * alpha1 * link - beta1 * alpha0)
        ) / beta2_square
        set_rows(4, alpha1)
        set_rows(5, beta1 * inverse)
        set_rows(6, 1.0 / beta2)
        real, imag = exponential([alpha0, alpha1, alpha2], [beta1, beta2])
        for k in range(KRYLOV):
            factor = norm if k else jnp.ones_like(norm)
            set_rows(7 + 2 * k, real[k] * factor)
            set_rows(8 + 2 * k, imag[k] * factor)
        set_rows(13, norm_square * (1.0 / count))

        @pl.loop(0, arms)
        def _(a):
            evolved = []
            squares = 0.0
            for s in range(2):
                re = im = 0.0
                second = v2[s, a] - row_of(4, a) * v1[s, a] - row_of(5, a) * z[t, s, a]
                for k, base in enumerate((z[t, s, a], v1[s, a], second * row_of(6, a))):
                    cosine, sine = row_of(7 + 2 * k, a), row_of(8 + 2 * k, a)
                    top, bottom = base[:width], base[width:]
                    re = re + cosine * top - sine * bottom
                    im = im + cosine * bottom + sine * top
                outs[t][s, 0, a, 0] = re
                outs[t][s, 1, a, 0] = im
                evolved.append((re, im))
                squares = squares + column_sum(re * re + im * im)
            if t + 1 < TENSORS:
                square = jnp.sum(squares, axis=1, keepdims=True)
                factor = SECTOR_BOUND / jnp.sqrt(
                    jnp.broadcast_to(square, (1, width)) + row_of(13, a))
                x = [(re * factor, im * factor) for re, im in evolved]
                flip = [split(jnp.concatenate([re.T, im.T], axis=1)) for re, im in x]

                def wide(re, im):
                    return split(jnp.concatenate(
                        [jnp.concatenate([re, im], axis=1), jnp.concatenate([im, -re], axis=1)],
                        axis=0))

                linked = dot3(flip[1], wide(*x[0]))
                gmove[t, 0, a, 0] = linked[:, :width]
                gmove[t, 0, a, 1] = linked[:, width:]

                @pl.when(has_next)
                def _():
                    move_copy(t, 1, a).start()

                whole = split(jnp.concatenate(
                    [jnp.concatenate(pair, axis=0) for pair in x], axis=1))
                image = dot3(get(lop, a), whole)
                energy = erow[t, pl.ds(a, 1), :]
                lifted = dot3(flip[1], wide(
                    image[:width, width:] + energy * x[1][0],
                    image[width:, width:] + energy * x[1][1]))
                pmove[t, 0, a] = jnp.where(rows <= cols, lifted[:, :width], lifted[:, width:])

                @pl.when(has_next)
                def _():
                    move_copy(t, 0, a).start()

                own = dot3(flip[0], wide(image[:width, :width], image[width:, :width]))
                rate = chain[t + 1, a, 1]
                put(hu, a, complex_block(
                    rate * linked[:, :width].T, -rate * linked[:, width:].T))
                v1[0, a] = jnp.concatenate([own[:, :width], own[:, width:]], axis=0)

    for t in range(TENSORS):
        for k, buf in enumerate((z, w, h)):
            end_halo(3 * t + k, buf.at[t])

        @pl.when(has_prev)
        def _():
            right_copy(t).wait_send()

    @pl.when(has_next)
    def _():
        hop_copy().wait_send()
        for t in range(TENSORS - 1):
            for n in range(2):
                for a in range(arms):
                    move_copy(t, n, a).wait_send()

    for r in range(2 * TENSORS + 1):
        end_reduce(r)


def hand_kernel(a, b, c, x, y, z, sem):
    copies = [
        pltpu.make_async_copy(i.at[s, p], o.at[s, p], sem.at[4 * k + 2 * s + p])
        for k, (i, o) in enumerate(((a, x), (b, y), (c, z))) for s in range(2) for p in range(2)]
    for copy in copies:
        copy.start()
    for copy in copies:
        copy.wait()


def hand(outs):
    anywhere = pl.BlockSpec(memory_space=pl.ANY)
    return pl.pallas_call(
        hand_kernel, out_shape=tuple(jax.ShapeDtypeStruct(o.shape, o.dtype) for o in outs),
        in_specs=[pl.BlockSpec(memory_space=pltpu.VMEM)] * 3, out_specs=(anywhere,) * 3,
        scratch_shapes=[pltpu.SemaphoreType.DMA((12,))],
    )(*(pltpu.with_memory_space_constraint(o, pltpu.VMEM) for o in outs))


def on_device(count, arm_devices, *args):
    site = args[0]
    args = args[:6] + (jnp.transpose(args[6], (1, 0, 2)),) + args[7:]
    arms, width = site.shape[2], site.shape[-1]
    rounds = 3 * TENSORS
    sums = 2 * TENSORS + 1
    rows = -(-5 * arms // 8) * 8
    arm_rows = -(-arms // 8) * 8
    state = (2, arms, 2 * width, width)
    half = (arms, 2 * width, width)
    vmem, sems = pltpu.VMEM, pltpu.SemaphoreType.DMA
    operator = vmem((2, arms, 2 * width, 2 * width), BF16)
    whole = pl.BlockSpec(memory_space=pltpu.VMEM)
    scalar = pl.BlockSpec(memory_space=pltpu.SMEM)
    out = pltpu.VMEM(site.shape, F32)
    moved = vmem((2, 2, arms, 2, width, width), F32)
    outs = pl.pallas_call(
        functools.partial(kernel, count, arms, arm_devices),
        out_shape=(out, out, out),
        in_specs=[whole] * 6 + [scalar] * 3,
        out_specs=(whole,) * 3,
        scratch_shapes=[
            vmem((TENSORS,) + state, F32),
            vmem((TENSORS,) + state, F32),
            vmem((TENSORS,) + state, F32),
            vmem(state, F32), vmem(state, F32), vmem(state, F32),
            vmem((rounds,) + half, F32),
            vmem((rounds,) + half, F32),
            vmem((TENSORS, arms, width, width), F32),
            vmem((2, 2, arms, width, width), F32), moved,
            operator, operator, operator, operator,
            vmem((arms, width, width), F32),
            vmem((sums, rows, width), F32),
            vmem((sums, count - 1, rows, width), F32),
            vmem((rows, width), F32),
            vmem((14, arm_rows, width), F32),
            vmem((arm_rows, width), F32),
            vmem((max(arm_devices - 1, 1), arm_rows, width), F32),
            vmem((TENSORS, arm_rows, width), F32),
            sems((rounds, arms)), sems((rounds, arms)), sems((rounds, arms)), sems((rounds, arms)),
            sems((TENSORS,)), sems((TENSORS,)),
            sems((2, 2, arms)), sems((2, 2, arms)), pltpu.SemaphoreType.DMA, pltpu.SemaphoreType.DMA,
            sems((sums,)), sems((sums,)),
            sems((max(arm_devices - 1, 1),)), sems((max(arm_devices - 1, 1),)),
        ],
        compiler_params=pltpu.CompilerParams(
            collective_id=0, has_side_effects=True, vmem_limit_bytes=56 * 1024 * 1024
        ),
    )(*args)
    return hand(outs)


def solution(mesh):
    tensor = P(None, None, "arm", "blk", None, None)
    in_specs = (
        tensor, tensor, tensor,
        P("arm", "blk", None, None),
        P("arm", "blk", None, None),
        P("arm", "blk", None, None, None, None),
        P("arm", None, None),
        P("arm", None),
        P("arm", None, None),
    )
    body = functools.partial(on_device, mesh.shape["blk"], mesh.shape["arm"])
    return jax.shard_map(
        body, mesh=mesh, in_specs=in_specs, out_specs=(tensor, tensor, tensor), check_vma=False
    )
```

```python
import functools

import jax
import jax.numpy as jnp
from jax import lax
from jax.experimental import pallas as pl
from jax.experimental.pallas import tpu as pltpu
from jax.sharding import PartitionSpec as P

KRYLOV = 3
TENSORS = 3
TIME_STEP = 0.4
EPSILON = 1e-06
TAYLOR = 12
HALVINGS = 5
SECTOR_BOUND = 3.0
F32 = jnp.float32
BF16 = jnp.bfloat16


def split(x):
    high = x.astype(BF16)
    return high, (x - high.astype(F32)).astype(BF16)


def rows_of(a):
    return [a[0], a[0], a[1]]


def columns_of(b):
    return [b[0], b[1], b[0]]


def long_dot(left, right):
    return jnp.dot(
        jnp.concatenate(left, axis=1), jnp.concatenate(right, axis=0), preferred_element_type=F32)


def dot3(a, b):
    return long_dot(rows_of(a), columns_of(b))


def put(ref, a, x):
    high, low = split(x)
    ref[0, a] = high
    ref[1, a] = low


def get(ref, a):
    return ref[0, a], ref[1, a]


def complex_block(real, imag):
    return jnp.concatenate(
        [jnp.concatenate([real, -imag], axis=1), jnp.concatenate([imag, real], axis=1)], axis=0
    )


def packed_half(x, width, late):
    half = width // 2
    real, imag = x[:width], x[width:]
    first = lax.broadcasted_iota(jnp.int32, (width, width), 1) < half
    if late:
        return jnp.where(first, pltpu.roll(real, half, 1), imag)
    return jnp.where(first, real, pltpu.roll(imag, half, 1))


def turned(x, width):
    half = width // 2
    first = lax.broadcasted_iota(jnp.int32, (width, width), 1) < half
    other = pltpu.roll(x, half, 1)
    return jnp.where(first, other, -other)


def column_sum(x):
    return jnp.sum(x, axis=0, keepdims=True)


def exponential(alphas, betas):
    step = TIME_STEP / 2.0**HALVINGS
    zero = jnp.zeros_like(alphas[0])
    one = jnp.ones_like(zero)
    s = {(0, 0): alphas[0], (1, 1): alphas[1], (2, 2): alphas[2], (0, 1): betas[0], (1, 2): betas[1]}
    s = {key: step * value for key, value in s.items()}
    keys = [(0, 0), (0, 1), (0, 2), (1, 1), (1, 2), (2, 2)]

    def at(m, i, j):
        return m[(min(i, j), max(i, j))]

    def times_s(m):
        out = {}
        for i, j in keys:
            terms = [at(m, i, k) * at(s, k, j) for k in range(3) if abs(k - j) < 2]
            out[(i, j)] = functools.reduce(jnp.add, terms)
        return out

    power = {key: one if key[0] == key[1] else zero for key in keys}
    real = dict(power)
    imag = {key: zero for key in keys}
    for order in range(1, TAYLOR + 1):
        power = {key: value * (1.0 / order) for key, value in times_s(power).items()}
        phase = order % 4
        target = imag if phase % 2 else real
        for key in keys:
            target[key] = target[key] - power[key] if phase in (1, 2) else target[key] + power[key]
    for _ in range(HALVINGS):
        new_real, new_imag = {}, {}
        for i, j in keys:
            re = im = None
            for k in range(3):
                a, b, c, d = at(real, i, k), at(imag, i, k), at(real, k, j), at(imag, k, j)
                x, y = a * c - b * d, a * d + b * c
                re, im = (x, y) if re is None else (re + x, im + y)
            new_real[(i, j)], new_imag[(i, j)] = re, im
        real, imag = new_real, new_imag
    return [at(real, k, 0) for k in range(3)], [at(imag, k, 0) for k in range(3)]


def kernel(
    count, arms, total_arms_dev,
    site0, site1, site2, left_in, hop_in, right_in, chain, inter, dims,
    out0, out1, out2,
    z, w, y, v1, v2, zup, zlow, wup, wlow, hsrc, hup, hlow, rnext, pmove, gmove,
    leftv, hopv, rightv, lop, rop, hu, hd, lown, part, red, opart, ored, coef,
    occ_src, occ_all, erow,
    z_in, left_s, hopv_s, rightv_s,
    zup_s, zup_r, zlow_s, zlow_r, wup_s, wup_r, wlow_s, wlow_r, hup_s, hup_r, hlow_s, hlow_r,
    rn_s, rn_r, hop_s, hop_r, mv_s, mv_r, red_s, red_r, ored_s, ored_r, occ_s, occ_r,
):
    me = lax.axis_index("blk")
    arm = lax.axis_index("arm")
    width = left_in.shape[-1]
    sites, outs = (site0, site1, site2), (out0, out1, out2)
    has_next, has_prev = me < count - 1, me > 0
    nxt, prv = lax.rem(me + 1, count), lax.rem(me + count - 1, count)

    def peer(d):
        return lax.rem(me + d, count)

    def arm_peer(d):
        return lax.rem(arm + d, total_arms_dev)

    barrier = pltpu.get_barrier_semaphore()

    @pl.loop(1, count)
    def _(d):
        pl.semaphore_signal(barrier, inc=1, device_id={"blk": peer(d)})

    for d in range(1, total_arms_dev):
        pl.semaphore_signal(barrier, inc=1, device_id={"arm": arm_peer(d)})

    def load(t, a):
        for s in range(2):
            for p in range(2):
                pltpu.make_async_copy(
                    sites[t].at[s, p, a, 0], z.at[t, s, p, a], z_in.at[t, a]).start()

    def wait_load(t, a):
        pltpu.make_async_copy(z.at[t, :, :, a], z.at[t, :, :, a], z_in.at[t, a]).wait()

    def left_load(a):
        return pltpu.make_async_copy(left_in.at[a, 0], leftv.at[a], left_s.at[a])

    def hop_load(a):
        return pltpu.make_async_copy(hop_in.at[a, 0], hopv.at[a], hopv_s.at[a])

    def right_load(t, a):
        return pltpu.make_async_copy(right_in.at[a, 0, t], rightv.at[t, a], rightv_s.at[t, a])

    for a in range(arms):
        load(0, a)
        left_load(a).start()
        hop_load(a).start()
        right_load(0, a).start()
    for t in (2, 1):
        for a in range(arms):
            load(t, a)
    for t in (1, 2):
        for a in range(arms):
            right_load(t, a).start()

    def zup_copy(t, a):
        return pltpu.make_async_remote_copy(
            src_ref=sites[t].at[1, :, a, 0], dst_ref=zup.at[t, a], send_sem=zup_s.at[t, a],
            recv_sem=zup_r.at[t, a], device_id={"blk": nxt})

    def zlow_copy(t, a):
        return pltpu.make_async_remote_copy(
            src_ref=sites[t].at[0, :, a, 0], dst_ref=zlow.at[t, a], send_sem=zlow_s.at[t, a],
            recv_sem=zlow_r.at[t, a], device_id={"blk": prv})

    def wup_copy(t, a):
        return pltpu.make_async_remote_copy(
            src_ref=w.at[t, 1, a], dst_ref=wup.at[t, a], send_sem=wup_s.at[t, a],
            recv_sem=wup_r.at[t, a], device_id={"blk": nxt})

    def wlow_copy(t, a):
        return pltpu.make_async_remote_copy(
            src_ref=w.at[t, 0, a], dst_ref=wlow.at[t, a], send_sem=wlow_s.at[t, a],
            recv_sem=wlow_r.at[t, a], device_id={"blk": prv})

    def hup_copy(t, a):
        return pltpu.make_async_remote_copy(
            src_ref=hsrc.at[t, 1, a], dst_ref=hup.at[t, a], send_sem=hup_s.at[t, a],
            recv_sem=hup_r.at[t, a], device_id={"blk": nxt})

    def hlow_copy(t, a):
        return pltpu.make_async_remote_copy(
            src_ref=hsrc.at[t, 0, a], dst_ref=hlow.at[t, a], send_sem=hlow_s.at[t, a],
            recv_sem=hlow_r.at[t, a], device_id={"blk": prv})

    def right_copy(t, a):
        return pltpu.make_async_remote_copy(
            src_ref=right_in.at[a, 0, t, 0], dst_ref=rnext.at[t, a], send_sem=rn_s.at[t, a],
            recv_sem=rn_r.at[t, a], device_id={"blk": prv})

    def hop_copy(a):
        return pltpu.make_async_remote_copy(
            src_ref=hop_in.at[a, 0], dst_ref=lown.at[a], send_sem=hop_s.at[a],
            recv_sem=hop_r.at[a], device_id={"blk": nxt})

    def move_copy(t, n, a):
        buf = (pmove, gmove)[n]
        return pltpu.make_async_remote_copy(
            src_ref=buf.at[t, 0, a], dst_ref=buf.at[t, 1, a], send_sem=mv_s.at[t, n, a],
            recv_sem=mv_r.at[t, n, a], device_id={"blk": nxt})

    def start_up(*copies):
        @pl.when(has_next)
        def _():
            for copy in copies:
                copy.start()

    def start_low(*copies):
        @pl.when(has_prev)
        def _():
            for copy in copies:
                copy.start()

    def wait_up(*copies):
        @pl.when(has_prev)
        def _():
            for copy in copies:
                copy.wait_recv()

    def wait_low(*copies):
        @pl.when(has_next)
        def _():
            for copy in copies:
                copy.wait_recv()

    @pl.when(jnp.logical_not(has_prev))
    def _():
        for buf in (zup, wup, hup, lown):
            buf[...] = jnp.zeros_like(buf)
        for buf in (pmove, gmove):
            buf[:, 1] = jnp.zeros_like(buf[:, 1])

    @pl.when(jnp.logical_not(has_next))
    def _():
        for buf in (zlow, wlow, hlow, rnext):
            buf[...] = jnp.zeros_like(buf)

    part[...] = jnp.zeros_like(part)
    opart[...] = jnp.zeros_like(opart)
    occ_src[...] = jnp.zeros_like(occ_src)
    pl.semaphore_wait(barrier, count - 1 + total_arms_dev - 1)

    for a in range(arms):
        start_low(right_copy(0, a), zlow_copy(0, a))
        start_up(zup_copy(0, a), hop_copy(a))

    def start_reduce(r, a):
        @pl.loop(1, count)
        def _(d):
            pltpu.make_async_remote_copy(
                src_ref=part.at[r, a], dst_ref=red.at[r, a, d - 1], send_sem=red_s.at[r, a],
                recv_sem=red_r.at[r, a], device_id={"blk": peer(d)}).start()

    def reduced(r, a):
        pltpu.make_async_copy(red.at[r, a], red.at[r, a], red_r.at[r, a]).wait()
        whole = part[r, a] + jnp.sum(red[r, a], axis=0)
        return jnp.broadcast_to(jnp.sum(whole, axis=1, keepdims=True), whole.shape)

    def end_reduce(r, a):
        pltpu.make_async_copy(red.at[r, a], red.at[r, a], red_s.at[r, a]).wait()

    rows = lax.broadcasted_iota(jnp.int32, (width, width), 0)
    cols = lax.broadcasted_iota(jnp.int32, (width, width), 1)
    eye = jnp.where(rows == cols, 1.0, 0.0).astype(F32)
    zero = jnp.zeros((width, width), F32)

    def mask_of(m_left, m_right):
        one = jnp.where((rows < m_left) & (cols < m_right), 1.0, 0.0).astype(F32)
        return jnp.concatenate([one, one], axis=0)

    def row_mask(m):
        return jnp.where(rows < m, 1.0, 0.0).astype(F32)

    def next_dim(a, t):
        return jnp.where(has_next, dims[a, t, nxt], 0)

    def tensor(t, s, a):
        return jnp.concatenate([z[t, s, 0, a], z[t, s, 1, a]], axis=0)

    def mask_source(t, a):
        wait_load(t, a)
        for s in range(2):
            one = mask_of(dims[a, t, me], dims[a, t + 1, me] if s == 0 else next_dim(a, t + 1))
            one = one[:width]
            for p in range(2):
                z[t, s, p, a] = z[t, s, p, a] * one

    def from_below(t, a):
        both = jnp.concatenate([zup[t, a, 0], zup[t, a, 1]], axis=0)
        return split(both * mask_of(dims[a, t, prv], dims[a, t + 1, me]))

    def from_above(t, a):
        both = jnp.concatenate([zlow[t, a, 0], zlow[t, a, 1]], axis=0)
        return split(both * mask_of(dims[a, t, nxt], next_dim(a, t + 1)))

    @pl.loop(0, arms)
    def _(a):
        mask_source(0, a)
        left_load(a).wait()
        live = row_mask(dims[a, 0, me])
        left = leftv[a]
        put(lop, a, complex_block(0.5 * (left + left.T) * live, zero))
        hop_load(a).wait()
        put(hu, a, complex_block(chain[0, a, 1] * hopv[a] * live, zero))
        erow[0, pl.ds(a, 1), :] = jnp.full((1, width), chain[0, a, 0], F32)
        erow[1, pl.ds(a, 1), :] = jnp.full((1, width), chain[1, a, 0], F32)

    def build_right(t, a):
        right_load(t, a).wait()
        wait_low(right_copy(t, a))
        own, other = rightv[t, a, 0], rnext[t, a]
        couple = chain[t, a, 2] * rightv[t, a, 1]
        first = 0.5 * (own + own.T)
        second = 0.5 * (other + other.T) + eye * erow[t, pl.ds(a, 1), :]
        keep = jnp.where(cols < dims[a, t + 1, me], 1.0, 0.0).astype(F32)
        keep_next = jnp.where(cols < next_dim(a, t + 1), 1.0, 0.0).astype(F32)
        top = jnp.concatenate([first * keep, couple * keep_next], axis=1)
        bottom = jnp.concatenate([couple.T * keep, second * keep_next], axis=1)
        put(rop, a, jnp.concatenate([top, bottom], axis=0))

    def set_image(a, image):
        y[0, a] = image[:, :width]
        y[1, a] = image[:, width:]

    def right_part(t, a):
        both = split(jnp.concatenate([tensor(t, 0, a), tensor(t, 1, a)], axis=1))
        set_image(a, dot3(both, get(rop, a)))

    def local_part(one, two, a):
        both = split(jnp.concatenate([one, two], axis=1))
        set_image(a, long_dot(
            rows_of(both) + rows_of(get(lop, a)), columns_of(get(rop, a)) + columns_of(both)))

    @pl.loop(0, arms)
    def _(a):
        build_right(0, a)
        local_part(tensor(0, 0, a), tensor(0, 1, a), a)

    @pl.loop(0, arms)
    def _(a):
        mask_source(2, a)
        empty, filled = tensor(2, 0, a), tensor(2, 1, a)
        square = column_sum(filled * filled)
        opart[pl.ds(a, 1), :] = square
        opart[pl.ds(arms + a, 1), :] = square + column_sum(empty * empty)

    @pl.loop(1, count)
    def _(d):
        pltpu.make_async_remote_copy(
            src_ref=opart, dst_ref=ored.at[d - 1], send_sem=ored_s,
            recv_sem=ored_r, device_id={"blk": peer(d)}).start()

    @pl.loop(0, arms)
    def _(a):
        mask_source(1, a)
        wait_up(hop_copy(a))
        put(hd, a, complex_block(
            chain[0, a, 1] * lown[a].T * row_mask(dims[a, 0, me]), zero))

    def add_row(r, a, n, row):
        part[r, a, n:n + 1, :] = row

    def row_of(a, n):
        return coef[a, n:n + 1, :]

    def set_row(a, n, value):
        coef[a, n:n + 1, :] = value

    for t in range(TENSORS):
        @pl.loop(0, arms)
        def _(a):
            wait_low(zlow_copy(t, a))
            filled = y[1, a] + dot3(get(hu, a), from_above(t, a))
            empty = y[0, a]
            wait_up(zup_copy(t, a))
            below = from_below(t, a)
            if t > 0:
                wait_up(move_copy(t - 1, 1, a))
                rate = chain[t, a, 1]
                put(hd, a, complex_block(
                    rate * gmove[t - 1, 1, a, 0], rate * gmove[t - 1, 1, a, 1]))
            empty = empty + dot3(get(hd, a), below)
            base = [tensor(t, s, a) for s in range(2)]
            if t > 0:
                wait_up(move_copy(t - 1, 0, a))
                packed = pmove[t - 1, 1, a]
                mirror = packed.T
                real = jnp.where(rows <= cols, packed, mirror)
                imag = jnp.where(rows > cols, packed, jnp.where(rows < cols, -mirror, 0.0))
                own = v1[0, a]
                put(lop, a, complex_block(own[:width] + real, own[width:] + imag))
                product = dot3(get(lop, a), split(jnp.concatenate(base, axis=1)))
                empty = empty + product[:, :width]
                filled = filled + product[:, width:]
            image = (empty, filled)
            for s in range(2):
                w[t, s, a] = image[s]
            start_up(wup_copy(t, a))
            start_low(wlow_copy(t, a))
            sums = [0.0, 0.0, 0.0]
            for s in range(2):
                pairs = ((base[s], base[s]), (base[s], image[s]), (image[s], image[s]))
                for n, pair in enumerate(pairs):
                    sums[n] = sums[n] + column_sum(pair[0] * pair[1])
            for n in range(3):
                add_row(2 * t, a, n, sums[n])
            start_reduce(2 * t, a)
            local_part(image[0], image[1], a)

        if t == 0:
            pltpu.make_async_copy(ored, ored, ored_r).wait()
            whole = opart[...] + jnp.sum(ored[...], axis=0)
            opart_tot = jnp.broadcast_to(jnp.sum(whole, axis=1, keepdims=True), whole.shape)
            occ_src[0:arms, :] = opart_tot[0:arms] / (opart_tot[arms:2 * arms] + EPSILON)
            for d in range(1, total_arms_dev):
                pltpu.make_async_remote_copy(
                    src_ref=occ_src, dst_ref=occ_all.at[d - 1], send_sem=occ_s.at[d - 1],
                    recv_sem=occ_r.at[d - 1], device_id={"arm": arm_peer(d)}).start()

        @pl.loop(0, arms)
        def _(a):
            wait_low(wlow_copy(t, a))
            filled = y[1, a] + dot3(get(hu, a), split(wlow[t, a]))
            wait_up(wup_copy(t, a))
            empty = y[0, a] + dot3(get(hd, a), split(wup[t, a]))
            hsrc[t, 1, a] = packed_half(filled, width, False)
            hsrc[t, 0, a] = packed_half(empty, width, True)
            start_up(hup_copy(t, a))
            start_low(hlow_copy(t, a))
            tot = reduced(2 * t, a)
            norm_square = tot[0:1] + EPSILON
            norm = jnp.sqrt(norm_square)
            alpha = tot[1:2] / norm_square
            beta = jnp.sqrt(jnp.maximum(tot[2:3] / norm_square - alpha * alpha, 0.0) + EPSILON)
            inv = 1.0 / norm
            scale = inv / beta
            for n, value in enumerate((alpha, scale, inv, beta, norm, norm_square)):
                set_row(a, n, value)
            sums = [0.0] * 5
            fresh = []
            for s, second in enumerate((empty, filled)):
                first = w[t, s, a]
                vector = (first - alpha * tensor(t, s, a)) * scale
                new = (second - alpha * first) * scale
                before = first * inv
                v1[s, a] = vector
                v2[s, a] = new
                fresh.append(new)
                pairs = ((vector, new), (new, new), (before, new), (vector, before))
                for n, pair in enumerate(pairs):
                    sums[n] = sums[n] + column_sum(pair[0] * pair[1])
            both = jnp.concatenate(fresh, axis=1).astype(BF16)
            image = long_dot([both, lop[0, a]], [rop[0, a], both])
            for s in range(2):
                sums[4] = sums[4] + column_sum(fresh[s] * image[:, s * width:(s + 1) * width])
            for n in range(5):
                add_row(2 * t + 1, a, n, sums[n])

        if t + 1 < TENSORS:
            for a in range(arms):
                start_low(right_copy(t + 1, a))

        @pl.loop(0, arms)
        def _(a):
            alpha, scale = row_of(a, 0), row_of(a, 1)

            def crossing(arrived, before, mine, operator, late):
                vector = (arrived - alpha * packed_half(before, width, late)) * scale
                image = jnp.dot(
                    operator[0, a][:, :width], vector.astype(BF16), preferred_element_type=F32)
                own = packed_half(mine, width, late)
                return 2.0 * column_sum(
                    own * image[:width] + turned(own, width) * image[width:])

            wait_up(hup_copy(t, a))
            total = crossing(hup[t, a], wup[t, a], v2[0, a], hd, False)
            wait_low(hlow_copy(t, a))
            total = total + crossing(hlow[t, a], wlow[t, a], v2[1, a], hu, True)
            add_row(2 * t + 1, a, 4, part[2 * t + 1, a, 4:5, :] + total)
            start_reduce(2 * t + 1, a)

        if t + 1 < TENSORS:
            for a in range(arms):
                start_up(zup_copy(t + 1, a))
                start_low(zlow_copy(t + 1, a))
        if t == 1:
            for d in range(1, total_arms_dev):
                pltpu.make_async_remote_copy(
                    src_ref=occ_src, dst_ref=occ_all.at[d - 1], send_sem=occ_s.at[d - 1],
                    recv_sem=occ_r.at[d - 1], device_id={"arm": arm_peer(d)}).wait()

            @pl.loop(0, arms)
            def _(a):
                energy = jnp.full((1, width), chain[2, a, 0], F32)
                for d in range(total_arms_dev):
                    owner = lax.rem(arm + total_arms_dev - d, total_arms_dev)
                    for j in range(arms):
                        values = occ_src[j:j + 1, :] if d == 0 else occ_all[d - 1, j:j + 1, :]
                        energy = energy + inter[a, owner * arms + j] * values
                erow[2, pl.ds(a, 1), :] = energy

        if t + 1 < TENSORS:
            @pl.loop(0, arms)
            def _(a):
                build_right(t + 1, a)
                right_part(t + 1, a)

        @pl.loop(0, arms)
        def _(a):
            alpha0, inverse, beta1, norm, norm_square = (row_of(a, n) for n in (0, 2, 3, 4, 5))
            tot = reduced(2 * t + 1, a)
            alpha1, square1, cross, link, third = (tot[n:n + 1] for n in range(5))
            beta2_square = jnp.maximum(square1 - alpha1 * alpha1 - beta1 * beta1, 0.0) + EPSILON
            beta2 = jnp.sqrt(beta2_square)
            alpha2 = (
                third - alpha1 * (2.0 * square1 - alpha1 * alpha1)
                - beta1 * (2.0 * cross - 2.0 * alpha1 * link - beta1 * alpha0)
            ) / beta2_square
            real, imag = exponential([alpha0, alpha1, alpha2], [beta1, beta2])
            last = 1.0 / beta2
            back = beta1 * inverse
            evolved = []
            squares = 0.0
            for s in range(2):
                re = im = 0.0
                base = tensor(t, s, a)
                second = v2[s, a] - alpha1 * v1[s, a] - back * base
                for k, part_of in enumerate((base, v1[s, a], second * last)):
                    factor = norm if k else 1.0
                    cosine, sine = real[k] * factor, imag[k] * factor
                    top, bottom = part_of[:width], part_of[width:]
                    re = re + cosine * top - sine * bottom
                    im = im + cosine * bottom + sine * top
                outs[t][s, 0, a, 0] = re
                outs[t][s, 1, a, 0] = im
                evolved.append((re, im))
                squares = squares + column_sum(re * re + im * im)
            if t + 1 < TENSORS:
                square = jnp.sum(squares, axis=1, keepdims=True)
                factor = SECTOR_BOUND / jnp.sqrt(
                    jnp.broadcast_to(square, (1, width)) + norm_square * (1.0 / count))
                x = [(re * factor, im * factor) for re, im in evolved]
                flip = [split(jnp.concatenate([re.T, im.T], axis=1)) for re, im in x]

                def wide(re, im):
                    return split(jnp.concatenate(
                        [jnp.concatenate([re, im], axis=1), jnp.concatenate([im, -re], axis=1)],
                        axis=0))

                linked = dot3(flip[1], wide(*x[0]))
                gmove[t, 0, a, 0] = linked[:, :width]
                gmove[t, 0, a, 1] = linked[:, width:]
                start_up(move_copy(t, 1, a))
                whole = split(jnp.concatenate(
                    [jnp.concatenate(pair, axis=0) for pair in x], axis=1))
                image = dot3(get(lop, a), whole)
                energy = erow[t, pl.ds(a, 1), :]
                lifted = dot3(flip[1], wide(
                    image[:width, width:] + energy * x[1][0],
                    image[width:, width:] + energy * x[1][1]))
                pmove[t, 0, a] = jnp.where(rows <= cols, lifted[:, :width], lifted[:, width:])
                start_up(move_copy(t, 0, a))
                own = dot3(flip[0], wide(image[:width, :width], image[width:, :width]))
                rate = chain[t + 1, a, 1]
                put(hu, a, complex_block(
                    rate * linked[:, :width].T, -rate * linked[:, width:].T))
                v1[0, a] = jnp.concatenate([own[:, :width], own[:, width:]], axis=0)

    @pl.when(has_next)
    def _():
        for a in range(arms):
            hop_copy(a).wait_send()
            for t in range(TENSORS):
                zup_copy(t, a).wait_send()
                wup_copy(t, a).wait_send()
                hup_copy(t, a).wait_send()
            for t in range(TENSORS - 1):
                for n in range(2):
                    move_copy(t, n, a).wait_send()

    @pl.when(has_prev)
    def _():
        for a in range(arms):
            for t in range(TENSORS):
                right_copy(t, a).wait_send()
                zlow_copy(t, a).wait_send()
                wlow_copy(t, a).wait_send()
                hlow_copy(t, a).wait_send()

    pltpu.make_async_copy(ored, ored, ored_s).wait()
    for a in range(arms):
        for r in range(2 * TENSORS):
            end_reduce(r, a)


def hand_kernel(a, b, c, x, y, z, sem):
    copies = [
        pltpu.make_async_copy(i.at[s, p], o.at[s, p], sem.at[4 * k + 2 * s + p])
        for k, (i, o) in enumerate(((a, x), (b, y), (c, z))) for s in range(2) for p in range(2)]
    for copy in copies:
        copy.start()
    for copy in copies:
        copy.wait()


def hand(outs):
    anywhere = pl.BlockSpec(memory_space=pl.ANY)
    return pl.pallas_call(
        hand_kernel, out_shape=tuple(jax.ShapeDtypeStruct(o.shape, o.dtype) for o in outs),
        in_specs=[pl.BlockSpec(memory_space=pltpu.VMEM)] * 3, out_specs=(anywhere,) * 3,
        scratch_shapes=[pltpu.SemaphoreType.DMA((12,))],
    )(*(pltpu.with_memory_space_constraint(o, pltpu.VMEM) for o in outs))


def on_device(count, arm_devices, *args):
    site = args[0]
    args = args[:6] + (jnp.transpose(args[6], (1, 0, 2)),) + args[7:]
    arms, width = site.shape[2], site.shape[-1]
    rounds = 2 * TENSORS
    occ_rows = -(-2 * arms // 8) * 8
    arm_rows = -(-arms // 8) * 8
    vmem, sems = pltpu.VMEM, pltpu.SemaphoreType.DMA
    state = vmem((2, arms, 2 * width, width), F32)
    source = vmem((TENSORS, arms, 2, width, width), F32)
    halo = vmem((TENSORS, arms, 2 * width, width), F32)
    square = vmem((TENSORS, arms, width, width), F32)
    operator = vmem((2, arms, 2 * width, 2 * width), BF16)
    block = vmem((arms, width, width), F32)
    whole = pl.BlockSpec(memory_space=pltpu.VMEM)
    distant = pl.BlockSpec(memory_space=pltpu.HBM)
    scalar = pl.BlockSpec(memory_space=pltpu.SMEM)
    out = pltpu.VMEM(site.shape, F32)
    each, single = sems((TENSORS, arms)), sems((arms,))
    moves, sums = sems((TENSORS - 1, 2, arms)), sems((rounds, arms))
    arm_sems = sems((max(arm_devices - 1, 1),))
    outs = pl.pallas_call(
        functools.partial(kernel, count, arms, arm_devices),
        out_shape=(out, out, out),
        in_specs=[distant] * 6 + [scalar] * 3,
        out_specs=(whole,) * 3,
        scratch_shapes=[
            vmem((TENSORS, 2, 2, arms, width, width), F32),
            vmem((TENSORS, 2, arms, 2 * width, width), F32),
            state, state, state,
            source, source, halo, halo,
            vmem((TENSORS, 2, arms, width, width), F32), square, square, square,
            vmem((TENSORS - 1, 2, arms, width, width), F32),
            vmem((TENSORS - 1, 2, arms, 2, width, width), F32),
            block, block, vmem((TENSORS, arms, 2, width, width), F32),
            operator, operator, operator, operator, block,
            vmem((rounds, arms, 8, width), F32),
            vmem((rounds, arms, count - 1, 8, width), F32),
            vmem((occ_rows, width), F32),
            vmem((count - 1, occ_rows, width), F32),
            vmem((arms, 8, width), F32),
            vmem((arm_rows, width), F32),
            vmem((max(arm_devices - 1, 1), arm_rows, width), F32),
            vmem((TENSORS, arm_rows, width), F32),
            each, single, single, each,
            each, each, each, each, each, each, each, each, each, each, each, each,
            each, each, single, single, moves, moves, sums, sums,
            pltpu.SemaphoreType.DMA, pltpu.SemaphoreType.DMA, arm_sems, arm_sems,
        ],
        compiler_params=pltpu.CompilerParams(
            collective_id=0, has_side_effects=True, vmem_limit_bytes=56 * 1024 * 1024
        ),
    )(*args)
    return hand(outs)


def solution(mesh):
    tensor = P(None, None, "arm", "blk", None, None)
    in_specs = (
        tensor, tensor, tensor,
        P("arm", "blk", None, None),
        P("arm", "blk", None, None),
        P("arm", "blk", None, None, None, None),
        P("arm", None, None),
        P("arm", None),
        P("arm", None, None),
    )
    body = functools.partial(on_device, mesh.shape["blk"], mesh.shape["arm"])
    return jax.shard_map(
        body, mesh=mesh, in_specs=in_specs, out_specs=(tensor, tensor, tensor), check_vma=False
    )
```

```python
import functools

import jax
import jax.numpy as jnp
from jax import lax
from jax.experimental import pallas as pl
from jax.experimental.pallas import tpu as pltpu
from jax.sharding import PartitionSpec as P

KRYLOV = 3
TENSORS = 3
TIME_STEP = 0.4
EPSILON = 1e-06
TAYLOR = 12
HALVINGS = 5
SECTOR_BOUND = 3.0
F32 = jnp.float32
BF16 = jnp.bfloat16


def split(x):
    high = x.astype(BF16)
    return high, (x - high.astype(F32)).astype(BF16)


def rows_of(a):
    return [a[0], a[0], a[1]]


def columns_of(b):
    return [b[0], b[1], b[0]]


def long_dot(left, right):
    return jnp.dot(
        jnp.concatenate(left, axis=1), jnp.concatenate(right, axis=0), preferred_element_type=F32)


def dot3(a, b):
    return long_dot(rows_of(a), columns_of(b))


def put(ref, a, x):
    high, low = split(x)
    ref[0, a] = high
    ref[1, a] = low


def get(ref, a):
    return ref[0, a], ref[1, a]


def complex_block(real, imag):
    return jnp.concatenate(
        [jnp.concatenate([real, -imag], axis=1), jnp.concatenate([imag, real], axis=1)], axis=0
    )


def packed_half(x, width, late):
    half = width // 2
    real, imag = x[:width], x[width:]
    first = lax.broadcasted_iota(jnp.int32, (width, width), 1) < half
    if late:
        return jnp.where(first, pltpu.roll(real, half, 1), imag)
    return jnp.where(first, real, pltpu.roll(imag, half, 1))


def turned(x, width):
    half = width // 2
    first = lax.broadcasted_iota(jnp.int32, (width, width), 1) < half
    other = pltpu.roll(x, half, 1)
    return jnp.where(first, other, -other)


def column_sum(x):
    return jnp.sum(x, axis=0, keepdims=True)


def exponential(alphas, betas):
    step = TIME_STEP / 2.0**HALVINGS
    zero = jnp.zeros_like(alphas[0])
    one = jnp.ones_like(zero)
    s = {(0, 0): alphas[0], (1, 1): alphas[1], (2, 2): alphas[2], (0, 1): betas[0], (1, 2): betas[1]}
    s = {key: step * value for key, value in s.items()}
    keys = [(0, 0), (0, 1), (0, 2), (1, 1), (1, 2), (2, 2)]

    def at(m, i, j):
        return m[(min(i, j), max(i, j))]

    def times_s(m):
        out = {}
        for i, j in keys:
            terms = [at(m, i, k) * at(s, k, j) for k in range(3) if abs(k - j) < 2]
            out[(i, j)] = functools.reduce(jnp.add, terms)
        return out

    power = {key: one if key[0] == key[1] else zero for key in keys}
    real = dict(power)
    imag = {key: zero for key in keys}
    for order in range(1, TAYLOR + 1):
        power = {key: value * (1.0 / order) for key, value in times_s(power).items()}
        phase = order % 4
        target = imag if phase % 2 else real
        for key in keys:
            target[key] = target[key] - power[key] if phase in (1, 2) else target[key] + power[key]
    for _ in range(HALVINGS):
        new_real, new_imag = {}, {}
        for i, j in keys:
            re = im = None
            for k in range(3):
                a, b, c, d = at(real, i, k), at(imag, i, k), at(real, k, j), at(imag, k, j)
                x, y = a * c - b * d, a * d + b * c
                re, im = (x, y) if re is None else (re + x, im + y)
            new_real[(i, j)], new_imag[(i, j)] = re, im
        real, imag = new_real, new_imag
    return [at(real, k, 0) for k in range(3)], [at(imag, k, 0) for k in range(3)]


def kernel(
    count, arms, total_arms_dev,
    site0, site1, site2, left_in, hop_in, right_in, chain, inter, dims,
    out0, out1, out2,
    z, w, y, v1, v2, back, zup, zlow, wup, wlow, hsrc, hup, hlow, rnext, pmove, gmove,
    leftv, hopv, rightv, lop, rop, hu, hd, lown, part, red, opart, ored, coef,
    occ_src, occ_all, erow,
    z_in, left_s, hopv_s, rightv_s,
    zup_s, zup_r, zlow_s, zlow_r, wup_s, wup_r, wlow_s, wlow_r, hup_s, hup_r, hlow_s, hlow_r,
    rn_s, rn_r, hop_s, hop_r, mv_s, mv_r, red_s, red_r, ored_s, ored_r, occ_s, occ_r,
):
    me = lax.axis_index("blk")
    arm = lax.axis_index("arm")
    width = left_in.shape[-1]
    sites, outs = (site0, site1, site2), (out0, out1, out2)
    has_next, has_prev = me < count - 1, me > 0
    nxt, prv = lax.rem(me + 1, count), lax.rem(me + count - 1, count)

    def peer(d):
        return lax.rem(me + d, count)

    def arm_peer(d):
        return lax.rem(arm + d, total_arms_dev)

    barrier = pltpu.get_barrier_semaphore()

    @pl.loop(1, count)
    def _(d):
        pl.semaphore_signal(barrier, inc=1, device_id={"blk": peer(d)})

    for d in range(1, total_arms_dev):
        pl.semaphore_signal(barrier, inc=1, device_id={"arm": arm_peer(d)})

    def load(t, a):
        for s in range(2):
            for p in range(2):
                pltpu.make_async_copy(
                    sites[t].at[s, p, a, 0], z.at[t, s, p, a], z_in.at[t, a]).start()

    def wait_load(t, a):
        pltpu.make_async_copy(z.at[t, :, :, a], z.at[t, :, :, a], z_in.at[t, a]).wait()

    def left_load(a):
        return pltpu.make_async_copy(left_in.at[a, 0], leftv.at[a], left_s.at[a])

    def hop_load(a):
        return pltpu.make_async_copy(hop_in.at[a, 0], hopv.at[a], hopv_s.at[a])

    def right_load(t, a):
        return pltpu.make_async_copy(right_in.at[a, 0, t], rightv.at[t, a], rightv_s.at[t, a])

    for a in range(arms):
        load(0, a)
        left_load(a).start()
        hop_load(a).start()
        right_load(0, a).start()
    for t in (2, 1):
        for a in range(arms):
            load(t, a)
    for t in (1, 2):
        for a in range(arms):
            right_load(t, a).start()

    def zup_copy(t, a):
        return pltpu.make_async_remote_copy(
            src_ref=sites[t].at[1, :, a, 0], dst_ref=zup.at[t, a], send_sem=zup_s.at[t, a],
            recv_sem=zup_r.at[t, a], device_id={"blk": nxt})

    def zlow_copy(t, a):
        return pltpu.make_async_remote_copy(
            src_ref=sites[t].at[0, :, a, 0], dst_ref=zlow.at[t, a], send_sem=zlow_s.at[t, a],
            recv_sem=zlow_r.at[t, a], device_id={"blk": prv})

    def wup_copy(t, a):
        return pltpu.make_async_remote_copy(
            src_ref=w.at[t, 1, a], dst_ref=wup.at[t, a], send_sem=wup_s.at[t, a],
            recv_sem=wup_r.at[t, a], device_id={"blk": nxt})

    def wlow_copy(t, a):
        return pltpu.make_async_remote_copy(
            src_ref=w.at[t, 0, a], dst_ref=wlow.at[t, a], send_sem=wlow_s.at[t, a],
            recv_sem=wlow_r.at[t, a], device_id={"blk": prv})

    def hup_copy(t, a):
        return pltpu.make_async_remote_copy(
            src_ref=hsrc.at[t, 1, a], dst_ref=hup.at[t, a], send_sem=hup_s.at[t, a],
            recv_sem=hup_r.at[t, a], device_id={"blk": nxt})

    def hlow_copy(t, a):
        return pltpu.make_async_remote_copy(
            src_ref=hsrc.at[t, 0, a], dst_ref=hlow.at[t, a], send_sem=hlow_s.at[t, a],
            recv_sem=hlow_r.at[t, a], device_id={"blk": prv})

    def right_copy(t, a):
        return pltpu.make_async_remote_copy(
            src_ref=right_in.at[a, 0, t, 0], dst_ref=rnext.at[t, a], send_sem=rn_s.at[t, a],
            recv_sem=rn_r.at[t, a], device_id={"blk": prv})

    def hop_copy(a):
        return pltpu.make_async_remote_copy(
            src_ref=hop_in.at[a, 0], dst_ref=lown.at[a], send_sem=hop_s.at[a],
            recv_sem=hop_r.at[a], device_id={"blk": nxt})

    def move_copy(t, n, a):
        buf = (pmove, gmove)[n]
        return pltpu.make_async_remote_copy(
            src_ref=buf.at[t, 0, a], dst_ref=buf.at[t, 1, a], send_sem=mv_s.at[t, n, a],
            recv_sem=mv_r.at[t, n, a], device_id={"blk": nxt})

    def start_up(*copies):
        @pl.when(has_next)
        def _():
            for copy in copies:
                copy.start()

    def start_low(*copies):
        @pl.when(has_prev)
        def _():
            for copy in copies:
                copy.start()

    def wait_up(*copies):
        @pl.when(has_prev)
        def _():
            for copy in copies:
                copy.wait_recv()

    def wait_low(*copies):
        @pl.when(has_next)
        def _():
            for copy in copies:
                copy.wait_recv()

    @pl.when(jnp.logical_not(has_prev))
    def _():
        for buf in (zup, wup, hup, lown):
            buf[...] = jnp.zeros_like(buf)
        for buf in (pmove, gmove):
            buf[:, 1] = jnp.zeros_like(buf[:, 1])

    @pl.when(jnp.logical_not(has_next))
    def _():
        for buf in (zlow, wlow, hlow, rnext):
            buf[...] = jnp.zeros_like(buf)

    part[...] = jnp.zeros_like(part)
    opart[...] = jnp.zeros_like(opart)
    occ_src[...] = jnp.zeros_like(occ_src)
    pl.semaphore_wait(barrier, count - 1 + total_arms_dev - 1)

    for a in range(arms):
        start_low(right_copy(0, a), zlow_copy(0, a))
        start_up(zup_copy(0, a), hop_copy(a))

    def start_reduce(r, a):
        @pl.loop(1, count)
        def _(d):
            pltpu.make_async_remote_copy(
                src_ref=part.at[r, a], dst_ref=red.at[r, a, d - 1], send_sem=red_s.at[r, a],
                recv_sem=red_r.at[r, a], device_id={"blk": peer(d)}).start()

    def reduced(r, a):
        pltpu.make_async_copy(red.at[r, a], red.at[r, a], red_r.at[r, a]).wait()
        whole = part[r, a] + jnp.sum(red[r, a], axis=0)
        return jnp.broadcast_to(jnp.sum(whole, axis=1, keepdims=True), whole.shape)

    def end_reduce(r, a):
        pltpu.make_async_copy(red.at[r, a], red.at[r, a], red_s.at[r, a]).wait()

    rows = lax.broadcasted_iota(jnp.int32, (width, width), 0)
    cols = lax.broadcasted_iota(jnp.int32, (width, width), 1)
    eye = jnp.where(rows == cols, 1.0, 0.0).astype(F32)
    zero = jnp.zeros((width, width), F32)

    def mask_of(m_left, m_right):
        one = jnp.where((rows < m_left) & (cols < m_right), 1.0, 0.0).astype(F32)
        return jnp.concatenate([one, one], axis=0)

    def row_mask(m):
        return jnp.where(rows < m, 1.0, 0.0).astype(F32)

    def next_dim(a, t):
        return jnp.where(has_next, dims[a, t, nxt], 0)

    def tensor(t, s, a):
        return jnp.concatenate([z[t, s, 0, a], z[t, s, 1, a]], axis=0)

    def mask_source(t, a):
        wait_load(t, a)
        for s in range(2):
            one = mask_of(dims[a, t, me], dims[a, t + 1, me] if s == 0 else next_dim(a, t + 1))
            one = one[:width]
            for p in range(2):
                z[t, s, p, a] = z[t, s, p, a] * one

    def from_below(t, a):
        both = jnp.concatenate([zup[t, a, 0], zup[t, a, 1]], axis=0)
        return split(both * mask_of(dims[a, t, prv], dims[a, t + 1, me]))

    def from_above(t, a):
        both = jnp.concatenate([zlow[t, a, 0], zlow[t, a, 1]], axis=0)
        return split(both * mask_of(dims[a, t, nxt], next_dim(a, t + 1)))

    @pl.loop(0, arms)
    def _(a):
        mask_source(0, a)
        left_load(a).wait()
        live = row_mask(dims[a, 0, me])
        left = leftv[a]
        put(lop, a, complex_block(0.5 * (left + left.T) * live, zero))
        hop_load(a).wait()
        both = mask_of(dims[a, 0, me], next_dim(a, 0))[:width]
        put(hu, a, complex_block(chain[0, a, 1] * hopv[a] * both, zero))
        erow[0, pl.ds(a, 1), :] = jnp.full((1, width), chain[0, a, 0], F32)
        erow[1, pl.ds(a, 1), :] = jnp.full((1, width), chain[1, a, 0], F32)

    def build_right(t, a):
        right_load(t, a).wait()
        wait_low(right_copy(t, a))
        own, other = rightv[t, a, 0], rnext[t, a]
        couple = chain[t, a, 2] * rightv[t, a, 1]
        first = 0.5 * (own + own.T)
        second = 0.5 * (other + other.T) + eye * erow[t, pl.ds(a, 1), :]
        keep = jnp.where(cols < dims[a, t + 1, me], 1.0, 0.0).astype(F32)
        keep_next = jnp.where(cols < next_dim(a, t + 1), 1.0, 0.0).astype(F32)
        top = jnp.concatenate([first * keep, couple * keep_next], axis=1)
        bottom = jnp.concatenate([couple.T * keep, second * keep_next], axis=1)
        put(rop, a, jnp.concatenate([top, bottom], axis=0))

    def set_image(a, image):
        y[0, a] = image[:, :width]
        y[1, a] = image[:, width:]

    def right_part(t, a):
        both = split(jnp.concatenate([tensor(t, 0, a), tensor(t, 1, a)], axis=1))
        set_image(a, dot3(both, get(rop, a)))

    def local_part(one, two, a):
        both = split(jnp.concatenate([one, two], axis=1))
        set_image(a, long_dot(
            rows_of(both) + rows_of(get(lop, a)), columns_of(get(rop, a)) + columns_of(both)))

    @pl.loop(0, arms)
    def _(a):
        build_right(0, a)
        local_part(tensor(0, 0, a), tensor(0, 1, a), a)

    @pl.loop(0, arms)
    def _(a):
        mask_source(2, a)
        empty, filled = tensor(2, 0, a), tensor(2, 1, a)
        square = column_sum(filled * filled)
        opart[pl.ds(a, 1), :] = square
        opart[pl.ds(arms + a, 1), :] = square + column_sum(empty * empty)

    @pl.loop(1, count)
    def _(d):
        pltpu.make_async_remote_copy(
            src_ref=opart, dst_ref=ored.at[d - 1], send_sem=ored_s,
            recv_sem=ored_r, device_id={"blk": peer(d)}).start()

    @pl.loop(0, arms)
    def _(a):
        mask_source(1, a)
        wait_up(hop_copy(a))
        put(hd, a, complex_block(
            chain[0, a, 1] * lown[a].T * mask_of(dims[a, 0, me], dims[a, 0, prv])[:width], zero))

    def add_row(r, a, n, row):
        part[r, a, n:n + 1, :] = row

    def row_of(a, n):
        return coef[a, n:n + 1, :]

    def set_row(a, n, value):
        coef[a, n:n + 1, :] = value

    for t in range(TENSORS):
        @pl.loop(0, arms)
        def _(a):
            wait_low(zlow_copy(t, a))
            wait_up(zup_copy(t, a))
            filled = y[1, a] + dot3(get(hu, a), from_above(t, a))
            empty = y[0, a]
            below = from_below(t, a)
            if t > 0:
                wait_up(move_copy(t - 1, 1, a))
                rate = chain[t, a, 1]
                put(hd, a, complex_block(
                    rate * gmove[t - 1, 1, a, 0], rate * gmove[t - 1, 1, a, 1]))
            empty = empty + dot3(get(hd, a), below)
            base = [tensor(t, s, a) for s in range(2)]
            if t > 0:
                wait_up(move_copy(t - 1, 0, a))
                packed = pmove[t - 1, 1, a]
                mirror = packed.T
                real = jnp.where(rows <= cols, packed, mirror)
                imag = jnp.where(rows > cols, packed, jnp.where(rows < cols, -mirror, 0.0))
                own = v1[0, a]
                put(lop, a, complex_block(own[:width] + real, own[width:] + imag))
                product = dot3(get(lop, a), split(jnp.concatenate(base, axis=1)))
                empty = empty + product[:, :width]
                filled = filled + product[:, width:]
            image = (empty, filled)
            for s in range(2):
                w[t, s, a] = image[s]
            sums = [0.0, 0.0, 0.0]
            for s in range(2):
                pairs = ((base[s], base[s]), (base[s], image[s]), (image[s], image[s]))
                for n, pair in enumerate(pairs):
                    sums[n] = sums[n] + column_sum(pair[0] * pair[1])
            for n in range(3):
                add_row(2 * t, a, n, sums[n])
            start_reduce(2 * t, a)
            start_up(wup_copy(t, a))
            start_low(wlow_copy(t, a))
            local_part(image[0], image[1], a)
            hsrc[t, 1, a] = packed_half(y[1, a], width, False)
            hsrc[t, 0, a] = packed_half(y[0, a], width, True)
            start_up(hup_copy(t, a))
            start_low(hlow_copy(t, a))
            for s, operator in enumerate((hd, hu)):
                own = packed_half(image[s], width, s == 1)
                own = jnp.concatenate([own, turned(own, width)], axis=0).astype(BF16)
                back[s, a] = lax.dot_general(
                    operator[0, a][:, :width], own, (((0,), (0,)), ((), ())),
                    preferred_element_type=F32)

        if t + 1 < TENSORS:
            for a in range(arms):
                start_low(right_copy(t + 1, a))

        if t == 0:
            pltpu.make_async_copy(ored, ored, ored_r).wait()
            whole = opart[...] + jnp.sum(ored[...], axis=0)
            opart_tot = jnp.broadcast_to(jnp.sum(whole, axis=1, keepdims=True), whole.shape)
            occ_src[0:arms, :] = opart_tot[0:arms] / (opart_tot[arms:2 * arms] + EPSILON)
            for d in range(1, total_arms_dev):
                pltpu.make_async_remote_copy(
                    src_ref=occ_src, dst_ref=occ_all.at[d - 1], send_sem=occ_s.at[d - 1],
                    recv_sem=occ_r.at[d - 1], device_id={"arm": arm_peer(d)}).start()

        @pl.loop(0, arms)
        def _(a):
            wait_low(wlow_copy(t, a))
            wait_up(wup_copy(t, a))
            filled = y[1, a] + dot3(get(hu, a), split(wlow[t, a]))
            empty = y[0, a] + dot3(get(hd, a), split(wup[t, a]))
            wait_low(hlow_copy(t, a))
            wait_up(hup_copy(t, a))
            tot = reduced(2 * t, a)
            norm_square = tot[0:1] + EPSILON
            norm = jnp.sqrt(norm_square)
            alpha = tot[1:2] / norm_square
            beta = jnp.sqrt(jnp.maximum(tot[2:3] / norm_square - alpha * alpha, 0.0) + EPSILON)
            inv = 1.0 / norm
            scale = inv / beta
            for n, value in enumerate((alpha, scale, inv, beta, norm, norm_square)):
                set_row(a, n, value)
            sums = [0.0] * 5
            fresh = []
            for s, second in enumerate((empty, filled)):
                first = w[t, s, a]
                vector = (first - alpha * tensor(t, s, a)) * scale
                new = (second - alpha * first) * scale
                before = first * inv
                v1[s, a] = vector
                v2[s, a] = new
                fresh.append(new)
                pairs = ((vector, new), (new, new), (before, new), (vector, before))
                for n, pair in enumerate(pairs):
                    sums[n] = sums[n] + column_sum(pair[0] * pair[1])
            both = jnp.concatenate(fresh, axis=1).astype(BF16)
            image = long_dot([both, lop[0, a]], [rop[0, a], both])
            for s in range(2):
                sums[4] = sums[4] + column_sum(fresh[s] * image[:, s * width:(s + 1) * width])

            def crossing(arrived, before, mine, operator, late):
                vector = (arrived - alpha * packed_half(before, width, late)) * scale
                image = jnp.dot(
                    operator[0, a][:, :width], vector.astype(BF16), preferred_element_type=F32)
                own = packed_half(mine, width, late)
                return 2.0 * column_sum(
                    own * image[:width] + turned(own, width) * image[width:])

            sums[4] = sums[4] + crossing(
                hup[t, a] + back[0, a], wup[t, a], fresh[0], hd, False)
            sums[4] = sums[4] + crossing(
                hlow[t, a] + back[1, a], wlow[t, a], fresh[1], hu, True)
            for n in range(5):
                add_row(2 * t + 1, a, n, sums[n])
            start_reduce(2 * t + 1, a)

        if t + 1 < TENSORS:
            for a in range(arms):
                start_up(zup_copy(t + 1, a))
                start_low(zlow_copy(t + 1, a))
        if t == 1:
            for d in range(1, total_arms_dev):
                pltpu.make_async_remote_copy(
                    src_ref=occ_src, dst_ref=occ_all.at[d - 1], send_sem=occ_s.at[d - 1],
                    recv_sem=occ_r.at[d - 1], device_id={"arm": arm_peer(d)}).wait()

            @pl.loop(0, arms)
            def _(a):
                energy = jnp.full((1, width), chain[2, a, 0], F32)
                for d in range(total_arms_dev):
                    owner = lax.rem(arm + total_arms_dev - d, total_arms_dev)
                    for j in range(arms):
                        values = occ_src[j:j + 1, :] if d == 0 else occ_all[d - 1, j:j + 1, :]
                        energy = energy + inter[a, owner * arms + j] * values
                erow[2, pl.ds(a, 1), :] = energy

        if t + 1 < TENSORS:
            @pl.loop(0, arms)
            def _(a):
                build_right(t + 1, a)
                right_part(t + 1, a)

        @pl.loop(0, arms)
        def _(a):
            alpha0, inverse, beta1, norm, norm_square = (row_of(a, n) for n in (0, 2, 3, 4, 5))
            tot = reduced(2 * t + 1, a)
            alpha1, square1, cross, link, third = (tot[n:n + 1] for n in range(5))
            beta2_square = jnp.maximum(square1 - alpha1 * alpha1 - beta1 * beta1, 0.0) + EPSILON
            beta2 = jnp.sqrt(beta2_square)
            alpha2 = (
                third - alpha1 * (2.0 * square1 - alpha1 * alpha1)
                - beta1 * (2.0 * cross - 2.0 * alpha1 * link - beta1 * alpha0)
            ) / beta2_square
            real, imag = exponential([alpha0, alpha1, alpha2], [beta1, beta2])
            last = 1.0 / beta2
            link_back = beta1 * inverse
            evolved = []
            squares = 0.0
            for s in range(2):
                re = im = 0.0
                base = tensor(t, s, a)
                second = v2[s, a] - alpha1 * v1[s, a] - link_back * base
                for k, part_of in enumerate((base, v1[s, a], second * last)):
                    factor = norm if k else 1.0
                    cosine, sine = real[k] * factor, imag[k] * factor
                    top, bottom = part_of[:width], part_of[width:]
                    re = re + cosine * top - sine * bottom
                    im = im + cosine * bottom + sine * top
                outs[t][s, 0, a, 0] = re
                outs[t][s, 1, a, 0] = im
                evolved.append((re, im))
                squares = squares + column_sum(re * re + im * im)
            if t + 1 < TENSORS:
                square = jnp.sum(squares, axis=1, keepdims=True)
                factor = SECTOR_BOUND / jnp.sqrt(
                    jnp.broadcast_to(square, (1, width)) + norm_square * (1.0 / count))
                x = [(re * factor, im * factor) for re, im in evolved]
                flip = [split(jnp.concatenate([re.T, im.T], axis=1)) for re, im in x]

                def wide(re, im):
                    return split(jnp.concatenate(
                        [jnp.concatenate([re, im], axis=1), jnp.concatenate([im, -re], axis=1)],
                        axis=0))

                linked = dot3(flip[1], wide(*x[0]))
                gmove[t, 0, a, 0] = linked[:, :width]
                gmove[t, 0, a, 1] = linked[:, width:]
                start_up(move_copy(t, 1, a))
                whole = split(jnp.concatenate(
                    [jnp.concatenate(pair, axis=0) for pair in x], axis=1))
                image = dot3(get(lop, a), whole)
                energy = erow[t, pl.ds(a, 1), :]
                lifted = dot3(flip[1], wide(
                    image[:width, width:] + energy * x[1][0],
                    image[width:, width:] + energy * x[1][1]))
                pmove[t, 0, a] = jnp.where(rows <= cols, lifted[:, :width], lifted[:, width:])
                start_up(move_copy(t, 0, a))
                own = dot3(flip[0], wide(image[:width, :width], image[width:, :width]))
                rate = chain[t + 1, a, 1]
                put(hu, a, complex_block(
                    rate * linked[:, :width].T, -rate * linked[:, width:].T))
                v1[0, a] = jnp.concatenate([own[:, :width], own[:, width:]], axis=0)

    @pl.when(has_next)
    def _():
        for a in range(arms):
            hop_copy(a).wait_send()
            for t in range(TENSORS):
                zup_copy(t, a).wait_send()
                wup_copy(t, a).wait_send()
                hup_copy(t, a).wait_send()
            for t in range(TENSORS - 1):
                for n in range(2):
                    move_copy(t, n, a).wait_send()

    @pl.when(has_prev)
    def _():
        for a in range(arms):
            for t in range(TENSORS):
                right_copy(t, a).wait_send()
                zlow_copy(t, a).wait_send()
                wlow_copy(t, a).wait_send()
                hlow_copy(t, a).wait_send()

    pltpu.make_async_copy(ored, ored, ored_s).wait()
    for a in range(arms):
        for r in range(2 * TENSORS):
            end_reduce(r, a)


def hand_kernel(a, b, c, x, y, z, sem):
    copies = [
        pltpu.make_async_copy(i.at[s, p], o.at[s, p], sem.at[4 * k + 2 * s + p])
        for k, (i, o) in enumerate(((a, x), (b, y), (c, z))) for s in range(2) for p in range(2)]
    for copy in copies:
        copy.start()
    for copy in copies:
        copy.wait()


def hand(outs):
    anywhere = pl.BlockSpec(memory_space=pl.ANY)
    return pl.pallas_call(
        hand_kernel, out_shape=tuple(jax.ShapeDtypeStruct(o.shape, o.dtype) for o in outs),
        in_specs=[pl.BlockSpec(memory_space=pltpu.VMEM)] * 3, out_specs=(anywhere,) * 3,
        scratch_shapes=[pltpu.SemaphoreType.DMA((12,))],
    )(*(pltpu.with_memory_space_constraint(o, pltpu.VMEM) for o in outs))


def on_device(count, arm_devices, *args):
    site = args[0]
    args = args[:6] + (jnp.transpose(args[6], (1, 0, 2)),) + args[7:]
    arms, width = site.shape[2], site.shape[-1]
    rounds = 2 * TENSORS
    occ_rows = -(-2 * arms // 8) * 8
    arm_rows = -(-arms // 8) * 8
    vmem, sems = pltpu.VMEM, pltpu.SemaphoreType.DMA
    state = vmem((2, arms, 2 * width, width), F32)
    source = vmem((TENSORS, arms, 2, width, width), F32)
    halo = vmem((TENSORS, arms, 2 * width, width), F32)
    square = vmem((TENSORS, arms, width, width), F32)
    operator = vmem((2, arms, 2 * width, 2 * width), BF16)
    block = vmem((arms, width, width), F32)
    whole = pl.BlockSpec(memory_space=pltpu.VMEM)
    distant = pl.BlockSpec(memory_space=pltpu.HBM)
    scalar = pl.BlockSpec(memory_space=pltpu.SMEM)
    out = pltpu.VMEM(site.shape, F32)
    each, single = sems((TENSORS, arms)), sems((arms,))
    moves, sums = sems((TENSORS - 1, 2, arms)), sems((rounds, arms))
    arm_sems = sems((max(arm_devices - 1, 1),))
    outs = pl.pallas_call(
        functools.partial(kernel, count, arms, arm_devices),
        out_shape=(out, out, out),
        in_specs=[distant] * 6 + [scalar] * 3,
        out_specs=(whole,) * 3,
        scratch_shapes=[
            vmem((TENSORS, 2, 2, arms, width, width), F32),
            vmem((TENSORS, 2, arms, 2 * width, width), F32),
            state, state, state, vmem((2, arms, width, width), F32),
            source, source, halo, halo,
            vmem((TENSORS, 2, arms, width, width), F32), square, square, square,
            vmem((TENSORS - 1, 2, arms, width, width), F32),
            vmem((TENSORS - 1, 2, arms, 2, width, width), F32),
            block, block, vmem((TENSORS, arms, 2, width, width), F32),
            operator, operator, operator, operator, block,
            vmem((rounds, arms, 8, width), F32),
            vmem((rounds, arms, count - 1, 8, width), F32),
            vmem((occ_rows, width), F32),
            vmem((count - 1, occ_rows, width), F32),
            vmem((arms, 8, width), F32),
            vmem((arm_rows, width), F32),
            vmem((max(arm_devices - 1, 1), arm_rows, width), F32),
            vmem((TENSORS, arm_rows, width), F32),
            each, single, single, each,
            each, each, each, each, each, each, each, each, each, each, each, each,
            each, each, single, single, moves, moves, sums, sums,
            pltpu.SemaphoreType.DMA, pltpu.SemaphoreType.DMA, arm_sems, arm_sems,
        ],
        compiler_params=pltpu.CompilerParams(
            collective_id=0, has_side_effects=True, vmem_limit_bytes=56 * 1024 * 1024
        ),
    )(*args)
    return hand(outs)


def solution(mesh):
    tensor = P(None, None, "arm", "blk", None, None)
    in_specs = (
        tensor, tensor, tensor,
        P("arm", "blk", None, None),
        P("arm", "blk", None, None),
        P("arm", "blk", None, None, None, None),
        P("arm", None, None),
        P("arm", None),
        P("arm", None, None),
    )
    body = functools.partial(on_device, mesh.shape["blk"], mesh.shape["arm"])
    return jax.shard_map(
        body, mesh=mesh, in_specs=in_specs, out_specs=(tensor, tensor, tensor), check_vma=False
    )
```

```python
import functools

import jax
import jax.numpy as jnp
from jax import lax
from jax.experimental import pallas as pl
from jax.experimental.pallas import tpu as pltpu
from jax.sharding import PartitionSpec as P

KRYLOV = 3
TENSORS = 3
TIME_STEP = 0.4
EPSILON = 1e-06
TAYLOR = 12
HALVINGS = 5
SECTOR_BOUND = 3.0
F32 = jnp.float32
BF16 = jnp.bfloat16


def split(x):
    high = x.astype(BF16)
    return high, (x - high.astype(F32)).astype(BF16)


def rows_of(a):
    return [a[0], a[0], a[1]]


def columns_of(b):
    return [b[0], b[1], b[0]]


def long_dot(left, right):
    return jnp.dot(
        jnp.concatenate(left, axis=1), jnp.concatenate(right, axis=0), preferred_element_type=F32)


def dot3(a, b):
    return long_dot(rows_of(a), columns_of(b))


def put(ref, a, x):
    high, low = split(x)
    ref[0, a] = high
    ref[1, a] = low


def get(ref, a):
    return ref[0, a], ref[1, a]


def complex_block(real, imag):
    return jnp.concatenate(
        [jnp.concatenate([real, -imag], axis=1), jnp.concatenate([imag, real], axis=1)], axis=0
    )


def packed_half(x, width, late):
    half = width // 2
    real, imag = x[:width], x[width:]
    first = lax.broadcasted_iota(jnp.int32, (width, width), 1) < half
    if late:
        return jnp.where(first, pltpu.roll(real, half, 1), imag)
    return jnp.where(first, real, pltpu.roll(imag, half, 1))


def turned(x, width):
    half = width // 2
    first = lax.broadcasted_iota(jnp.int32, (width, width), 1) < half
    other = pltpu.roll(x, half, 1)
    return jnp.where(first, other, -other)


def column_sum(x):
    return jnp.sum(x, axis=0, keepdims=True)


def exponential(alphas, betas):
    step = TIME_STEP / 2.0**HALVINGS
    zero = jnp.zeros_like(alphas[0])
    one = jnp.ones_like(zero)
    s = {(0, 0): alphas[0], (1, 1): alphas[1], (2, 2): alphas[2], (0, 1): betas[0], (1, 2): betas[1]}
    s = {key: step * value for key, value in s.items()}
    keys = [(0, 0), (0, 1), (0, 2), (1, 1), (1, 2), (2, 2)]

    def at(m, i, j):
        return m[(min(i, j), max(i, j))]

    def times_s(m):
        out = {}
        for i, j in keys:
            terms = [at(m, i, k) * at(s, k, j) for k in range(3) if abs(k - j) < 2]
            out[(i, j)] = functools.reduce(jnp.add, terms)
        return out

    power = {key: one if key[0] == key[1] else zero for key in keys}
    real = dict(power)
    imag = {key: zero for key in keys}
    for order in range(1, TAYLOR + 1):
        power = {key: value * (1.0 / order) for key, value in times_s(power).items()}
        phase = order % 4
        target = imag if phase % 2 else real
        for key in keys:
            target[key] = target[key] - power[key] if phase in (1, 2) else target[key] + power[key]
    for _ in range(HALVINGS):
        new_real, new_imag = {}, {}
        for i, j in keys:
            re = im = None
            for k in range(3):
                a, b, c, d = at(real, i, k), at(imag, i, k), at(real, k, j), at(imag, k, j)
                x, y = a * c - b * d, a * d + b * c
                re, im = (x, y) if re is None else (re + x, im + y)
            new_real[(i, j)], new_imag[(i, j)] = re, im
        real, imag = new_real, new_imag
    return [at(real, k, 0) for k in range(3)], [at(imag, k, 0) for k in range(3)]


def kernel(
    count, arms, total_arms_dev,
    site0, site1, site2, left_in, hop_in, right_in, chain, inter, dims,
    out0, out1, out2,
    z, w, y, h, kept, back, zup, zlow, wup, wlow, hsrc, hup, hlow, rnext, pmove, gmove,
    leftv, hopv, rightv, lop, rop, hu, hd, lown, part, red, opart, ored,
    occ_src, occ_all, erow,
    z_in, left_s, hopv_s, rightv_s,
    zup_s, zup_r, zlow_s, zlow_r, wup_s, wup_r, wlow_s, wlow_r, hup_s, hup_r, hlow_s, hlow_r,
    rn_s, rn_r, hop_s, hop_r, mv_s, mv_r, red_s, red_r, ored_s, ored_r, occ_s, occ_r,
):
    me = lax.axis_index("blk")
    arm = lax.axis_index("arm")
    width = left_in.shape[-1]
    sites, outs = (site0, site1, site2), (out0, out1, out2)
    has_next, has_prev = me < count - 1, me > 0
    nxt, prv = lax.rem(me + 1, count), lax.rem(me + count - 1, count)

    def peer(d):
        return lax.rem(me + d, count)

    def arm_peer(d):
        return lax.rem(arm + d, total_arms_dev)

    barrier = pltpu.get_barrier_semaphore()

    @pl.loop(1, count)
    def _(d):
        pl.semaphore_signal(barrier, inc=1, device_id={"blk": peer(d)})

    for d in range(1, total_arms_dev):
        pl.semaphore_signal(barrier, inc=1, device_id={"arm": arm_peer(d)})

    def load(t, a):
        for s in range(2):
            for p in range(2):
                pltpu.make_async_copy(
                    sites[t].at[s, p, a, 0], z.at[t, s, p, a], z_in.at[t, a]).start()

    def wait_load(t, a):
        pltpu.make_async_copy(z.at[t, :, :, a], z.at[t, :, :, a], z_in.at[t, a]).wait()

    def left_load(a):
        return pltpu.make_async_copy(left_in.at[a, 0], leftv.at[a], left_s.at[a])

    def hop_load(a):
        return pltpu.make_async_copy(hop_in.at[a, 0], hopv.at[a], hopv_s.at[a])

    def right_load(t, a):
        return pltpu.make_async_copy(right_in.at[a, 0, t], rightv.at[t, a], rightv_s.at[t, a])

    for a in range(arms):
        load(0, a)
        left_load(a).start()
        hop_load(a).start()
        right_load(0, a).start()
    for t in (2, 1):
        for a in range(arms):
            load(t, a)
    for t in (1, 2):
        for a in range(arms):
            right_load(t, a).start()

    def zup_copy(t, a):
        return pltpu.make_async_remote_copy(
            src_ref=sites[t].at[1, :, a, 0], dst_ref=zup.at[t, a], send_sem=zup_s.at[t, a],
            recv_sem=zup_r.at[t, a], device_id={"blk": nxt})

    def zlow_copy(t, a):
        return pltpu.make_async_remote_copy(
            src_ref=sites[t].at[0, :, a, 0], dst_ref=zlow.at[t, a], send_sem=zlow_s.at[t, a],
            recv_sem=zlow_r.at[t, a], device_id={"blk": prv})

    def wup_copy(t, a):
        return pltpu.make_async_remote_copy(
            src_ref=w.at[t, 1, a], dst_ref=wup.at[t, a], send_sem=wup_s.at[t, a],
            recv_sem=wup_r.at[t, a], device_id={"blk": nxt})

    def wlow_copy(t, a):
        return pltpu.make_async_remote_copy(
            src_ref=w.at[t, 0, a], dst_ref=wlow.at[t, a], send_sem=wlow_s.at[t, a],
            recv_sem=wlow_r.at[t, a], device_id={"blk": prv})

    def hup_copy(t, a):
        return pltpu.make_async_remote_copy(
            src_ref=hsrc.at[t, 1, a], dst_ref=hup.at[t, a], send_sem=hup_s.at[t, a],
            recv_sem=hup_r.at[t, a], device_id={"blk": nxt})

    def hlow_copy(t, a):
        return pltpu.make_async_remote_copy(
            src_ref=hsrc.at[t, 0, a], dst_ref=hlow.at[t, a], send_sem=hlow_s.at[t, a],
            recv_sem=hlow_r.at[t, a], device_id={"blk": prv})

    def right_copy(t, a):
        return pltpu.make_async_remote_copy(
            src_ref=right_in.at[a, 0, t, 0], dst_ref=rnext.at[t, a], send_sem=rn_s.at[t, a],
            recv_sem=rn_r.at[t, a], device_id={"blk": prv})

    def hop_copy(a):
        return pltpu.make_async_remote_copy(
            src_ref=hop_in.at[a, 0], dst_ref=lown.at[a], send_sem=hop_s.at[a],
            recv_sem=hop_r.at[a], device_id={"blk": nxt})

    def move_copy(t, n, a):
        buf = (pmove, gmove)[n]
        return pltpu.make_async_remote_copy(
            src_ref=buf.at[t, 0, a], dst_ref=buf.at[t, 1, a], send_sem=mv_s.at[t, n, a],
            recv_sem=mv_r.at[t, n, a], device_id={"blk": nxt})

    def start_up(*copies):
        @pl.when(has_next)
        def _():
            for copy in copies:
                copy.start()

    def start_low(*copies):
        @pl.when(has_prev)
        def _():
            for copy in copies:
                copy.start()

    def wait_up(*copies):
        @pl.when(has_prev)
        def _():
            for copy in copies:
                copy.wait_recv()

    def wait_low(*copies):
        @pl.when(has_next)
        def _():
            for copy in copies:
                copy.wait_recv()

    @pl.when(jnp.logical_not(has_prev))
    def _():
        for buf in (zup, wup, hup, lown):
            buf[...] = jnp.zeros_like(buf)
        for buf in (pmove, gmove):
            buf[:, 1] = jnp.zeros_like(buf[:, 1])

    @pl.when(jnp.logical_not(has_next))
    def _():
        for buf in (zlow, wlow, hlow, rnext):
            buf[...] = jnp.zeros_like(buf)

    part[...] = jnp.zeros_like(part)
    opart[...] = jnp.zeros_like(opart)
    occ_src[...] = jnp.zeros_like(occ_src)
    pl.semaphore_wait(barrier, count - 1 + total_arms_dev - 1)

    for a in range(arms):
        start_low(right_copy(0, a), zlow_copy(0, a))
        start_up(zup_copy(0, a), hop_copy(a))

    def start_reduce(r, a):
        @pl.loop(1, count)
        def _(d):
            pltpu.make_async_remote_copy(
                src_ref=part.at[r, a], dst_ref=red.at[r, a, d - 1], send_sem=red_s.at[r, a],
                recv_sem=red_r.at[r, a], device_id={"blk": peer(d)}).start()

    def reduced(r, a):
        pltpu.make_async_copy(red.at[r, a], red.at[r, a], red_r.at[r, a]).wait()
        whole = part[r, a] + jnp.sum(red[r, a], axis=0)
        return jnp.broadcast_to(jnp.sum(whole, axis=1, keepdims=True), whole.shape)

    def end_reduce(r, a):
        pltpu.make_async_copy(red.at[r, a], red.at[r, a], red_s.at[r, a]).wait()

    rows = lax.broadcasted_iota(jnp.int32, (width, width), 0)
    cols = lax.broadcasted_iota(jnp.int32, (width, width), 1)
    eye = jnp.where(rows == cols, 1.0, 0.0).astype(F32)
    zero = jnp.zeros((width, width), F32)

    def mask_of(m_left, m_right):
        one = jnp.where((rows < m_left) & (cols < m_right), 1.0, 0.0).astype(F32)
        return jnp.concatenate([one, one], axis=0)

    def row_mask(m):
        return jnp.where(rows < m, 1.0, 0.0).astype(F32)

    def next_dim(a, t):
        return jnp.where(has_next, dims[a, t, nxt], 0)

    def tensor(t, s, a):
        return jnp.concatenate([z[t, s, 0, a], z[t, s, 1, a]], axis=0)

    def mask_source(t, a):
        wait_load(t, a)
        for s in range(2):
            one = mask_of(dims[a, t, me], dims[a, t + 1, me] if s == 0 else next_dim(a, t + 1))
            one = one[:width]
            for p in range(2):
                z[t, s, p, a] = z[t, s, p, a] * one

    def from_below(t, a):
        both = jnp.concatenate([zup[t, a, 0], zup[t, a, 1]], axis=0)
        return split(both * mask_of(dims[a, t, prv], dims[a, t + 1, me]))

    def from_above(t, a):
        both = jnp.concatenate([zlow[t, a, 0], zlow[t, a, 1]], axis=0)
        return split(both * mask_of(dims[a, t, nxt], next_dim(a, t + 1)))

    @pl.loop(0, arms)
    def _(a):
        mask_source(0, a)
        left_load(a).wait()
        live = row_mask(dims[a, 0, me])
        left = leftv[a]
        put(lop, a, complex_block(0.5 * (left + left.T) * live, zero))
        hop_load(a).wait()
        both = mask_of(dims[a, 0, me], next_dim(a, 0))[:width]
        put(hu, a, complex_block(chain[0, a, 1] * hopv[a] * both, zero))
        erow[0, pl.ds(a, 1), :] = jnp.full((1, width), chain[0, a, 0], F32)
        erow[1, pl.ds(a, 1), :] = jnp.full((1, width), chain[1, a, 0], F32)

    def build_right(t, a):
        right_load(t, a).wait()
        wait_low(right_copy(t, a))
        own, other = rightv[t, a, 0], rnext[t, a]
        couple = chain[t, a, 2] * rightv[t, a, 1]
        middle = eye * (0.5 * erow[t, pl.ds(a, 1), :])
        first = 0.5 * (own + own.T) - middle
        second = 0.5 * (other + other.T) + middle
        keep = jnp.where(cols < dims[a, t + 1, me], 1.0, 0.0).astype(F32)
        keep_next = jnp.where(cols < next_dim(a, t + 1), 1.0, 0.0).astype(F32)
        top = jnp.concatenate([first * keep, couple * keep_next], axis=1)
        bottom = jnp.concatenate([couple.T * keep, second * keep_next], axis=1)
        put(rop, a, jnp.concatenate([top, bottom], axis=0))

    def set_image(a, image):
        y[0, a] = image[:, :width]
        y[1, a] = image[:, width:]

    def right_part(t, a):
        both = split(jnp.concatenate([tensor(t, 0, a), tensor(t, 1, a)], axis=1))
        set_image(a, dot3(both, get(rop, a)))

    def local_part(one, two, a):
        both = split(jnp.concatenate([one, two], axis=1))
        set_image(a, long_dot(
            rows_of(both) + rows_of(get(lop, a)), columns_of(get(rop, a)) + columns_of(both)))

    @pl.loop(0, arms)
    def _(a):
        build_right(0, a)
        local_part(tensor(0, 0, a), tensor(0, 1, a), a)

    @pl.loop(0, arms)
    def _(a):
        mask_source(2, a)
        empty, filled = tensor(2, 0, a), tensor(2, 1, a)
        square = column_sum(filled * filled)
        opart[pl.ds(a, 1), :] = square
        opart[pl.ds(arms + a, 1), :] = square + column_sum(empty * empty)

    @pl.loop(1, count)
    def _(d):
        pltpu.make_async_remote_copy(
            src_ref=opart, dst_ref=ored.at[d - 1], send_sem=ored_s,
            recv_sem=ored_r, device_id={"blk": peer(d)}).start()

    @pl.loop(0, arms)
    def _(a):
        mask_source(1, a)
        wait_up(hop_copy(a))
        put(hd, a, complex_block(
            chain[0, a, 1] * lown[a].T * mask_of(dims[a, 0, me], dims[a, 0, prv])[:width], zero))

    def add_row(r, a, n, row):
        part[r, a, n:n + 1, :] = row

    for t in range(TENSORS):
        @pl.loop(0, arms)
        def _(a):
            wait_low(zlow_copy(t, a))
            wait_up(zup_copy(t, a))
            filled = y[1, a] + dot3(get(hu, a), from_above(t, a))
            empty = y[0, a]
            below = from_below(t, a)
            if t > 0:
                wait_up(move_copy(t - 1, 1, a))
                rate = chain[t, a, 1]
                put(hd, a, complex_block(
                    rate * gmove[t - 1, 1, a, 0], rate * gmove[t - 1, 1, a, 1]))
            empty = empty + dot3(get(hd, a), below)
            base = [tensor(t, s, a) for s in range(2)]
            if t > 0:
                wait_up(move_copy(t - 1, 0, a))
                packed = pmove[t - 1, 1, a]
                mirror = packed.T
                real = jnp.where(rows <= cols, packed, mirror)
                imag = jnp.where(rows > cols, packed, jnp.where(rows < cols, -mirror, 0.0))
                own = kept[a]
                put(lop, a, complex_block(own[:width] + real, own[width:] + imag))
                product = dot3(get(lop, a), split(jnp.concatenate(base, axis=1)))
                empty = empty + product[:, :width]
                filled = filled + product[:, width:]
            image = (empty, filled)
            for s in range(2):
                w[t, s, a] = image[s]
            sums = [0.0, 0.0, 0.0]
            for s in range(2):
                pairs = ((base[s], base[s]), (base[s], image[s]), (image[s], image[s]))
                for n, pair in enumerate(pairs):
                    sums[n] = sums[n] + column_sum(pair[0] * pair[1])
            for n in range(3):
                add_row(t, a, n, sums[n])
            start_up(wup_copy(t, a))
            start_low(wlow_copy(t, a))
            local_part(image[0], image[1], a)
            hsrc[t, 1, a] = packed_half(y[1, a], width, False)
            hsrc[t, 0, a] = packed_half(y[0, a], width, True)
            start_up(hup_copy(t, a))
            start_low(hlow_copy(t, a))
            for s, operator in enumerate((hd, hu)):
                own = packed_half(image[s], width, s == 1)
                own = jnp.concatenate([own, turned(own, width)], axis=0).astype(BF16)
                back[s, a] = lax.dot_general(
                    operator[0, a][:, :width], own, (((0,), (0,)), ((), ())),
                    preferred_element_type=F32)

        if t + 1 < TENSORS:
            for a in range(arms):
                start_low(right_copy(t + 1, a))

        if t == 0:
            pltpu.make_async_copy(ored, ored, ored_r).wait()
            whole = opart[...] + jnp.sum(ored[...], axis=0)
            opart_tot = jnp.broadcast_to(jnp.sum(whole, axis=1, keepdims=True), whole.shape)
            occ_src[0:arms, :] = opart_tot[0:arms] / (opart_tot[arms:2 * arms] + EPSILON)
            for d in range(1, total_arms_dev):
                pltpu.make_async_remote_copy(
                    src_ref=occ_src, dst_ref=occ_all.at[d - 1], send_sem=occ_s.at[d - 1],
                    recv_sem=occ_r.at[d - 1], device_id={"arm": arm_peer(d)}).start()

        @pl.loop(0, arms)
        def _(a):
            wait_low(wlow_copy(t, a))
            wait_up(wup_copy(t, a))
            filled = y[1, a] + dot3(get(hu, a), split(wlow[t, a]))
            empty = y[0, a] + dot3(get(hd, a), split(wup[t, a]))
            fresh = (empty, filled)
            for s in range(2):
                h[s, a] = fresh[s]
            both = jnp.concatenate(fresh, axis=1).astype(BF16)
            image = long_dot(
                [both, both, lop[0, a]], [rop[0, a], rop[1, a], both])
            wait_low(hlow_copy(t, a))
            wait_up(hup_copy(t, a))

            def crossing(arrived, mine, operator, late):
                image = jnp.dot(
                    operator[0, a][:, :width], arrived.astype(BF16), preferred_element_type=F32)
                own = packed_half(mine, width, late)
                return 2.0 * column_sum(
                    own * image[:width] + turned(own, width) * image[width:])

            sums = [0.0, 0.0, crossing(hup[t, a] + back[0, a], empty, hd, False)]
            sums[2] = sums[2] + crossing(hlow[t, a] + back[1, a], filled, hu, True)
            for s in range(2):
                pairs = (
                    (w[t, s, a], fresh[s]), (fresh[s], fresh[s]),
                    (fresh[s], image[:, s * width:(s + 1) * width]))
                for n, pair in enumerate(pairs):
                    sums[n] = sums[n] + column_sum(pair[0] * pair[1])
            for n in range(3):
                add_row(t, a, 3 + n, sums[n])
            start_reduce(t, a)

        if t + 1 < TENSORS:
            for a in range(arms):
                start_up(zup_copy(t + 1, a))
                start_low(zlow_copy(t + 1, a))
        if t == 1:
            for d in range(1, total_arms_dev):
                pltpu.make_async_remote_copy(
                    src_ref=occ_src, dst_ref=occ_all.at[d - 1], send_sem=occ_s.at[d - 1],
                    recv_sem=occ_r.at[d - 1], device_id={"arm": arm_peer(d)}).wait()

            @pl.loop(0, arms)
            def _(a):
                energy = jnp.full((1, width), chain[2, a, 0], F32)
                for d in range(total_arms_dev):
                    owner = lax.rem(arm + total_arms_dev - d, total_arms_dev)
                    for j in range(arms):
                        values = occ_src[j:j + 1, :] if d == 0 else occ_all[d - 1, j:j + 1, :]
                        energy = energy + inter[a, owner * arms + j] * values
                erow[2, pl.ds(a, 1), :] = energy

        if t + 1 < TENSORS:
            @pl.loop(0, arms)
            def _(a):
                build_right(t + 1, a)
                right_part(t + 1, a)

        @pl.loop(0, arms)
        def _(a):
            tot = reduced(t, a)
            norm_square = tot[0:1] + EPSILON
            inverse = 1.0 / norm_square
            mean, second, third, fourth, fifth = (tot[n:n + 1] * inverse for n in range(1, 6))
            alpha0 = mean
            beta1_square = jnp.maximum(second - alpha0 * alpha0, 0.0) + EPSILON
            beta1 = jnp.sqrt(beta1_square)
            scale = 1.0 / beta1_square

            def moved_on(low, middle, high):
                return (high - alpha0 * (2.0 * middle - alpha0 * low)) * scale

            alpha1 = moved_on(mean, second, third)
            square1 = moved_on(second, third, fourth)
            cross_link = (third - alpha0 * second - alpha1 * (second - alpha0 * mean)) * 2.0
            beta2_square = jnp.maximum(square1 - alpha1 * alpha1 - beta1_square, 0.0) + EPSILON
            beta2 = jnp.sqrt(beta2_square)
            alpha2 = (
                moved_on(third, fourth, fifth) - alpha1 * (2.0 * square1 - alpha1 * alpha1)
                - cross_link + beta1_square * alpha0
            ) / beta2_square
            real, imag = exponential(
                [alpha + 0.5 * erow[t, pl.ds(a, 1), :] for alpha in (alpha0, alpha1, alpha2)],
                [beta1, beta2])

            def weights(e):
                middle, last = e[1] / beta1, e[2] / (beta1 * beta2)
                return (
                    e[0] - alpha0 * middle + (alpha0 * alpha1 - beta1_square) * last,
                    middle - (alpha0 + alpha1) * last, last)

            cosines, sines = weights(real), weights(imag)
            evolved = []
            squares = 0.0
            for s in range(2):
                re = im = 0.0
                for k, part_of in enumerate((tensor(t, s, a), w[t, s, a], h[s, a])):
                    cosine, sine = cosines[k], sines[k]
                    top, bottom = part_of[:width], part_of[width:]
                    re = re + cosine * top - sine * bottom
                    im = im + cosine * bottom + sine * top
                outs[t][s, 0, a, 0] = re
                outs[t][s, 1, a, 0] = im
                evolved.append((re, im))
                squares = squares + column_sum(re * re + im * im)
            if t + 1 < TENSORS:
                square = jnp.sum(squares, axis=1, keepdims=True)
                factor = SECTOR_BOUND / jnp.sqrt(
                    jnp.broadcast_to(square, (1, width)) + norm_square * (1.0 / count))
                x = [(re * factor, im * factor) for re, im in evolved]
                flip = [split(jnp.concatenate([re.T, im.T], axis=1)) for re, im in x]

                def wide(re, im):
                    return split(jnp.concatenate(
                        [jnp.concatenate([re, im], axis=1), jnp.concatenate([im, -re], axis=1)],
                        axis=0))

                linked = dot3(flip[1], wide(*x[0]))
                gmove[t, 0, a, 0] = linked[:, :width]
                gmove[t, 0, a, 1] = linked[:, width:]
                start_up(move_copy(t, 1, a))
                whole = split(jnp.concatenate(
                    [jnp.concatenate(pair, axis=0) for pair in x], axis=1))
                image = dot3(get(lop, a), whole)
                energy = erow[t, pl.ds(a, 1), :]
                lifted = dot3(flip[1], wide(
                    image[:width, width:] + energy * x[1][0],
                    image[width:, width:] + energy * x[1][1]))
                pmove[t, 0, a] = jnp.where(rows <= cols, lifted[:, :width], lifted[:, width:])
                start_up(move_copy(t, 0, a))
                own = dot3(flip[0], wide(image[:width, :width], image[width:, :width]))
                rate = chain[t + 1, a, 1]
                put(hu, a, complex_block(
                    rate * linked[:, :width].T, -rate * linked[:, width:].T))
                kept[a] = jnp.concatenate([own[:, :width], own[:, width:]], axis=0)

    @pl.when(has_next)
    def _():
        for a in range(arms):
            hop_copy(a).wait_send()
            for t in range(TENSORS):
                zup_copy(t, a).wait_send()
                wup_copy(t, a).wait_send()
                hup_copy(t, a).wait_send()
            for t in range(TENSORS - 1):
                for n in range(2):
                    move_copy(t, n, a).wait_send()

    @pl.when(has_prev)
    def _():
        for a in range(arms):
            for t in range(TENSORS):
                right_copy(t, a).wait_send()
                zlow_copy(t, a).wait_send()
                wlow_copy(t, a).wait_send()
                hlow_copy(t, a).wait_send()

    pltpu.make_async_copy(ored, ored, ored_s).wait()
    for a in range(arms):
        for t in range(TENSORS):
            end_reduce(t, a)


def hand_kernel(a, b, c, x, y, z, sem):
    copies = [
        pltpu.make_async_copy(i.at[s, p], o.at[s, p], sem.at[4 * k + 2 * s + p])
        for k, (i, o) in enumerate(((a, x), (b, y), (c, z))) for s in range(2) for p in range(2)]
    for copy in copies:
        copy.start()
    for copy in copies:
        copy.wait()


def hand(outs):
    anywhere = pl.BlockSpec(memory_space=pl.ANY)
    return pl.pallas_call(
        hand_kernel, out_shape=tuple(jax.ShapeDtypeStruct(o.shape, o.dtype) for o in outs),
        in_specs=[pl.BlockSpec(memory_space=pltpu.VMEM)] * 3, out_specs=(anywhere,) * 3,
        scratch_shapes=[pltpu.SemaphoreType.DMA((12,))],
    )(*(pltpu.with_memory_space_constraint(o, pltpu.VMEM) for o in outs))


def on_device(count, arm_devices, *args):
    site = args[0]
    args = args[:6] + (jnp.transpose(args[6], (1, 0, 2)),) + args[7:]
    arms, width = site.shape[2], site.shape[-1]
    occ_rows = -(-2 * arms // 8) * 8
    arm_rows = -(-arms // 8) * 8
    vmem, sems = pltpu.VMEM, pltpu.SemaphoreType.DMA
    state = vmem((2, arms, 2 * width, width), F32)
    source = vmem((TENSORS, arms, 2, width, width), F32)
    halo = vmem((TENSORS, arms, 2 * width, width), F32)
    square = vmem((TENSORS, arms, width, width), F32)
    operator = vmem((2, arms, 2 * width, 2 * width), BF16)
    block = vmem((arms, width, width), F32)
    whole = pl.BlockSpec(memory_space=pltpu.VMEM)
    distant = pl.BlockSpec(memory_space=pltpu.HBM)
    scalar = pl.BlockSpec(memory_space=pltpu.SMEM)
    out = pltpu.VMEM(site.shape, F32)
    each, single = sems((TENSORS, arms)), sems((arms,))
    moves, sums = sems((TENSORS - 1, 2, arms)), each
    arm_sems = sems((max(arm_devices - 1, 1),))
    outs = pl.pallas_call(
        functools.partial(kernel, count, arms, arm_devices),
        out_shape=(out, out, out),
        in_specs=[distant] * 6 + [scalar] * 3,
        out_specs=(whole,) * 3,
        scratch_shapes=[
            vmem((TENSORS, 2, 2, arms, width, width), F32),
            vmem((TENSORS, 2, arms, 2 * width, width), F32),
            state, state, vmem((arms, 2 * width, width), F32), vmem((2, arms, width, width), F32),
            source, source, halo, halo,
            vmem((TENSORS, 2, arms, width, width), F32), square, square, square,
            vmem((TENSORS - 1, 2, arms, width, width), F32),
            vmem((TENSORS - 1, 2, arms, 2, width, width), F32),
            block, block, vmem((TENSORS, arms, 2, width, width), F32),
            operator, operator, operator, operator, block,
            vmem((TENSORS, arms, 8, width), F32),
            vmem((TENSORS, arms, count - 1, 8, width), F32),
            vmem((occ_rows, width), F32),
            vmem((count - 1, occ_rows, width), F32),
            vmem((arm_rows, width), F32),
            vmem((max(arm_devices - 1, 1), arm_rows, width), F32),
            vmem((TENSORS, arm_rows, width), F32),
            each, single, single, each,
            each, each, each, each, each, each, each, each, each, each, each, each,
            each, each, single, single, moves, moves, sums, sums,
            pltpu.SemaphoreType.DMA, pltpu.SemaphoreType.DMA, arm_sems, arm_sems,
        ],
        compiler_params=pltpu.CompilerParams(
            collective_id=0, has_side_effects=True, vmem_limit_bytes=56 * 1024 * 1024
        ),
    )(*args)
    return hand(outs)


def solution(mesh):
    tensor = P(None, None, "arm", "blk", None, None)
    in_specs = (
        tensor, tensor, tensor,
        P("arm", "blk", None, None),
        P("arm", "blk", None, None),
        P("arm", "blk", None, None, None, None),
        P("arm", None, None),
        P("arm", None),
        P("arm", None, None),
    )
    body = functools.partial(on_device, mesh.shape["blk"], mesh.shape["arm"])
    return jax.shard_map(
        body, mesh=mesh, in_specs=in_specs, out_specs=(tensor, tensor, tensor), check_vma=False
    )
```

```python
import functools

import jax
import jax.numpy as jnp
from jax import lax
from jax.experimental import pallas as pl
from jax.experimental.pallas import tpu as pltpu
from jax.sharding import PartitionSpec as P

KRYLOV = 3
TENSORS = 3
TIME_STEP = 0.4
EPSILON = 1e-06
TAYLOR = 12
HALVINGS = 5
SECTOR_BOUND = 3.0
F32 = jnp.float32
BF16 = jnp.bfloat16


def split(x):
    high = x.astype(BF16)
    return high, (x - high.astype(F32)).astype(BF16)


def rows_of(a):
    return [a[0], a[0], a[1]]


def columns_of(b):
    return [b[0], b[1], b[0]]


def long_dot(left, right):
    return jnp.dot(
        jnp.concatenate(left, axis=1), jnp.concatenate(right, axis=0), preferred_element_type=F32)


def dot3(a, b):
    return long_dot(rows_of(a), columns_of(b))


def put(ref, a, x):
    high, low = split(x)
    ref[0, a] = high
    ref[1, a] = low


def get(ref, a):
    return ref[0, a], ref[1, a]


def complex_block(real, imag):
    return jnp.concatenate(
        [jnp.concatenate([real, -imag], axis=1), jnp.concatenate([imag, real], axis=1)], axis=0
    )


def packed_half(x, width, late):
    half = width // 2
    real, imag = x[:width], x[width:]
    first = lax.broadcasted_iota(jnp.int32, (width, width), 1) < half
    if late:
        return jnp.where(first, pltpu.roll(real, half, 1), imag)
    return jnp.where(first, real, pltpu.roll(imag, half, 1))


def turned(x, width):
    half = width // 2
    first = lax.broadcasted_iota(jnp.int32, (width, width), 1) < half
    other = pltpu.roll(x, half, 1)
    return jnp.where(first, other, -other)


def column_sum(x):
    return jnp.sum(x, axis=0, keepdims=True)


def exponential(alphas, betas):
    step = TIME_STEP / 2.0**HALVINGS
    zero = jnp.zeros_like(alphas[0])
    one = jnp.ones_like(zero)
    s = {(0, 0): alphas[0], (1, 1): alphas[1], (2, 2): alphas[2], (0, 1): betas[0], (1, 2): betas[1]}
    s = {key: step * value for key, value in s.items()}
    keys = [(0, 0), (0, 1), (0, 2), (1, 1), (1, 2), (2, 2)]

    def at(m, i, j):
        return m[(min(i, j), max(i, j))]

    def times_s(m):
        out = {}
        for i, j in keys:
            terms = [at(m, i, k) * at(s, k, j) for k in range(3) if abs(k - j) < 2]
            out[(i, j)] = functools.reduce(jnp.add, terms)
        return out

    power = {key: one if key[0] == key[1] else zero for key in keys}
    real = dict(power)
    imag = {key: zero for key in keys}
    for order in range(1, TAYLOR + 1):
        power = {key: value * (1.0 / order) for key, value in times_s(power).items()}
        phase = order % 4
        target = imag if phase % 2 else real
        for key in keys:
            target[key] = target[key] - power[key] if phase in (1, 2) else target[key] + power[key]
    for _ in range(HALVINGS):
        new_real, new_imag = {}, {}
        for i, j in keys:
            re = im = None
            for k in range(3):
                a, b, c, d = at(real, i, k), at(imag, i, k), at(real, k, j), at(imag, k, j)
                x, y = a * c - b * d, a * d + b * c
                re, im = (x, y) if re is None else (re + x, im + y)
            new_real[(i, j)], new_imag[(i, j)] = re, im
        real, imag = new_real, new_imag
    return [at(real, k, 0) for k in range(3)], [at(imag, k, 0) for k in range(3)]


def kernel(
    count, arms, total_arms_dev,
    site0, site1, site2, left_in, hop_in, right_in, chain, inter, dims,
    out0, out1, out2,
    z, w, y, h, kept, back, zup, zlow, wup, wlow, hsrc, hup, hlow, rnext, pmove, gmove,
    leftv, hopv, rightv, lop, rop, hu, hd, lown, part, red, opart, ored,
    occ_src, occ_all, erow,
    z_in, left_s, hopv_s, rightv_s,
    zup_s, zup_r, zlow_s, zlow_r, wup_s, wup_r, wlow_s, wlow_r, hup_s, hup_r, hlow_s, hlow_r,
    rn_s, rn_r, hop_s, hop_r, mv_s, mv_r, red_s, red_r, ored_s, ored_r, occ_s, occ_r,
):
    me = lax.axis_index("blk")
    arm = lax.axis_index("arm")
    width = left_in.shape[-1]
    sites, outs = (site0, site1, site2), (out0, out1, out2)
    has_next, has_prev = me < count - 1, me > 0
    nxt, prv = lax.rem(me + 1, count), lax.rem(me + count - 1, count)

    def peer(d):
        return lax.rem(me + d, count)

    def arm_peer(d):
        return lax.rem(arm + d, total_arms_dev)

    barrier = pltpu.get_barrier_semaphore()

    @pl.loop(1, count)
    def _(d):
        pl.semaphore_signal(barrier, inc=1, device_id={"blk": peer(d)})

    for d in range(1, total_arms_dev):
        pl.semaphore_signal(barrier, inc=1, device_id={"arm": arm_peer(d)})

    def load(t, a):
        for s in range(2):
            for p in range(2):
                pltpu.make_async_copy(
                    sites[t].at[s, p, a, 0], z.at[t, s, p, a], z_in.at[t, a]).start()

    def wait_load(t, a):
        pltpu.make_async_copy(z.at[t, :, :, a], z.at[t, :, :, a], z_in.at[t, a]).wait()

    def left_load(a):
        return pltpu.make_async_copy(left_in.at[a, 0], leftv.at[a], left_s.at[a])

    def hop_load(a):
        return pltpu.make_async_copy(hop_in.at[a, 0], hopv.at[a], hopv_s.at[a])

    def right_load(t, a):
        return pltpu.make_async_copy(right_in.at[a, 0, t], rightv.at[t, a], rightv_s.at[t, a])

    for a in range(arms):
        load(0, a)
        left_load(a).start()
        hop_load(a).start()
        right_load(0, a).start()
    for t in (2, 1):
        for a in range(arms):
            load(t, a)
    for t in (1, 2):
        for a in range(arms):
            right_load(t, a).start()

    def zup_copy(t, a):
        return pltpu.make_async_remote_copy(
            src_ref=sites[t].at[1, :, a, 0], dst_ref=zup.at[t, a], send_sem=zup_s.at[t, a],
            recv_sem=zup_r.at[t, a], device_id={"blk": nxt})

    def zlow_copy(t, a):
        return pltpu.make_async_remote_copy(
            src_ref=sites[t].at[0, :, a, 0], dst_ref=zlow.at[t, a], send_sem=zlow_s.at[t, a],
            recv_sem=zlow_r.at[t, a], device_id={"blk": prv})

    def wup_copy(t, a):
        return pltpu.make_async_remote_copy(
            src_ref=w.at[t, 1, a], dst_ref=wup.at[t, a], send_sem=wup_s.at[t, a],
            recv_sem=wup_r.at[t, a], device_id={"blk": nxt})

    def wlow_copy(t, a):
        return pltpu.make_async_remote_copy(
            src_ref=w.at[t, 0, a], dst_ref=wlow.at[t, a], send_sem=wlow_s.at[t, a],
            recv_sem=wlow_r.at[t, a], device_id={"blk": prv})

    def hup_copy(t, a):
        return pltpu.make_async_remote_copy(
            src_ref=hsrc.at[t, 1, a], dst_ref=hup.at[t, a], send_sem=hup_s.at[t, a],
            recv_sem=hup_r.at[t, a], device_id={"blk": nxt})

    def hlow_copy(t, a):
        return pltpu.make_async_remote_copy(
            src_ref=hsrc.at[t, 0, a], dst_ref=hlow.at[t, a], send_sem=hlow_s.at[t, a],
            recv_sem=hlow_r.at[t, a], device_id={"blk": prv})

    def right_copy(t, a):
        return pltpu.make_async_remote_copy(
            src_ref=right_in.at[a, 0, t, 0], dst_ref=rnext.at[t, a], send_sem=rn_s.at[t, a],
            recv_sem=rn_r.at[t, a], device_id={"blk": prv})

    def hop_copy(a):
        return pltpu.make_async_remote_copy(
            src_ref=hop_in.at[a, 0], dst_ref=lown.at[a], send_sem=hop_s.at[a],
            recv_sem=hop_r.at[a], device_id={"blk": nxt})

    def move_copy(t, n, a):
        buf = (pmove, gmove)[n]
        return pltpu.make_async_remote_copy(
            src_ref=buf.at[t, 0, a], dst_ref=buf.at[t, 1, a], send_sem=mv_s.at[t, n, a],
            recv_sem=mv_r.at[t, n, a], device_id={"blk": nxt})

    def start_up(*copies):
        @pl.when(has_next)
        def _():
            for copy in copies:
                copy.start()

    def start_low(*copies):
        @pl.when(has_prev)
        def _():
            for copy in copies:
                copy.start()

    def wait_up(*copies):
        @pl.when(has_prev)
        def _():
            for copy in copies:
                copy.wait_recv()

    def wait_low(*copies):
        @pl.when(has_next)
        def _():
            for copy in copies:
                copy.wait_recv()

    @pl.when(jnp.logical_not(has_prev))
    def _():
        for buf in (zup, wup, hup, lown):
            buf[...] = jnp.zeros_like(buf)
        for buf in (pmove, gmove):
            buf[:, 1] = jnp.zeros_like(buf[:, 1])

    @pl.when(jnp.logical_not(has_next))
    def _():
        for buf in (zlow, wlow, hlow, rnext):
            buf[...] = jnp.zeros_like(buf)

    part[...] = jnp.zeros_like(part)
    opart[...] = jnp.zeros_like(opart)
    occ_src[...] = jnp.zeros_like(occ_src)
    pl.semaphore_wait(barrier, count - 1 + total_arms_dev - 1)

    for a in range(arms):
        start_low(right_copy(0, a), zlow_copy(0, a))
        start_up(zup_copy(0, a), hop_copy(a))

    def start_reduce(r, a):
        @pl.loop(1, count)
        def _(d):
            pltpu.make_async_remote_copy(
                src_ref=part.at[r, a], dst_ref=red.at[r, a, d - 1], send_sem=red_s.at[r, a],
                recv_sem=red_r.at[r, a], device_id={"blk": peer(d)}).start()

    def reduced(r, a):
        pltpu.make_async_copy(red.at[r, a], red.at[r, a], red_r.at[r, a]).wait()
        whole = part[r, a] + jnp.sum(red[r, a], axis=0)
        return jnp.broadcast_to(jnp.sum(whole, axis=1, keepdims=True), whole.shape)

    def end_reduce(r, a):
        pltpu.make_async_copy(red.at[r, a], red.at[r, a], red_s.at[r, a]).wait()

    rows = lax.broadcasted_iota(jnp.int32, (width, width), 0)
    cols = lax.broadcasted_iota(jnp.int32, (width, width), 1)
    eye = jnp.where(rows == cols, 1.0, 0.0).astype(F32)
    zero = jnp.zeros((width, width), F32)

    def mask_of(m_left, m_right):
        one = jnp.where((rows < m_left) & (cols < m_right), 1.0, 0.0).astype(F32)
        return jnp.concatenate([one, one], axis=0)

    def row_mask(m):
        return jnp.where(rows < m, 1.0, 0.0).astype(F32)

    def next_dim(a, t):
        return jnp.where(has_next, dims[a, t, nxt], 0)

    def tensor(t, s, a):
        return jnp.concatenate([z[t, s, 0, a], z[t, s, 1, a]], axis=0)

    def mask_source(t, a):
        wait_load(t, a)
        for s in range(2):
            one = mask_of(dims[a, t, me], dims[a, t + 1, me] if s == 0 else next_dim(a, t + 1))
            one = one[:width]
            for p in range(2):
                z[t, s, p, a] = z[t, s, p, a] * one

    def from_below(t, a):
        both = jnp.concatenate([zup[t, a, 0], zup[t, a, 1]], axis=0)
        return split(both * mask_of(dims[a, t, prv], dims[a, t + 1, me]))

    def from_above(t, a):
        both = jnp.concatenate([zlow[t, a, 0], zlow[t, a, 1]], axis=0)
        return split(both * mask_of(dims[a, t, nxt], next_dim(a, t + 1)))

    @pl.loop(0, arms)
    def _(a):
        mask_source(0, a)
        left_load(a).wait()
        live = row_mask(dims[a, 0, me])
        left = leftv[a]
        put(lop, a, complex_block(0.5 * (left + left.T) * live, zero))
        hop_load(a).wait()
        both = mask_of(dims[a, 0, me], next_dim(a, 0))[:width]
        put(hu, a, complex_block(chain[0, a, 1] * hopv[a] * both, zero))
        erow[0, pl.ds(a, 1), :] = jnp.full((1, width), chain[0, a, 0], F32)
        erow[1, pl.ds(a, 1), :] = jnp.full((1, width), chain[1, a, 0], F32)

    def build_right(t, a):
        right_load(t, a).wait()
        wait_low(right_copy(t, a))
        own, other = rightv[t, a, 0], rnext[t, a]
        couple = chain[t, a, 2] * rightv[t, a, 1]
        middle = eye * (0.5 * erow[t, pl.ds(a, 1), :])
        first = 0.5 * (own + own.T) - middle
        second = 0.5 * (other + other.T) + middle
        keep = jnp.where(cols < dims[a, t + 1, me], 1.0, 0.0).astype(F32)
        keep_next = jnp.where(cols < next_dim(a, t + 1), 1.0, 0.0).astype(F32)
        top = jnp.concatenate([first * keep, couple * keep_next], axis=1)
        bottom = jnp.concatenate([couple.T * keep, second * keep_next], axis=1)
        put(rop, a, jnp.concatenate([top, bottom], axis=0))

    def set_image(a, image):
        y[0, a] = image[:, :width]
        y[1, a] = image[:, width:]

    def right_part(t, a):
        both = split(jnp.concatenate([tensor(t, 0, a), tensor(t, 1, a)], axis=1))
        set_image(a, dot3(both, get(rop, a)))

    def local_part(one, two, a):
        both = split(jnp.concatenate([one, two], axis=1))
        set_image(a, long_dot(
            rows_of(both) + rows_of(get(lop, a)), columns_of(get(rop, a)) + columns_of(both)))

    @pl.loop(0, arms)
    def _(a):
        mask_source(2, a)
        empty, filled = tensor(2, 0, a), tensor(2, 1, a)
        square = column_sum(filled * filled)
        opart[pl.ds(a, 1), :] = square
        opart[pl.ds(arms + a, 1), :] = square + column_sum(empty * empty)

    @pl.loop(1, count)
    def _(d):
        pltpu.make_async_remote_copy(
            src_ref=opart, dst_ref=ored.at[d - 1], send_sem=ored_s,
            recv_sem=ored_r, device_id={"blk": peer(d)}).start()

    @pl.loop(0, arms)
    def _(a):
        mask_source(1, a)

    def add_row(r, a, n, row):
        part[r, a, n:n + 1, :] = row

    for t in range(TENSORS):
        @pl.loop(0, arms)
        def _(a):
            if t == 0:
                build_right(0, a)
                local_part(tensor(0, 0, a), tensor(0, 1, a), a)
                wait_up(hop_copy(a))
                put(hd, a, complex_block(
                    chain[0, a, 1] * lown[a].T * mask_of(dims[a, 0, me], dims[a, 0, prv])[:width],
                    zero))
            wait_low(zlow_copy(t, a))
            wait_up(zup_copy(t, a))
            filled = y[1, a] + dot3(get(hu, a), from_above(t, a))
            empty = y[0, a]
            below = from_below(t, a)
            if t > 0:
                wait_up(move_copy(t - 1, 1, a))
                rate = chain[t, a, 1]
                put(hd, a, complex_block(
                    rate * gmove[t - 1, 1, a, 0], rate * gmove[t - 1, 1, a, 1]))
            empty = empty + dot3(get(hd, a), below)
            base = [tensor(t, s, a) for s in range(2)]
            if t > 0:
                wait_up(move_copy(t - 1, 0, a))
                packed = pmove[t - 1, 1, a]
                mirror = packed.T
                real = jnp.where(rows <= cols, packed, mirror)
                imag = jnp.where(rows > cols, packed, jnp.where(rows < cols, -mirror, 0.0))
                own = kept[a]
                put(lop, a, complex_block(own[:width] + real, own[width:] + imag))
                product = dot3(get(lop, a), split(jnp.concatenate(base, axis=1)))
                empty = empty + product[:, :width]
                filled = filled + product[:, width:]
            image = (empty, filled)
            for s in range(2):
                w[t, s, a] = image[s]
            start_up(wup_copy(t, a))
            start_low(wlow_copy(t, a))
            sums = [0.0, 0.0, 0.0]
            for s in range(2):
                pairs = ((base[s], base[s]), (base[s], image[s]), (image[s], image[s]))
                for n, pair in enumerate(pairs):
                    sums[n] = sums[n] + column_sum(pair[0] * pair[1])
            for n in range(3):
                add_row(t, a, n, sums[n])
            local_part(image[0], image[1], a)
            hsrc[t, 1, a] = packed_half(y[1, a], width, False)
            hsrc[t, 0, a] = packed_half(y[0, a], width, True)
            start_up(hup_copy(t, a))
            start_low(hlow_copy(t, a))
            for s, operator in enumerate((hd, hu)):
                own = packed_half(image[s], width, s == 1)
                own = jnp.concatenate([own, turned(own, width)], axis=0).astype(BF16)
                back[s, a] = lax.dot_general(
                    operator[0, a][:, :width], own, (((0,), (0,)), ((), ())),
                    preferred_element_type=F32)

        if t + 1 < TENSORS:
            for a in range(arms):
                start_low(right_copy(t + 1, a))

        @pl.loop(0, arms)
        def _(a):
            wait_low(wlow_copy(t, a))
            wait_up(wup_copy(t, a))
            filled = y[1, a] + dot3(get(hu, a), split(wlow[t, a]))
            empty = y[0, a] + dot3(get(hd, a), split(wup[t, a]))
            fresh = (empty, filled)
            for s in range(2):
                h[s, a] = fresh[s]
            both = jnp.concatenate(fresh, axis=1).astype(BF16)
            image = long_dot(
                [both, both, lop[0, a]], [rop[0, a], rop[1, a], both])
            wait_low(hlow_copy(t, a))
            wait_up(hup_copy(t, a))

            def crossing(arrived, mine, operator, late):
                image = jnp.dot(
                    operator[0, a][:, :width], arrived.astype(BF16), preferred_element_type=F32)
                own = packed_half(mine, width, late)
                return 2.0 * column_sum(
                    own * image[:width] + turned(own, width) * image[width:])

            sums = [0.0, 0.0, crossing(hup[t, a] + back[0, a], empty, hd, False)]
            sums[2] = sums[2] + crossing(hlow[t, a] + back[1, a], filled, hu, True)
            for s in range(2):
                pairs = (
                    (w[t, s, a], fresh[s]), (fresh[s], fresh[s]),
                    (fresh[s], image[:, s * width:(s + 1) * width]))
                for n, pair in enumerate(pairs):
                    sums[n] = sums[n] + column_sum(pair[0] * pair[1])
            for n in range(3):
                add_row(t, a, 3 + n, sums[n])
            start_reduce(t, a)

        if t + 1 < TENSORS:
            for a in range(arms):
                start_up(zup_copy(t + 1, a))
                start_low(zlow_copy(t + 1, a))
        if t == 0:
            pltpu.make_async_copy(ored, ored, ored_r).wait()
            whole = opart[...] + jnp.sum(ored[...], axis=0)
            opart_tot = jnp.broadcast_to(jnp.sum(whole, axis=1, keepdims=True), whole.shape)
            occ_src[0:arms, :] = opart_tot[0:arms] / (opart_tot[arms:2 * arms] + EPSILON)
            for d in range(1, total_arms_dev):
                pltpu.make_async_remote_copy(
                    src_ref=occ_src, dst_ref=occ_all.at[d - 1], send_sem=occ_s.at[d - 1],
                    recv_sem=occ_r.at[d - 1], device_id={"arm": arm_peer(d)}).start()
        if t == 1:
            for d in range(1, total_arms_dev):
                pltpu.make_async_remote_copy(
                    src_ref=occ_src, dst_ref=occ_all.at[d - 1], send_sem=occ_s.at[d - 1],
                    recv_sem=occ_r.at[d - 1], device_id={"arm": arm_peer(d)}).wait()

            @pl.loop(0, arms)
            def _(a):
                energy = jnp.full((1, width), chain[2, a, 0], F32)
                for d in range(total_arms_dev):
                    owner = lax.rem(arm + total_arms_dev - d, total_arms_dev)
                    for j in range(arms):
                        values = occ_src[j:j + 1, :] if d == 0 else occ_all[d - 1, j:j + 1, :]
                        energy = energy + inter[a, owner * arms + j] * values
                erow[2, pl.ds(a, 1), :] = energy

        if t + 1 < TENSORS:
            @pl.loop(0, arms)
            def _(a):
                build_right(t + 1, a)
                right_part(t + 1, a)

        @pl.loop(0, arms)
        def _(a):
            tot = reduced(t, a)
            norm_square = tot[0:1] + EPSILON
            inverse = 1.0 / norm_square
            mean, second, third, fourth, fifth = (tot[n:n + 1] * inverse for n in range(1, 6))
            alpha0 = mean
            beta1_square = jnp.maximum(second - alpha0 * alpha0, 0.0) + EPSILON
            beta1 = jnp.sqrt(beta1_square)
            scale = 1.0 / beta1_square

            def moved_on(low, middle, high):
                return (high - alpha0 * (2.0 * middle - alpha0 * low)) * scale

            alpha1 = moved_on(mean, second, third)
            square1 = moved_on(second, third, fourth)
            cross_link = (third - alpha0 * second - alpha1 * (second - alpha0 * mean)) * 2.0
            beta2_square = jnp.maximum(square1 - alpha1 * alpha1 - beta1_square, 0.0) + EPSILON
            beta2 = jnp.sqrt(beta2_square)
            alpha2 = (
                moved_on(third, fourth, fifth) - alpha1 * (2.0 * square1 - alpha1 * alpha1)
                - cross_link + beta1_square * alpha0
            ) / beta2_square
            real, imag = exponential(
                [alpha + 0.5 * erow[t, pl.ds(a, 1), :] for alpha in (alpha0, alpha1, alpha2)],
                [beta1, beta2])

            def weights(e):
                middle, last = e[1] / beta1, e[2] / (beta1 * beta2)
                return (
                    e[0] - alpha0 * middle + (alpha0 * alpha1 - beta1_square) * last,
                    middle - (alpha0 + alpha1) * last, last)

            cosines, sines = weights(real), weights(imag)
            evolved = []
            squares = 0.0
            for s in range(2):
                re = im = 0.0
                for k, part_of in enumerate((tensor(t, s, a), w[t, s, a], h[s, a])):
                    cosine, sine = cosines[k], sines[k]
                    top, bottom = part_of[:width], part_of[width:]
                    re = re + cosine * top - sine * bottom
                    im = im + cosine * bottom + sine * top
                outs[t][s, 0, a, 0] = re
                outs[t][s, 1, a, 0] = im
                evolved.append((re, im))
                squares = squares + column_sum(re * re + im * im)
            if t + 1 < TENSORS:
                square = jnp.sum(squares, axis=1, keepdims=True)
                factor = SECTOR_BOUND / jnp.sqrt(
                    jnp.broadcast_to(square, (1, width)) + norm_square * (1.0 / count))
                x = [(re * factor, im * factor) for re, im in evolved]
                flip = [split(jnp.concatenate([re.T, im.T], axis=1)) for re, im in x]

                def wide(re, im):
                    return split(jnp.concatenate(
                        [jnp.concatenate([re, im], axis=1), jnp.concatenate([im, -re], axis=1)],
                        axis=0))

                linked = dot3(flip[1], wide(*x[0]))
                gmove[t, 0, a, 0] = linked[:, :width]
                gmove[t, 0, a, 1] = linked[:, width:]
                start_up(move_copy(t, 1, a))
                whole = split(jnp.concatenate(
                    [jnp.concatenate(pair, axis=0) for pair in x], axis=1))
                image = dot3(get(lop, a), whole)
                energy = erow[t, pl.ds(a, 1), :]
                lifted = dot3(flip[1], wide(
                    image[:width, width:] + energy * x[1][0],
                    image[width:, width:] + energy * x[1][1]))
                pmove[t, 0, a] = jnp.where(rows <= cols, lifted[:, :width], lifted[:, width:])
                start_up(move_copy(t, 0, a))
                own = dot3(flip[0], wide(image[:width, :width], image[width:, :width]))
                rate = chain[t + 1, a, 1]
                put(hu, a, complex_block(
                    rate * linked[:, :width].T, -rate * linked[:, width:].T))
                kept[a] = jnp.concatenate([own[:, :width], own[:, width:]], axis=0)

    @pl.when(has_next)
    def _():
        for a in range(arms):
            hop_copy(a).wait_send()
            for t in range(TENSORS):
                zup_copy(t, a).wait_send()
                wup_copy(t, a).wait_send()
                hup_copy(t, a).wait_send()
            for t in range(TENSORS - 1):
                for n in range(2):
                    move_copy(t, n, a).wait_send()

    @pl.when(has_prev)
    def _():
        for a in range(arms):
            for t in range(TENSORS):
                right_copy(t, a).wait_send()
                zlow_copy(t, a).wait_send()
                wlow_copy(t, a).wait_send()
                hlow_copy(t, a).wait_send()

    pltpu.make_async_copy(ored, ored, ored_s).wait()
    for a in range(arms):
        for t in range(TENSORS):
            end_reduce(t, a)


def hand_kernel(a, b, c, x, y, z, sem):
    copies = [
        pltpu.make_async_copy(i.at[s, p], o.at[s, p], sem.at[4 * k + 2 * s + p])
        for k, (i, o) in enumerate(((a, x), (b, y), (c, z))) for s in range(2) for p in range(2)]
    for copy in copies:
        copy.start()
    for copy in copies:
        copy.wait()


def hand(outs):
    anywhere = pl.BlockSpec(memory_space=pl.ANY)
    return pl.pallas_call(
        hand_kernel, out_shape=tuple(jax.ShapeDtypeStruct(o.shape, o.dtype) for o in outs),
        in_specs=[pl.BlockSpec(memory_space=pltpu.VMEM)] * 3, out_specs=(anywhere,) * 3,
        scratch_shapes=[pltpu.SemaphoreType.DMA((12,))],
    )(*(pltpu.with_memory_space_constraint(o, pltpu.VMEM) for o in outs))


def on_device(count, arm_devices, *args):
    site = args[0]
    args = args[:6] + (jnp.transpose(args[6], (1, 0, 2)),) + args[7:]
    arms, width = site.shape[2], site.shape[-1]
    occ_rows = -(-2 * arms // 8) * 8
    arm_rows = -(-arms // 8) * 8
    vmem, sems = pltpu.VMEM, pltpu.SemaphoreType.DMA
    state = vmem((2, arms, 2 * width, width), F32)
    source = vmem((TENSORS, arms, 2, width, width), F32)
    halo = vmem((TENSORS, arms, 2 * width, width), F32)
    square = vmem((TENSORS, arms, width, width), F32)
    operator = vmem((2, arms, 2 * width, 2 * width), BF16)
    block = vmem((arms, width, width), F32)
    whole = pl.BlockSpec(memory_space=pltpu.VMEM)
    distant = pl.BlockSpec(memory_space=pltpu.HBM)
    scalar = pl.BlockSpec(memory_space=pltpu.SMEM)
    out = pltpu.VMEM(site.shape, F32)
    each, single = sems((TENSORS, arms)), sems((arms,))
    moves, sums = sems((TENSORS - 1, 2, arms)), each
    arm_sems = sems((max(arm_devices - 1, 1),))
    outs = pl.pallas_call(
        functools.partial(kernel, count, arms, arm_devices),
        out_shape=(out, out, out),
        in_specs=[distant] * 6 + [scalar] * 3,
        out_specs=(whole,) * 3,
        scratch_shapes=[
            vmem((TENSORS, 2, 2, arms, width, width), F32),
            vmem((TENSORS, 2, arms, 2 * width, width), F32),
            state, state, vmem((arms, 2 * width, width), F32), vmem((2, arms, width, width), F32),
            source, source, halo, halo,
            vmem((TENSORS, 2, arms, width, width), F32), square, square, square,
            vmem((TENSORS - 1, 2, arms, width, width), F32),
            vmem((TENSORS - 1, 2, arms, 2, width, width), F32),
            block, block, vmem((TENSORS, arms, 2, width, width), F32),
            operator, operator, operator, operator, block,
            vmem((TENSORS, arms, 8, width), F32),
            vmem((TENSORS, arms, count - 1, 8, width), F32),
            vmem((occ_rows, width), F32),
            vmem((count - 1, occ_rows, width), F32),
            vmem((arm_rows, width), F32),
            vmem((max(arm_devices - 1, 1), arm_rows, width), F32),
            vmem((TENSORS, arm_rows, width), F32),
            each, single, single, each,
            each, each, each, each, each, each, each, each, each, each, each, each,
            each, each, single, single, moves, moves, sums, sums,
            pltpu.SemaphoreType.DMA, pltpu.SemaphoreType.DMA, arm_sems, arm_sems,
        ],
        compiler_params=pltpu.CompilerParams(
            collective_id=0, has_side_effects=True, vmem_limit_bytes=56 * 1024 * 1024
        ),
    )(*args)
    return hand(outs)


def solution(mesh):
    tensor = P(None, None, "arm", "blk", None, None)
    in_specs = (
        tensor, tensor, tensor,
        P("arm", "blk", None, None),
        P("arm", "blk", None, None),
        P("arm", "blk", None, None, None, None),
        P("arm", None, None),
        P("arm", None),
        P("arm", None, None),
    )
    body = functools.partial(on_device, mesh.shape["blk"], mesh.shape["arm"])
    return jax.shard_map(
        body, mesh=mesh, in_specs=in_specs, out_specs=(tensor, tensor, tensor), check_vma=False
    )
```

```python
import functools

import jax
import jax.numpy as jnp
from jax import lax
from jax.experimental import pallas as pl
from jax.experimental.pallas import tpu as pltpu
from jax.sharding import PartitionSpec as P

KRYLOV = 3
TENSORS = 3
TIME_STEP = 0.4
EPSILON = 1e-06
TAYLOR = 12
HALVINGS = 5
SECTOR_BOUND = 3.0
F32 = jnp.float32
BF16 = jnp.bfloat16


def split(x):
    high = x.astype(BF16)
    return high, (x - high.astype(F32)).astype(BF16)


def rows_of(a):
    return [a[0], a[0], a[1]]


def columns_of(b):
    return [b[0], b[1], b[0]]


def long_dot(left, right):
    return jnp.dot(
        jnp.concatenate(left, axis=1), jnp.concatenate(right, axis=0), preferred_element_type=F32)


def dot3(a, b):
    return long_dot(rows_of(a), columns_of(b))


def put(ref, a, x):
    high, low = split(x)
    ref[0, a] = high
    ref[1, a] = low


def get(ref, a):
    return ref[0, a], ref[1, a]


def complex_block(real, imag):
    return jnp.concatenate(
        [jnp.concatenate([real, -imag], axis=1), jnp.concatenate([imag, real], axis=1)], axis=0
    )


def packed_half(x, width, late):
    half = width // 2
    real, imag = x[:width], x[width:]
    first = lax.broadcasted_iota(jnp.int32, (width, width), 1) < half
    if late:
        return jnp.where(first, pltpu.roll(real, half, 1), imag)
    return jnp.where(first, real, pltpu.roll(imag, half, 1))


def turned(x, width):
    half = width // 2
    first = lax.broadcasted_iota(jnp.int32, (width, width), 1) < half
    other = pltpu.roll(x, half, 1)
    return jnp.where(first, other, -other)


def column_sum(x):
    return jnp.sum(x, axis=0, keepdims=True)


def exponential(alphas, betas):
    step = TIME_STEP / 2.0**HALVINGS
    zero = jnp.zeros_like(alphas[0])
    one = jnp.ones_like(zero)
    s = {(0, 0): alphas[0], (1, 1): alphas[1], (2, 2): alphas[2], (0, 1): betas[0], (1, 2): betas[1]}
    s = {key: step * value for key, value in s.items()}
    keys = [(0, 0), (0, 1), (0, 2), (1, 1), (1, 2), (2, 2)]

    def at(m, i, j):
        return m[(min(i, j), max(i, j))]

    def times_s(m):
        out = {}
        for i, j in keys:
            terms = [at(m, i, k) * at(s, k, j) for k in range(3) if abs(k - j) < 2]
            out[(i, j)] = functools.reduce(jnp.add, terms)
        return out

    power = {key: one if key[0] == key[1] else zero for key in keys}
    real = dict(power)
    imag = {key: zero for key in keys}
    for order in range(1, TAYLOR + 1):
        power = {key: value * (1.0 / order) for key, value in times_s(power).items()}
        phase = order % 4
        target = imag if phase % 2 else real
        for key in keys:
            target[key] = target[key] - power[key] if phase in (1, 2) else target[key] + power[key]
    for _ in range(HALVINGS):
        new_real, new_imag = {}, {}
        for i, j in keys:
            re = im = None
            for k in range(3):
                a, b, c, d = at(real, i, k), at(imag, i, k), at(real, k, j), at(imag, k, j)
                x, y = a * c - b * d, a * d + b * c
                re, im = (x, y) if re is None else (re + x, im + y)
            new_real[(i, j)], new_imag[(i, j)] = re, im
        real, imag = new_real, new_imag
    return [at(real, k, 0) for k in range(3)], [at(imag, k, 0) for k in range(3)]


def kernel(
    count, arms, total_arms_dev,
    site0, site1, site2, left_in, hop_in, right_in, chain, inter, dims,
    out0, out1, out2,
    z, w, y, h, kept, back, zup, zlow, wup, wlow, hsrc, hup, hlow, rnext, pmove, gmove,
    leftv, hopv, rightv, lop, rop, hu, hd, lown, part, red, opart, ored,
    occ_src, occ_all, erow,
    z_in, left_s, hopv_s, rightv_s,
    zup_s, zup_r, zlow_s, zlow_r, wup_s, wup_r, wlow_s, wlow_r, hup_s, hup_r, hlow_s, hlow_r,
    rn_s, rn_r, hop_s, hop_r, mv_s, mv_r, red_s, red_r, ored_s, ored_r, occ_s, occ_r,
):
    me = lax.axis_index("blk")
    arm = lax.axis_index("arm")
    width = left_in.shape[-1]
    sites, outs = (site0, site1, site2), (out0, out1, out2)
    has_next, has_prev = me < count - 1, me > 0
    nxt, prv = lax.rem(me + 1, count), lax.rem(me + count - 1, count)

    def peer(d):
        return lax.rem(me + d, count)

    def arm_peer(d):
        return lax.rem(arm + d, total_arms_dev)

    barrier = pltpu.get_barrier_semaphore()

    @pl.loop(1, count)
    def _(d):
        pl.semaphore_signal(barrier, inc=1, device_id={"blk": peer(d)})

    for d in range(1, total_arms_dev):
        pl.semaphore_signal(barrier, inc=1, device_id={"arm": arm_peer(d)})

    def load(t, a):
        for s in range(2):
            for p in range(2):
                pltpu.make_async_copy(
                    sites[t].at[s, p, a, 0], z.at[t, s, p, a], z_in.at[t, a]).start()

    def wait_load(t, a):
        pltpu.make_async_copy(z.at[t, :, :, a], z.at[t, :, :, a], z_in.at[t, a]).wait()

    def left_load(a):
        return pltpu.make_async_copy(left_in.at[a, 0], leftv.at[a], left_s.at[a])

    def hop_load(a):
        return pltpu.make_async_copy(hop_in.at[a, 0], hopv.at[a], hopv_s.at[a])

    def right_load(t, a):
        return pltpu.make_async_copy(right_in.at[a, 0, t], rightv.at[t, a], rightv_s.at[t, a])

    for a in range(arms):
        load(0, a)
        left_load(a).start()
        hop_load(a).start()
        right_load(0, a).start()
    for t in (2, 1):
        for a in range(arms):
            load(t, a)
    for t in (1, 2):
        for a in range(arms):
            right_load(t, a).start()

    def zup_copy(t, a):
        return pltpu.make_async_remote_copy(
            src_ref=sites[t].at[1, :, a, 0], dst_ref=zup.at[t, a], send_sem=zup_s.at[t, a],
            recv_sem=zup_r.at[t, a], device_id={"blk": nxt})

    def zlow_copy(t, a):
        return pltpu.make_async_remote_copy(
            src_ref=sites[t].at[0, :, a, 0], dst_ref=zlow.at[t, a], send_sem=zlow_s.at[t, a],
            recv_sem=zlow_r.at[t, a], device_id={"blk": prv})

    def wup_copy(t, a):
        return pltpu.make_async_remote_copy(
            src_ref=w.at[t, 1, a], dst_ref=wup.at[t, a], send_sem=wup_s.at[t, a],
            recv_sem=wup_r.at[t, a], device_id={"blk": nxt})

    def wlow_copy(t, a):
        return pltpu.make_async_remote_copy(
            src_ref=w.at[t, 0, a], dst_ref=wlow.at[t, a], send_sem=wlow_s.at[t, a],
            recv_sem=wlow_r.at[t, a], device_id={"blk": prv})

    def hup_copy(t, a):
        return pltpu.make_async_remote_copy(
            src_ref=hsrc.at[t, 1, a], dst_ref=hup.at[t, a], send_sem=hup_s.at[t, a],
            recv_sem=hup_r.at[t, a], device_id={"blk": nxt})

    def hlow_copy(t, a):
        return pltpu.make_async_remote_copy(
            src_ref=hsrc.at[t, 0, a], dst_ref=hlow.at[t, a], send_sem=hlow_s.at[t, a],
            recv_sem=hlow_r.at[t, a], device_id={"blk": prv})

    def right_copy(t, a):
        return pltpu.make_async_remote_copy(
            src_ref=right_in.at[a, 0, t, 0], dst_ref=rnext.at[t, a], send_sem=rn_s.at[t, a],
            recv_sem=rn_r.at[t, a], device_id={"blk": prv})

    def hop_copy(a):
        return pltpu.make_async_remote_copy(
            src_ref=hop_in.at[a, 0], dst_ref=lown.at[a], send_sem=hop_s.at[a],
            recv_sem=hop_r.at[a], device_id={"blk": nxt})

    def move_copy(t, n, a):
        buf = (pmove, gmove)[n]
        return pltpu.make_async_remote_copy(
            src_ref=buf.at[t, 0, a], dst_ref=buf.at[t, 1, a], send_sem=mv_s.at[t, n, a],
            recv_sem=mv_r.at[t, n, a], device_id={"blk": nxt})

    def start_up(*copies):
        @pl.when(has_next)
        def _():
            for copy in copies:
                copy.start()

    def start_low(*copies):
        @pl.when(has_prev)
        def _():
            for copy in copies:
                copy.start()

    def wait_up(*copies):
        @pl.when(has_prev)
        def _():
            for copy in copies:
                copy.wait_recv()

    def wait_low(*copies):
        @pl.when(has_next)
        def _():
            for copy in copies:
                copy.wait_recv()

    @pl.when(jnp.logical_not(has_prev))
    def _():
        for buf in (zup, wup, hup, lown):
            buf[...] = jnp.zeros_like(buf)
        for buf in (pmove, gmove):
            buf[:, 1] = jnp.zeros_like(buf[:, 1])

    @pl.when(jnp.logical_not(has_next))
    def _():
        for buf in (zlow, wlow, hlow, rnext):
            buf[...] = jnp.zeros_like(buf)

    part[...] = jnp.zeros_like(part)
    opart[...] = jnp.zeros_like(opart)
    occ_src[...] = jnp.zeros_like(occ_src)
    pl.semaphore_wait(barrier, count - 1 + total_arms_dev - 1)

    for a in range(arms):
        start_low(right_copy(0, a), zlow_copy(0, a))
        start_up(zup_copy(0, a), hop_copy(a))

    def start_reduce(r, a):
        @pl.loop(1, count)
        def _(d):
            pltpu.make_async_remote_copy(
                src_ref=part.at[r, a], dst_ref=red.at[r, a, d - 1], send_sem=red_s.at[r, a],
                recv_sem=red_r.at[r, a], device_id={"blk": peer(d)}).start()

    def reduced(r, a):
        pltpu.make_async_copy(red.at[r, a], red.at[r, a], red_r.at[r, a]).wait()
        whole = part[r, a] + jnp.sum(red[r, a], axis=0)
        return jnp.broadcast_to(jnp.sum(whole, axis=1, keepdims=True), whole.shape)

    def end_reduce(r, a):
        pltpu.make_async_copy(red.at[r, a], red.at[r, a], red_s.at[r, a]).wait()

    rows = lax.broadcasted_iota(jnp.int32, (width, width), 0)
    cols = lax.broadcasted_iota(jnp.int32, (width, width), 1)
    eye = jnp.where(rows == cols, 1.0, 0.0).astype(F32)
    zero = jnp.zeros((width, width), F32)

    def mask_of(m_left, m_right):
        one = jnp.where((rows < m_left) & (cols < m_right), 1.0, 0.0).astype(F32)
        return jnp.concatenate([one, one], axis=0)

    def row_mask(m):
        return jnp.where(rows < m, 1.0, 0.0).astype(F32)

    def next_dim(a, t):
        return jnp.where(has_next, dims[a, t, nxt], 0)

    def tensor(t, s, a):
        return jnp.concatenate([z[t, s, 0, a], z[t, s, 1, a]], axis=0)

    def mask_source(t, a):
        wait_load(t, a)
        for s in range(2):
            one = mask_of(dims[a, t, me], dims[a, t + 1, me] if s == 0 else next_dim(a, t + 1))
            one = one[:width]
            for p in range(2):
                z[t, s, p, a] = z[t, s, p, a] * one

    def from_below(t, a):
        both = jnp.concatenate([zup[t, a, 0], zup[t, a, 1]], axis=0)
        return split(both * mask_of(dims[a, t, prv], dims[a, t + 1, me]))

    def from_above(t, a):
        both = jnp.concatenate([zlow[t, a, 0], zlow[t, a, 1]], axis=0)
        return split(both * mask_of(dims[a, t, nxt], next_dim(a, t + 1)))

    @pl.loop(0, arms)
    def _(a):
        mask_source(0, a)
        left_load(a).wait()
        live = row_mask(dims[a, 0, me])
        left = leftv[a]
        put(lop, a, complex_block(0.5 * (left + left.T) * live, zero))
        hop_load(a).wait()
        both = mask_of(dims[a, 0, me], next_dim(a, 0))[:width]
        put(hu, a, complex_block(chain[0, a, 1] * hopv[a] * both, zero))
        erow[0, pl.ds(a, 1), :] = jnp.full((1, width), chain[0, a, 0], F32)
        erow[1, pl.ds(a, 1), :] = jnp.full((1, width), chain[1, a, 0], F32)

    def build_right(t, a):
        right_load(t, a).wait()
        wait_low(right_copy(t, a))
        own, other = rightv[t, a, 0], rnext[t, a]
        couple = chain[t, a, 2] * rightv[t, a, 1]
        middle = eye * (0.5 * erow[t, pl.ds(a, 1), :])
        first = 0.5 * (own + own.T) - middle
        second = 0.5 * (other + other.T) + middle
        keep = jnp.where(cols < dims[a, t + 1, me], 1.0, 0.0).astype(F32)
        keep_next = jnp.where(cols < next_dim(a, t + 1), 1.0, 0.0).astype(F32)
        top = jnp.concatenate([first * keep, couple * keep_next], axis=1)
        bottom = jnp.concatenate([couple.T * keep, second * keep_next], axis=1)
        put(rop, a, jnp.concatenate([top, bottom], axis=0))

    def set_image(a, image):
        y[0, a] = image[:, :width]
        y[1, a] = image[:, width:]

    def right_part(t, a):
        both = split(jnp.concatenate([tensor(t, 0, a), tensor(t, 1, a)], axis=1))
        set_image(a, dot3(both, get(rop, a)))

    def local_part(one, two, a):
        both = split(jnp.concatenate([one, two], axis=1))
        set_image(a, long_dot(
            rows_of(both) + rows_of(get(lop, a)), columns_of(get(rop, a)) + columns_of(both)))

    @pl.loop(0, arms)
    def _(a):
        mask_source(2, a)
        empty, filled = tensor(2, 0, a), tensor(2, 1, a)
        square = column_sum(filled * filled)
        opart[pl.ds(a, 1), :] = square
        opart[pl.ds(arms + a, 1), :] = square + column_sum(empty * empty)

    @pl.loop(1, count)
    def _(d):
        pltpu.make_async_remote_copy(
            src_ref=opart, dst_ref=ored.at[d - 1], send_sem=ored_s,
            recv_sem=ored_r, device_id={"blk": peer(d)}).start()

    @pl.loop(0, arms)
    def _(a):
        mask_source(1, a)

    def add_row(r, a, n, row):
        part[r, a, n:n + 1, :] = row

    for t in range(TENSORS):
        @pl.loop(0, arms)
        def _(a):
            if t == 0:
                build_right(0, a)
                local_part(tensor(0, 0, a), tensor(0, 1, a), a)
                wait_up(hop_copy(a))
                put(hd, a, complex_block(
                    chain[0, a, 1] * lown[a].T * mask_of(dims[a, 0, me], dims[a, 0, prv])[:width],
                    zero))
            wait_low(zlow_copy(t, a))
            wait_up(zup_copy(t, a))
            filled = y[1, a] + dot3(get(hu, a), from_above(t, a))
            empty = y[0, a]
            below = from_below(t, a)
            if t > 0:
                wait_up(move_copy(t - 1, 1, a))
                rate = chain[t, a, 1]
                put(hd, a, complex_block(
                    rate * gmove[t - 1, 1, a, 0], rate * gmove[t - 1, 1, a, 1]))
            empty = empty + dot3(get(hd, a), below)
            base = [tensor(t, s, a) for s in range(2)]
            if t > 0:
                wait_up(move_copy(t - 1, 0, a))
                packed = pmove[t - 1, 1, a]
                mirror = packed.T
                real = jnp.where(rows <= cols, packed, mirror)
                imag = jnp.where(rows > cols, packed, jnp.where(rows < cols, -mirror, 0.0))
                own = kept[a]
                put(lop, a, complex_block(own[:width] + real, own[width:] + imag))
                product = dot3(get(lop, a), split(jnp.concatenate(base, axis=1)))
                empty = empty + product[:, :width]
                filled = filled + product[:, width:]
            image = (empty, filled)
            for s in range(2):
                w[t, s, a] = image[s]
            start_up(wup_copy(t, a))
            start_low(wlow_copy(t, a))
            sums = [0.0, 0.0, 0.0]
            for s in range(2):
                pairs = ((base[s], base[s]), (base[s], image[s]), (image[s], image[s]))
                for n, pair in enumerate(pairs):
                    sums[n] = sums[n] + column_sum(pair[0] * pair[1])
            for n in range(3):
                add_row(t, a, n, sums[n])
            local_part(image[0], image[1], a)
            hsrc[t, 1, a] = packed_half(y[1, a], width, False)
            hsrc[t, 0, a] = packed_half(y[0, a], width, True)
            start_up(hup_copy(t, a))
            start_low(hlow_copy(t, a))
            for s, operator in enumerate((hd, hu)):
                own = packed_half(image[s], width, s == 1)
                own = jnp.concatenate([own, turned(own, width)], axis=0).astype(BF16)
                back[s, a] = lax.dot_general(
                    operator[0, a][:, :width], own, (((0,), (0,)), ((), ())),
                    preferred_element_type=F32)

        if t + 1 < TENSORS:
            for a in range(arms):
                start_low(right_copy(t + 1, a))

        @pl.loop(0, arms)
        def _(a):
            wait_low(wlow_copy(t, a))
            wait_up(wup_copy(t, a))
            filled = y[1, a] + dot3(get(hu, a), split(wlow[t, a]))
            empty = y[0, a] + dot3(get(hd, a), split(wup[t, a]))
            fresh = (empty, filled)
            for s in range(2):
                h[s, a] = fresh[s]
            both = jnp.concatenate(fresh, axis=1).astype(BF16)
            image = long_dot(
                [both, both, lop[0, a]], [rop[0, a], rop[1, a], both])
            wait_low(hlow_copy(t, a))
            wait_up(hup_copy(t, a))

            def crossing(arrived, mine, operator, late):
                image = jnp.dot(
                    operator[0, a][:, :width], arrived.astype(BF16), preferred_element_type=F32)
                own = packed_half(mine, width, late)
                return 2.0 * column_sum(
                    own * image[:width] + turned(own, width) * image[width:])

            sums = [0.0, 0.0, crossing(hup[t, a] + back[0, a], empty, hd, False)]
            sums[2] = sums[2] + crossing(hlow[t, a] + back[1, a], filled, hu, True)
            for s in range(2):
                pairs = (
                    (w[t, s, a], fresh[s]), (fresh[s], fresh[s]),
                    (fresh[s], image[:, s * width:(s + 1) * width]))
                for n, pair in enumerate(pairs):
                    sums[n] = sums[n] + column_sum(pair[0] * pair[1])
            for n in range(3):
                add_row(t, a, 3 + n, sums[n])
            start_reduce(t, a)
            if t + 1 < TENSORS:
                start_up(zup_copy(t + 1, a))
                start_low(zlow_copy(t + 1, a))

        if t == 0:
            pltpu.make_async_copy(ored, ored, ored_r).wait()
            whole = opart[...] + jnp.sum(ored[...], axis=0)
            opart_tot = jnp.broadcast_to(jnp.sum(whole, axis=1, keepdims=True), whole.shape)
            occ_src[0:arms, :] = opart_tot[0:arms] / (opart_tot[arms:2 * arms] + EPSILON)
            for d in range(1, total_arms_dev):
                pltpu.make_async_remote_copy(
                    src_ref=occ_src, dst_ref=occ_all.at[d - 1], send_sem=occ_s.at[d - 1],
                    recv_sem=occ_r.at[d - 1], device_id={"arm": arm_peer(d)}).start()
        if t == 1:
            for d in range(1, total_arms_dev):
                pltpu.make_async_remote_copy(
                    src_ref=occ_src, dst_ref=occ_all.at[d - 1], send_sem=occ_s.at[d - 1],
                    recv_sem=occ_r.at[d - 1], device_id={"arm": arm_peer(d)}).wait()

            @pl.loop(0, arms)
            def _(a):
                energy = jnp.full((1, width), chain[2, a, 0], F32)
                for d in range(total_arms_dev):
                    owner = lax.rem(arm + total_arms_dev - d, total_arms_dev)
                    for j in range(arms):
                        values = occ_src[j:j + 1, :] if d == 0 else occ_all[d - 1, j:j + 1, :]
                        energy = energy + inter[a, owner * arms + j] * values
                erow[2, pl.ds(a, 1), :] = energy

        if t + 1 < TENSORS:
            @pl.loop(0, arms)
            def _(a):
                build_right(t + 1, a)
                right_part(t + 1, a)

        @pl.loop(0, arms)
        def _(a):
            tot = reduced(t, a)
            norm_square = tot[0:1] + EPSILON
            inverse = 1.0 / norm_square
            mean, second, third, fourth, fifth = (tot[n:n + 1] * inverse for n in range(1, 6))
            alpha0 = mean
            beta1_square = jnp.maximum(second - alpha0 * alpha0, 0.0) + EPSILON
            beta1 = jnp.sqrt(beta1_square)
            scale = 1.0 / beta1_square

            def moved_on(low, middle, high):
                return (high - alpha0 * (2.0 * middle - alpha0 * low)) * scale

            alpha1 = moved_on(mean, second, third)
            square1 = moved_on(second, third, fourth)
            cross_link = (third - alpha0 * second - alpha1 * (second - alpha0 * mean)) * 2.0
            beta2_square = jnp.maximum(square1 - alpha1 * alpha1 - beta1_square, 0.0) + EPSILON
            beta2 = jnp.sqrt(beta2_square)
            alpha2 = (
                moved_on(third, fourth, fifth) - alpha1 * (2.0 * square1 - alpha1 * alpha1)
                - cross_link + beta1_square * alpha0
            ) / beta2_square
            real, imag = exponential(
                [alpha + 0.5 * erow[t, pl.ds(a, 1), :] for alpha in (alpha0, alpha1, alpha2)],
                [beta1, beta2])

            def weights(e):
                middle, last = e[1] / beta1, e[2] / (beta1 * beta2)
                return (
                    e[0] - alpha0 * middle + (alpha0 * alpha1 - beta1_square) * last,
                    middle - (alpha0 + alpha1) * last, last)

            cosines, sines = weights(real), weights(imag)
            evolved = []
            squares = 0.0
            for s in range(2):
                re = im = 0.0
                for k, part_of in enumerate((tensor(t, s, a), w[t, s, a], h[s, a])):
                    cosine, sine = cosines[k], sines[k]
                    top, bottom = part_of[:width], part_of[width:]
                    re = re + cosine * top - sine * bottom
                    im = im + cosine * bottom + sine * top
                outs[t][s, 0, a, 0] = re
                outs[t][s, 1, a, 0] = im
                evolved.append((re, im))
                squares = squares + column_sum(re * re + im * im)
            if t + 1 < TENSORS:
                square = jnp.sum(squares, axis=1, keepdims=True)
                factor = SECTOR_BOUND / jnp.sqrt(
                    jnp.broadcast_to(square, (1, width)) + norm_square * (1.0 / count))
                x = [(re * factor, im * factor) for re, im in evolved]
                flip = [split(jnp.concatenate([re.T, im.T], axis=1)) for re, im in x]

                def wide(re, im):
                    return split(jnp.concatenate(
                        [jnp.concatenate([re, im], axis=1), jnp.concatenate([im, -re], axis=1)],
                        axis=0))

                linked = dot3(flip[1], wide(*x[0]))
                gmove[t, 0, a, 0] = linked[:, :width]
                gmove[t, 0, a, 1] = linked[:, width:]
                start_up(move_copy(t, 1, a))
                whole = split(jnp.concatenate(
                    [jnp.concatenate(pair, axis=0) for pair in x], axis=1))
                image = dot3(get(lop, a), whole)
                energy = erow[t, pl.ds(a, 1), :]
                lifted = dot3(flip[1], wide(
                    image[:width, width:] + energy * x[1][0],
                    image[width:, width:] + energy * x[1][1]))
                pmove[t, 0, a] = jnp.where(rows <= cols, lifted[:, :width], lifted[:, width:])
                start_up(move_copy(t, 0, a))
                own = dot3(flip[0], wide(image[:width, :width], image[width:, :width]))
                rate = chain[t + 1, a, 1]
                put(hu, a, complex_block(
                    rate * linked[:, :width].T, -rate * linked[:, width:].T))
                kept[a] = jnp.concatenate([own[:, :width], own[:, width:]], axis=0)

    @pl.when(has_next)
    def _():
        for a in range(arms):
            hop_copy(a).wait_send()
            for t in range(TENSORS):
                zup_copy(t, a).wait_send()
                wup_copy(t, a).wait_send()
                hup_copy(t, a).wait_send()
            for t in range(TENSORS - 1):
                for n in range(2):
                    move_copy(t, n, a).wait_send()

    @pl.when(has_prev)
    def _():
        for a in range(arms):
            for t in range(TENSORS):
                right_copy(t, a).wait_send()
                zlow_copy(t, a).wait_send()
                wlow_copy(t, a).wait_send()
                hlow_copy(t, a).wait_send()

    pltpu.make_async_copy(ored, ored, ored_s).wait()
    for a in range(arms):
        for t in range(TENSORS):
            end_reduce(t, a)


def hand_kernel(a, b, c, x, y, z, sem):
    copies = [
        pltpu.make_async_copy(i.at[s, p], o.at[s, p], sem.at[4 * k + 2 * s + p])
        for k, (i, o) in enumerate(((a, x), (b, y), (c, z))) for s in range(2) for p in range(2)]
    for copy in copies:
        copy.start()
    for copy in copies:
        copy.wait()


def hand(outs):
    anywhere = pl.BlockSpec(memory_space=pl.ANY)
    return pl.pallas_call(
        hand_kernel, out_shape=tuple(jax.ShapeDtypeStruct(o.shape, o.dtype) for o in outs),
        in_specs=[pl.BlockSpec(memory_space=pltpu.VMEM)] * 3, out_specs=(anywhere,) * 3,
        scratch_shapes=[pltpu.SemaphoreType.DMA((12,))],
    )(*(pltpu.with_memory_space_constraint(o, pltpu.VMEM) for o in outs))


def on_device(count, arm_devices, *args):
    site = args[0]
    args = args[:6] + (jnp.transpose(args[6], (1, 0, 2)),) + args[7:]
    arms, width = site.shape[2], site.shape[-1]
    occ_rows = -(-2 * arms // 8) * 8
    arm_rows = -(-arms // 8) * 8
    vmem, sems = pltpu.VMEM, pltpu.SemaphoreType.DMA
    state = vmem((2, arms, 2 * width, width), F32)
    source = vmem((TENSORS, arms, 2, width, width), F32)
    halo = vmem((TENSORS, arms, 2 * width, width), F32)
    square = vmem((TENSORS, arms, width, width), F32)
    operator = vmem((2, arms, 2 * width, 2 * width), BF16)
    block = vmem((arms, width, width), F32)
    whole = pl.BlockSpec(memory_space=pltpu.VMEM)
    distant = pl.BlockSpec(memory_space=pltpu.HBM)
    scalar = pl.BlockSpec(memory_space=pltpu.SMEM)
    out = pltpu.VMEM(site.shape, F32)
    each, single = sems((TENSORS, arms)), sems((arms,))
    moves, sums = sems((TENSORS - 1, 2, arms)), each
    arm_sems = sems((max(arm_devices - 1, 1),))
    outs = pl.pallas_call(
        functools.partial(kernel, count, arms, arm_devices),
        out_shape=(out, out, out),
        in_specs=[distant] * 6 + [scalar] * 3,
        out_specs=(whole,) * 3,
        scratch_shapes=[
            vmem((TENSORS, 2, 2, arms, width, width), F32),
            vmem((TENSORS, 2, arms, 2 * width, width), F32),
            state, state, vmem((arms, 2 * width, width), F32), vmem((2, arms, width, width), F32),
            source, source, halo, halo,
            vmem((TENSORS, 2, arms, width, width), F32), square, square, square,
            vmem((TENSORS - 1, 2, arms, width, width), F32),
            vmem((TENSORS - 1, 2, arms, 2, width, width), F32),
            block, block, vmem((TENSORS, arms, 2, width, width), F32),
            operator, operator, operator, operator, block,
            vmem((TENSORS, arms, 8, width), F32),
            vmem((TENSORS, arms, count - 1, 8, width), F32),
            vmem((occ_rows, width), F32),
            vmem((count - 1, occ_rows, width), F32),
            vmem((arm_rows, width), F32),
            vmem((max(arm_devices - 1, 1), arm_rows, width), F32),
            vmem((TENSORS, arm_rows, width), F32),
            each, single, single, each,
            each, each, each, each, each, each, each, each, each, each, each, each,
            each, each, single, single, moves, moves, sums, sums,
            pltpu.SemaphoreType.DMA, pltpu.SemaphoreType.DMA, arm_sems, arm_sems,
        ],
        compiler_params=pltpu.CompilerParams(
            collective_id=0, has_side_effects=True, vmem_limit_bytes=56 * 1024 * 1024
        ),
    )(*args)
    return hand(outs)


def solution(mesh):
    tensor = P(None, None, "arm", "blk", None, None)
    in_specs = (
        tensor, tensor, tensor,
        P("arm", "blk", None, None),
        P("arm", "blk", None, None),
        P("arm", "blk", None, None, None, None),
        P("arm", None, None),
        P("arm", None),
        P("arm", None, None),
    )
    body = functools.partial(on_device, mesh.shape["blk"], mesh.shape["arm"])
    return jax.shard_map(
        body, mesh=mesh, in_specs=in_specs, out_specs=(tensor, tensor, tensor), check_vma=False
    )
```

```python
import functools

import jax
import jax.numpy as jnp
from jax import lax
from jax.experimental import pallas as pl
from jax.experimental.pallas import tpu as pltpu
from jax.sharding import PartitionSpec as P

KRYLOV = 3
TENSORS = 3
TIME_STEP = 0.4
EPSILON = 1e-06
TAYLOR = 12
HALVINGS = 5
SECTOR_BOUND = 3.0
F32 = jnp.float32
BF16 = jnp.bfloat16


def split(x):
    high = x.astype(BF16)
    return high, (x - high.astype(F32)).astype(BF16)


def rows_of(a):
    return [a[0], a[0], a[1]]


def columns_of(b):
    return [b[0], b[1], b[0]]


def long_dot(left, right):
    return jnp.dot(
        jnp.concatenate(left, axis=1), jnp.concatenate(right, axis=0), preferred_element_type=F32)


def dot3(a, b):
    return long_dot(rows_of(a), columns_of(b))


def put(ref, a, x):
    high, low = split(x)
    ref[0, a] = high
    ref[1, a] = low


def get(ref, a):
    return ref[0, a], ref[1, a]


def complex_block(real, imag):
    return jnp.concatenate(
        [jnp.concatenate([real, -imag], axis=1), jnp.concatenate([imag, real], axis=1)], axis=0
    )


def packed_half(x, width, late):
    half = width // 2
    real, imag = x[:width], x[width:]
    first = lax.broadcasted_iota(jnp.int32, (width, width), 1) < half
    if late:
        return jnp.where(first, pltpu.roll(real, half, 1), imag)
    return jnp.where(first, real, pltpu.roll(imag, half, 1))


def turned(x, width):
    half = width // 2
    first = lax.broadcasted_iota(jnp.int32, (width, width), 1) < half
    other = pltpu.roll(x, half, 1)
    return jnp.where(first, other, -other)


def column_sum(x):
    return jnp.sum(x, axis=0, keepdims=True)


def exponential(alphas, betas):
    step = TIME_STEP / 2.0**HALVINGS
    zero = jnp.zeros_like(alphas[0])
    one = jnp.ones_like(zero)
    s = {(0, 0): alphas[0], (1, 1): alphas[1], (2, 2): alphas[2], (0, 1): betas[0], (1, 2): betas[1]}
    s = {key: step * value for key, value in s.items()}
    keys = [(0, 0), (0, 1), (0, 2), (1, 1), (1, 2), (2, 2)]

    def at(m, i, j):
        return m[(min(i, j), max(i, j))]

    def times_s(m):
        out = {}
        for i, j in keys:
            terms = [at(m, i, k) * at(s, k, j) for k in range(3) if abs(k - j) < 2]
            out[(i, j)] = functools.reduce(jnp.add, terms)
        return out

    power = {key: one if key[0] == key[1] else zero for key in keys}
    real = dict(power)
    imag = {key: zero for key in keys}
    for order in range(1, TAYLOR + 1):
        power = {key: value * (1.0 / order) for key, value in times_s(power).items()}
        phase = order % 4
        target = imag if phase % 2 else real
        for key in keys:
            target[key] = target[key] - power[key] if phase in (1, 2) else target[key] + power[key]
    for _ in range(HALVINGS):
        new_real, new_imag = {}, {}
        for i, j in keys:
            re = im = None
            for k in range(3):
                a, b, c, d = at(real, i, k), at(imag, i, k), at(real, k, j), at(imag, k, j)
                x, y = a * c - b * d, a * d + b * c
                re, im = (x, y) if re is None else (re + x, im + y)
            new_real[(i, j)], new_imag[(i, j)] = re, im
        real, imag = new_real, new_imag
    return [at(real, k, 0) for k in range(3)], [at(imag, k, 0) for k in range(3)]


def kernel(
    count, arms, total_arms_dev,
    site0, site1, site2, left_in, hop_in, right_in, chain, inter, dims,
    out0, out1, out2,
    z, w, y, h, kept, back, zup, zlow, wup, wlow, hsrc, hup, hlow, rnext, pmove, gmove,
    leftv, hopv, rightv, lop, rop, hu, hd, lown, part, red, opart, ored,
    occ_src, occ_all, erow,
    z_in, left_s, hopv_s, rightv_s,
    zup_s, zup_r, zlow_s, zlow_r, wup_s, wup_r, wlow_s, wlow_r, hup_s, hup_r, hlow_s, hlow_r,
    rn_s, rn_r, hop_s, hop_r, mv_s, mv_r, red_s, red_r, ored_s, ored_r, occ_s, occ_r,
):
    me = lax.axis_index("blk")
    arm = lax.axis_index("arm")
    width = left_in.shape[-1]
    sites, outs = (site0, site1, site2), (out0, out1, out2)
    has_next, has_prev = me < count - 1, me > 0
    nxt, prv = lax.rem(me + 1, count), lax.rem(me + count - 1, count)

    def peer(d):
        return lax.rem(me + d, count)

    def arm_peer(d):
        return lax.rem(arm + d, total_arms_dev)

    barrier = pltpu.get_barrier_semaphore()

    @pl.loop(1, count)
    def _(d):
        pl.semaphore_signal(barrier, inc=1, device_id={"blk": peer(d)})

    for d in range(1, total_arms_dev):
        pl.semaphore_signal(barrier, inc=1, device_id={"arm": arm_peer(d)})

    def load(t, a):
        for s in range(2):
            for p in range(2):
                pltpu.make_async_copy(
                    sites[t].at[s, p, a, 0], z.at[t, s, p, a], z_in.at[t, a]).start()

    def wait_load(t, a):
        pltpu.make_async_copy(z.at[t, :, :, a], z.at[t, :, :, a], z_in.at[t, a]).wait()

    def left_load(a):
        return pltpu.make_async_copy(left_in.at[a, 0], leftv.at[a], left_s.at[a])

    def hop_load(a):
        return pltpu.make_async_copy(hop_in.at[a, 0], hopv.at[a], hopv_s.at[a])

    def right_load(t, a):
        return pltpu.make_async_copy(right_in.at[a, 0, t], rightv.at[t, a], rightv_s.at[t, a])

    for a in range(arms):
        load(0, a)
        left_load(a).start()
        hop_load(a).start()
        right_load(0, a).start()
    for t in (2, 1):
        for a in range(arms):
            load(t, a)
    for t in (1, 2):
        for a in range(arms):
            right_load(t, a).start()

    def zup_copy(t, a):
        return pltpu.make_async_remote_copy(
            src_ref=sites[t].at[1, :, a, 0], dst_ref=zup.at[t, a], send_sem=zup_s.at[t, a],
            recv_sem=zup_r.at[t, a], device_id={"blk": nxt})

    def zlow_copy(t, a):
        return pltpu.make_async_remote_copy(
            src_ref=sites[t].at[0, :, a, 0], dst_ref=zlow.at[t, a], send_sem=zlow_s.at[t, a],
            recv_sem=zlow_r.at[t, a], device_id={"blk": prv})

    def wup_copy(t, a):
        return pltpu.make_async_remote_copy(
            src_ref=w.at[t, 1, a], dst_ref=wup.at[t, a], send_sem=wup_s.at[t, a],
            recv_sem=wup_r.at[t, a], device_id={"blk": nxt})

    def wlow_copy(t, a):
        return pltpu.make_async_remote_copy(
            src_ref=w.at[t, 0, a], dst_ref=wlow.at[t, a], send_sem=wlow_s.at[t, a],
            recv_sem=wlow_r.at[t, a], device_id={"blk": prv})

    def hup_copy(t, a):
        return pltpu.make_async_remote_copy(
            src_ref=hsrc.at[t, 1, a], dst_ref=hup.at[t, a], send_sem=hup_s.at[t, a],
            recv_sem=hup_r.at[t, a], device_id={"blk": nxt})

    def hlow_copy(t, a):
        return pltpu.make_async_remote_copy(
            src_ref=hsrc.at[t, 0, a], dst_ref=hlow.at[t, a], send_sem=hlow_s.at[t, a],
            recv_sem=hlow_r.at[t, a], device_id={"blk": prv})

    def right_copy(t, a):
        return pltpu.make_async_remote_copy(
            src_ref=right_in.at[a, 0, t, 0], dst_ref=rnext.at[t, a], send_sem=rn_s.at[t, a],
            recv_sem=rn_r.at[t, a], device_id={"blk": prv})

    def hop_copy(a):
        return pltpu.make_async_remote_copy(
            src_ref=hop_in.at[a, 0], dst_ref=lown.at[a], send_sem=hop_s.at[a],
            recv_sem=hop_r.at[a], device_id={"blk": nxt})

    def move_copy(t, n, a):
        buf = (pmove, gmove)[n]
        return pltpu.make_async_remote_copy(
            src_ref=buf.at[t, 0, a], dst_ref=buf.at[t, 1, a], send_sem=mv_s.at[t, n, a],
            recv_sem=mv_r.at[t, n, a], device_id={"blk": nxt})

    def start_up(*copies):
        @pl.when(has_next)
        def _():
            for copy in copies:
                copy.start()

    def start_low(*copies):
        @pl.when(has_prev)
        def _():
            for copy in copies:
                copy.start()

    def wait_up(*copies):
        @pl.when(has_prev)
        def _():
            for copy in copies:
                copy.wait_recv()

    def wait_low(*copies):
        @pl.when(has_next)
        def _():
            for copy in copies:
                copy.wait_recv()

    @pl.when(jnp.logical_not(has_prev))
    def _():
        for buf in (zup, wup, hup, lown):
            buf[...] = jnp.zeros_like(buf)
        for buf in (pmove, gmove):
            buf[:, 1] = jnp.zeros_like(buf[:, 1])

    @pl.when(jnp.logical_not(has_next))
    def _():
        for buf in (zlow, wlow, hlow, rnext):
            buf[...] = jnp.zeros_like(buf)

    part[...] = jnp.zeros_like(part)
    opart[...] = jnp.zeros_like(opart)
    occ_src[...] = jnp.zeros_like(occ_src)
    pl.semaphore_wait(barrier, count - 1 + total_arms_dev - 1)

    for a in range(arms):
        start_low(right_copy(0, a), zlow_copy(0, a))
        start_up(zup_copy(0, a), hop_copy(a))

    def start_reduce(r, a):
        @pl.loop(1, count)
        def _(d):
            pltpu.make_async_remote_copy(
                src_ref=part.at[r, a], dst_ref=red.at[r, a, d - 1], send_sem=red_s.at[r, a],
                recv_sem=red_r.at[r, a], device_id={"blk": peer(d)}).start()

    def reduced(r, a):
        pltpu.make_async_copy(red.at[r, a], red.at[r, a], red_r.at[r, a]).wait()
        whole = part[r, a] + jnp.sum(red[r, a], axis=0)
        return jnp.broadcast_to(jnp.sum(whole, axis=1, keepdims=True), whole.shape)

    def end_reduce(r, a):
        pltpu.make_async_copy(red.at[r, a], red.at[r, a], red_s.at[r, a]).wait()

    rows = lax.broadcasted_iota(jnp.int32, (width, width), 0)
    cols = lax.broadcasted_iota(jnp.int32, (width, width), 1)
    eye = jnp.where(rows == cols, 1.0, 0.0).astype(F32)
    zero = jnp.zeros((width, width), F32)

    def mask_of(m_left, m_right):
        one = jnp.where((rows < m_left) & (cols < m_right), 1.0, 0.0).astype(F32)
        return jnp.concatenate([one, one], axis=0)

    def row_mask(m):
        return jnp.where(rows < m, 1.0, 0.0).astype(F32)

    def next_dim(a, t):
        return jnp.where(has_next, dims[a, t, nxt], 0)

    def tensor(t, s, a):
        return jnp.concatenate([z[t, s, 0, a], z[t, s, 1, a]], axis=0)

    def mask_source(t, a):
        wait_load(t, a)
        for s in range(2):
            one = mask_of(dims[a, t, me], dims[a, t + 1, me] if s == 0 else next_dim(a, t + 1))
            one = one[:width]
            for p in range(2):
                z[t, s, p, a] = z[t, s, p, a] * one

    def from_below(t, a):
        both = jnp.concatenate([zup[t, a, 0], zup[t, a, 1]], axis=0)
        return split(both * mask_of(dims[a, t, prv], dims[a, t + 1, me]))

    def from_above(t, a):
        both = jnp.concatenate([zlow[t, a, 0], zlow[t, a, 1]], axis=0)
        return split(both * mask_of(dims[a, t, nxt], next_dim(a, t + 1)))

    @pl.loop(0, arms)
    def _(a):
        mask_source(0, a)
        left_load(a).wait()
        live = row_mask(dims[a, 0, me])
        left = leftv[a]
        put(lop, a, complex_block(0.5 * (left + left.T) * live, zero))
        hop_load(a).wait()
        both = mask_of(dims[a, 0, me], next_dim(a, 0))[:width]
        put(hu, a, complex_block(chain[0, a, 1] * hopv[a] * both, zero))
        erow[0, pl.ds(a, 1), :] = jnp.full((1, width), chain[0, a, 0], F32)
        erow[1, pl.ds(a, 1), :] = jnp.full((1, width), chain[1, a, 0], F32)

    def build_right(t, a):
        right_load(t, a).wait()
        wait_low(right_copy(t, a))
        own, other = rightv[t, a, 0], rnext[t, a]
        couple = chain[t, a, 2] * rightv[t, a, 1]
        middle = eye * (0.5 * erow[t, pl.ds(a, 1), :])
        first = 0.5 * (own + own.T) - middle
        second = 0.5 * (other + other.T) + middle
        keep = jnp.where(cols < dims[a, t + 1, me], 1.0, 0.0).astype(F32)
        keep_next = jnp.where(cols < next_dim(a, t + 1), 1.0, 0.0).astype(F32)
        top = jnp.concatenate([first * keep, couple * keep_next], axis=1)
        bottom = jnp.concatenate([couple.T * keep, second * keep_next], axis=1)
        put(rop, a, jnp.concatenate([top, bottom], axis=0))

    def set_image(a, image):
        y[0, a] = image[:, :width]
        y[1, a] = image[:, width:]

    def right_part(t, a):
        both = split(jnp.concatenate([tensor(t, 0, a), tensor(t, 1, a)], axis=1))
        set_image(a, dot3(both, get(rop, a)))

    def local_part(one, two, a):
        both = split(jnp.concatenate([one, two], axis=1))
        set_image(a, long_dot(
            rows_of(both) + rows_of(get(lop, a)), columns_of(get(rop, a)) + columns_of(both)))

    @pl.loop(0, arms)
    def _(a):
        mask_source(2, a)
        empty, filled = tensor(2, 0, a), tensor(2, 1, a)
        square = column_sum(filled * filled)
        opart[pl.ds(a, 1), :] = square
        opart[pl.ds(arms + a, 1), :] = square + column_sum(empty * empty)

    @pl.loop(1, count)
    def _(d):
        pltpu.make_async_remote_copy(
            src_ref=opart, dst_ref=ored.at[d - 1], send_sem=ored_s,
            recv_sem=ored_r, device_id={"blk": peer(d)}).start()

    @pl.loop(0, arms)
    def _(a):
        mask_source(1, a)

    def add_row(r, a, n, row):
        part[r, a, n:n + 1, :] = row

    for t in range(TENSORS):
        @pl.loop(0, arms)
        def _(a):
            if t == 0:
                build_right(0, a)
                local_part(tensor(0, 0, a), tensor(0, 1, a), a)
                wait_up(hop_copy(a))
                put(hd, a, complex_block(
                    chain[0, a, 1] * lown[a].T * mask_of(dims[a, 0, me], dims[a, 0, prv])[:width],
                    zero))
            wait_low(zlow_copy(t, a))
            wait_up(zup_copy(t, a))
            filled = y[1, a] + dot3(get(hu, a), from_above(t, a))
            empty = y[0, a]
            below = from_below(t, a)
            if t > 0:
                wait_up(move_copy(t - 1, 1, a))
                rate = chain[t, a, 1]
                put(hd, a, complex_block(
                    rate * gmove[t - 1, 1, a, 0], rate * gmove[t - 1, 1, a, 1]))
            empty = empty + dot3(get(hd, a), below)
            base = [tensor(t, s, a) for s in range(2)]
            if t > 0:
                wait_up(move_copy(t - 1, 0, a))
                packed = pmove[t - 1, 1, a]
                mirror = packed.T
                real = jnp.where(rows <= cols, packed, mirror)
                imag = jnp.where(rows > cols, packed, jnp.where(rows < cols, -mirror, 0.0))
                own = kept[a]
                put(lop, a, complex_block(own[:width] + real, own[width:] + imag))
                product = dot3(get(lop, a), split(jnp.concatenate(base, axis=1)))
                empty = empty + product[:, :width]
                filled = filled + product[:, width:]
            image = (empty, filled)
            for s in range(2):
                w[t, s, a] = image[s]
            start_up(wup_copy(t, a))
            start_low(wlow_copy(t, a))
            sums = [0.0, 0.0, 0.0]
            for s in range(2):
                pairs = ((base[s], base[s]), (base[s], image[s]), (image[s], image[s]))
                for n, pair in enumerate(pairs):
                    sums[n] = sums[n] + column_sum(pair[0] * pair[1])
            for n in range(3):
                add_row(t, a, n, sums[n])
            local_part(image[0], image[1], a)
            hsrc[t, 1, a] = packed_half(y[1, a], width, False)
            hsrc[t, 0, a] = packed_half(y[0, a], width, True)
            start_up(hup_copy(t, a))
            start_low(hlow_copy(t, a))
            for s, operator in enumerate((hd, hu)):
                own = packed_half(image[s], width, s == 1)
                own = jnp.concatenate([own, turned(own, width)], axis=0).astype(BF16)
                back[s, a] = lax.dot_general(
                    operator[0, a][:, :width], own, (((0,), (0,)), ((), ())),
                    preferred_element_type=F32)

        if t + 1 < TENSORS:
            for a in range(arms):
                start_low(right_copy(t + 1, a))

        @pl.loop(0, arms)
        def _(a):
            wait_low(wlow_copy(t, a))
            wait_up(wup_copy(t, a))
            filled = y[1, a] + dot3(get(hu, a), split(wlow[t, a]))
            empty = y[0, a] + dot3(get(hd, a), split(wup[t, a]))
            fresh = (empty, filled)
            for s in range(2):
                h[s, a] = fresh[s]
            both = jnp.concatenate(fresh, axis=1).astype(BF16)
            image = long_dot(
                [both, both, lop[0, a]], [rop[0, a], rop[1, a], both])
            wait_low(hlow_copy(t, a))
            wait_up(hup_copy(t, a))

            def crossing(arrived, mine, operator, late):
                image = jnp.dot(
                    operator[0, a][:, :width], arrived.astype(BF16), preferred_element_type=F32)
                own = packed_half(mine, width, late)
                return 2.0 * column_sum(
                    own * image[:width] + turned(own, width) * image[width:])

            sums = [0.0, 0.0, crossing(hup[t, a] + back[0, a], empty, hd, False)]
            sums[2] = sums[2] + crossing(hlow[t, a] + back[1, a], filled, hu, True)
            for s in range(2):
                pairs = (
                    (w[t, s, a], fresh[s]), (fresh[s], fresh[s]),
                    (fresh[s], image[:, s * width:(s + 1) * width]))
                for n, pair in enumerate(pairs):
                    sums[n] = sums[n] + column_sum(pair[0] * pair[1])
            for n in range(3):
                add_row(t, a, 3 + n, sums[n])
            start_reduce(t, a)
            if t + 1 < TENSORS:
                start_up(zup_copy(t + 1, a))
                start_low(zlow_copy(t + 1, a))

        if t == 0:
            pltpu.make_async_copy(ored, ored, ored_r).wait()
            whole = opart[...] + jnp.sum(ored[...], axis=0)
            opart_tot = jnp.broadcast_to(jnp.sum(whole, axis=1, keepdims=True), whole.shape)
            occ_src[0:arms, :] = opart_tot[0:arms] / (opart_tot[arms:2 * arms] + EPSILON)
            for d in range(1, total_arms_dev):
                pltpu.make_async_remote_copy(
                    src_ref=occ_src, dst_ref=occ_all.at[d - 1], send_sem=occ_s.at[d - 1],
                    recv_sem=occ_r.at[d - 1], device_id={"arm": arm_peer(d)}).start()
        if t == 1:
            for d in range(1, total_arms_dev):
                pltpu.make_async_remote_copy(
                    src_ref=occ_src, dst_ref=occ_all.at[d - 1], send_sem=occ_s.at[d - 1],
                    recv_sem=occ_r.at[d - 1], device_id={"arm": arm_peer(d)}).wait()

            @pl.loop(0, arms)
            def _(a):
                energy = jnp.full((1, width), chain[2, a, 0], F32)
                for d in range(total_arms_dev):
                    owner = lax.rem(arm + total_arms_dev - d, total_arms_dev)
                    for j in range(arms):
                        values = occ_src[j:j + 1, :] if d == 0 else occ_all[d - 1, j:j + 1, :]
                        energy = energy + inter[a, owner * arms + j] * values
                erow[2, pl.ds(a, 1), :] = energy

        if t + 1 < TENSORS:
            @pl.loop(0, arms)
            def _(a):
                build_right(t + 1, a)
                right_part(t + 1, a)

        @pl.loop(0, arms)
        def _(a):
            tot = reduced(t, a)
            norm_square = tot[0:1] + EPSILON
            inverse = 1.0 / norm_square
            mean, second, third, fourth, fifth = (tot[n:n + 1] * inverse for n in range(1, 6))
            alpha0 = mean
            beta1_square = jnp.maximum(second - alpha0 * alpha0, 0.0) + EPSILON
            beta1 = jnp.sqrt(beta1_square)
            scale = 1.0 / beta1_square

            def moved_on(low, middle, high):
                return (high - alpha0 * (2.0 * middle - alpha0 * low)) * scale

            alpha1 = moved_on(mean, second, third)
            square1 = moved_on(second, third, fourth)
            cross_link = (third - alpha0 * second - alpha1 * (second - alpha0 * mean)) * 2.0
            beta2_square = jnp.maximum(square1 - alpha1 * alpha1 - beta1_square, 0.0) + EPSILON
            beta2 = jnp.sqrt(beta2_square)
            alpha2 = (
                moved_on(third, fourth, fifth) - alpha1 * (2.0 * square1 - alpha1 * alpha1)
                - cross_link + beta1_square * alpha0
            ) / beta2_square
            real, imag = exponential(
                [alpha + 0.5 * erow[t, pl.ds(a, 1), :] for alpha in (alpha0, alpha1, alpha2)],
                [beta1, beta2])

            def weights(e):
                middle, last = e[1] / beta1, e[2] / (beta1 * beta2)
                return (
                    e[0] - alpha0 * middle + (alpha0 * alpha1 - beta1_square) * last,
                    middle - (alpha0 + alpha1) * last, last)

            cosines, sines = weights(real), weights(imag)
            evolved = []
            squares = 0.0
            for s in range(2):
                re = im = 0.0
                for k, part_of in enumerate((tensor(t, s, a), w[t, s, a], h[s, a])):
                    cosine, sine = cosines[k], sines[k]
                    top, bottom = part_of[:width], part_of[width:]
                    re = re + cosine * top - sine * bottom
                    im = im + cosine * bottom + sine * top
                outs[t][s, 0, a, 0] = re
                outs[t][s, 1, a, 0] = im
                evolved.append((re, im))
                squares = squares + column_sum(re * re + im * im)
            if t + 1 < TENSORS:
                square = jnp.sum(squares, axis=1, keepdims=True)
                factor = SECTOR_BOUND / jnp.sqrt(
                    jnp.broadcast_to(square, (1, width)) + norm_square * (1.0 / count))
                factor = jnp.concatenate([factor * factor] * 2, axis=1)
                x = evolved
                flip = [split(jnp.concatenate([re.T, im.T], axis=1)) for re, im in x]

                def wide(re, im):
                    return split(jnp.concatenate(
                        [jnp.concatenate([re, im], axis=1), jnp.concatenate([im, -re], axis=1)],
                        axis=0))

                linked = dot3(flip[1], wide(*x[0])) * factor
                gmove[t, 0, a, 0] = linked[:, :width]
                gmove[t, 0, a, 1] = linked[:, width:]
                start_up(move_copy(t, 1, a))
                whole = split(jnp.concatenate(
                    [jnp.concatenate(pair, axis=0) for pair in x], axis=1))
                image = dot3(get(lop, a), whole)
                energy = erow[t, pl.ds(a, 1), :]
                lifted = dot3(flip[1], wide(
                    image[:width, width:] + energy * x[1][0],
                    image[width:, width:] + energy * x[1][1])) * factor
                pmove[t, 0, a] = jnp.where(rows <= cols, lifted[:, :width], lifted[:, width:])
                start_up(move_copy(t, 0, a))
                own = dot3(flip[0], wide(image[:width, :width], image[width:, :width])) * factor
                rate = chain[t + 1, a, 1]
                put(hu, a, complex_block(
                    rate * linked[:, :width].T, -rate * linked[:, width:].T))
                kept[a] = jnp.concatenate([own[:, :width], own[:, width:]], axis=0)

    @pl.when(has_next)
    def _():
        for a in range(arms):
            hop_copy(a).wait_send()
            for t in range(TENSORS):
                zup_copy(t, a).wait_send()
                wup_copy(t, a).wait_send()
                hup_copy(t, a).wait_send()
            for t in range(TENSORS - 1):
                for n in range(2):
                    move_copy(t, n, a).wait_send()

    @pl.when(has_prev)
    def _():
        for a in range(arms):
            for t in range(TENSORS):
                right_copy(t, a).wait_send()
                zlow_copy(t, a).wait_send()
                wlow_copy(t, a).wait_send()
                hlow_copy(t, a).wait_send()

    pltpu.make_async_copy(ored, ored, ored_s).wait()
    for a in range(arms):
        for t in range(TENSORS):
            end_reduce(t, a)


def hand_kernel(a, b, c, x, y, z, sem):
    copies = [
        pltpu.make_async_copy(i, o, sem.at[k]) for k, (i, o) in enumerate(((a, x), (b, y), (c, z)))]
    for copy in copies:
        copy.start()
    for copy in copies:
        copy.wait()


def hand(outs):
    anywhere = pl.BlockSpec(memory_space=pl.ANY)
    return pl.pallas_call(
        hand_kernel, out_shape=tuple(jax.ShapeDtypeStruct(o.shape, o.dtype) for o in outs),
        in_specs=[pl.BlockSpec(memory_space=pltpu.VMEM)] * 3, out_specs=(anywhere,) * 3,
        scratch_shapes=[pltpu.SemaphoreType.DMA((3,))],
    )(*(pltpu.with_memory_space_constraint(o, pltpu.VMEM) for o in outs))


def on_device(count, arm_devices, *args):
    site = args[0]
    args = args[:6] + (jnp.transpose(args[6], (1, 0, 2)),) + args[7:]
    arms, width = site.shape[2], site.shape[-1]
    occ_rows = -(-2 * arms // 8) * 8
    arm_rows = -(-arms // 8) * 8
    vmem, sems = pltpu.VMEM, pltpu.SemaphoreType.DMA
    state = vmem((2, arms, 2 * width, width), F32)
    source = vmem((TENSORS, arms, 2, width, width), F32)
    halo = vmem((TENSORS, arms, 2 * width, width), F32)
    square = vmem((TENSORS, arms, width, width), F32)
    operator = vmem((2, arms, 2 * width, 2 * width), BF16)
    block = vmem((arms, width, width), F32)
    whole = pl.BlockSpec(memory_space=pltpu.VMEM)
    distant = pl.BlockSpec(memory_space=pltpu.HBM)
    scalar = pl.BlockSpec(memory_space=pltpu.SMEM)
    out = pltpu.VMEM(site.shape, F32)
    each, single = sems((TENSORS, arms)), sems((arms,))
    moves, sums = sems((TENSORS - 1, 2, arms)), each
    arm_sems = sems((max(arm_devices - 1, 1),))
    outs = pl.pallas_call(
        functools.partial(kernel, count, arms, arm_devices),
        out_shape=(out, out, out),
        in_specs=[distant] * 6 + [scalar] * 3,
        out_specs=(whole,) * 3,
        scratch_shapes=[
            vmem((TENSORS, 2, 2, arms, width, width), F32),
            vmem((TENSORS, 2, arms, 2 * width, width), F32),
            state, state, vmem((arms, 2 * width, width), F32), vmem((2, arms, width, width), F32),
            source, source, halo, halo,
            vmem((TENSORS, 2, arms, width, width), F32), square, square, square,
            vmem((TENSORS - 1, 2, arms, width, width), F32),
            vmem((TENSORS - 1, 2, arms, 2, width, width), F32),
            block, block, vmem((TENSORS, arms, 2, width, width), F32),
            operator, operator, operator, operator, block,
            vmem((TENSORS, arms, 8, width), F32),
            vmem((TENSORS, arms, count - 1, 8, width), F32),
            vmem((occ_rows, width), F32),
            vmem((count - 1, occ_rows, width), F32),
            vmem((arm_rows, width), F32),
            vmem((max(arm_devices - 1, 1), arm_rows, width), F32),
            vmem((TENSORS, arm_rows, width), F32),
            each, single, single, each,
            each, each, each, each, each, each, each, each, each, each, each, each,
            each, each, single, single, moves, moves, sums, sums,
            pltpu.SemaphoreType.DMA, pltpu.SemaphoreType.DMA, arm_sems, arm_sems,
        ],
        compiler_params=pltpu.CompilerParams(
            collective_id=0, has_side_effects=True, vmem_limit_bytes=56 * 1024 * 1024
        ),
    )(*args)
    return hand(outs)


def solution(mesh):
    tensor = P(None, None, "arm", "blk", None, None)
    in_specs = (
        tensor, tensor, tensor,
        P("arm", "blk", None, None),
        P("arm", "blk", None, None),
        P("arm", "blk", None, None, None, None),
        P("arm", None, None),
        P("arm", None),
        P("arm", None, None),
    )
    body = functools.partial(on_device, mesh.shape["blk"], mesh.shape["arm"])
    return jax.shard_map(
        body, mesh=mesh, in_specs=in_specs, out_specs=(tensor, tensor, tensor), check_vma=False
    )
```
